128 devices in a mesh: ctx: 32 (over y, z, x_lo), seq: 2 (over core), fsdp: 2 (over x_hi).
Axes of the slice: x: 4 (x_hi: 2, x_lo: 2; x = x_hi * 2 + x_lo), y: 4, z: 4, core: 2. Of those that a mesh axis runs over, the one named last changes fastest.
Arguments:
- tokens: bfloat16 [4, 4096, 768], P(('seq', 'fsdp'), 'ctx'), may hold values from -6 to 6
- cotangent: bfloat16 [4, 4096, 768], P(('seq', 'fsdp'), 'ctx'), may hold values from -6 to 6
- w_query: bfloat16 [768, 768], P('fsdp'), may hold values from -0.21875 to 0.21875
- w_key: bfloat16 [768, 768], P('fsdp'), may hold values from -0.21875 to 0.21875
- w_value: bfloat16 [768, 768], P('fsdp'), may hold values from -0.21875 to 0.21875
- w_output: bfloat16 [768, 768], P('fsdp'), may hold values from -6 to 6
- b_query: bfloat16 [768], P('fsdp'), may hold values from -1.5 to 1.5
- b_value: bfloat16 [768], P('fsdp'), may hold values from -0.15625 to 0.15625
- b_output: bfloat16 [768], P('fsdp'), may hold values from -1.5 to 1.5
- first_gain: bfloat16 [768], P('fsdp'), may hold values from 0.5 to 1.5
- first_shift: bfloat16 [768], P('fsdp'), may hold values from -1.5 to 1.5
- w_inner: bfloat16 [768, 3072], P('fsdp'), may hold values from -0.21875 to 0.21875
- b_inner: bfloat16 [3072], P('fsdp'), may hold values from -1.5 to 1.5
- w_outer: bfloat16 [3072, 768], P('fsdp'), may hold values from -0.109375 to 0.109375
- b_outer: bfloat16 [768], P('fsdp'), may hold values from -1.5 to 1.5
- second_gain: bfloat16 [768], P('fsdp'), may hold values from 0.5 to 1.5
- second_shift: bfloat16 [768], P('fsdp'), may hold values from -1.5 to 1.5
Outputs:
- layer_out: bfloat16 [4, 4096, 768], P(('seq', 'fsdp'), 'ctx')
- tokens_grad: float32 [4, 4096, 768], P(('seq', 'fsdp'), 'ctx')
- w_query_grad: float32 [768, 768], P('fsdp')
- w_key_grad: float32 [768, 768], P('fsdp')
- w_value_grad: float32 [768, 768], P('fsdp')
- w_output_grad: float32 [768, 768], P('fsdp')
- b_query_grad: float32 [768], P('fsdp')
- b_value_grad: float32 [768], P('fsdp')
- b_output_grad: float32 [768], P('fsdp')
- first_gain_grad: float32 [768], P('fsdp')
- first_shift_grad: float32 [768], P('fsdp')
- w_inner_grad: float32 [768, 3072], P('fsdp')
- b_inner_grad: float32 [3072], P('fsdp')
- w_outer_grad: float32 [3072, 768], P('fsdp')
- b_outer_grad: float32 [768], P('fsdp')
- second_gain_grad: float32 [768], P('fsdp')
- second_shift_grad: float32 [768], P('fsdp')
The draws below stay inside these ranges and needn't reach their ends.
All inputs are finite; a program needn't handle non-finite values.
Results may differ from the reference program's by a relative error of at most 0.022.
Values may be sent and summed in bfloat16 or wider, within the bound.
A program may use at most 192 MiB of HBM per device.

```python
import math
import jax
import jax.numpy as jnp
from jax import lax

D = 768
HEADS = 12
HEAD_DIM = 64
FF = 3072
LENGTH = 4096
SEQUENCES = 4


def steps_of(rng, dims, pieces, smallest, largest):
    level = 1.0
    for axis_at, blocks in pieces:
        draws = jax.random.uniform(jax.random.fold_in(jax.random.fold_in(rng, 6), axis_at), (blocks,), jnp.float32, smallest / len(pieces), largest / len(pieces))
        level = level * jnp.repeat(jnp.exp(draws), dims[axis_at] // blocks).reshape((-1,) + (1,) * (len(dims) - 1 - axis_at))
    return level


def bell_draw(rng, extent, spread, most, pieces=(), dtype=jnp.bfloat16):
    level = steps_of(rng, extent, pieces, -0.22, 0.18) if pieces else 1.0
    array = jax.random.normal(rng, extent, jnp.float32) * spread * level
    return jnp.minimum(jnp.maximum(array, -most), most).astype(dtype)


def setup_inputs(seed: int = 0) -> dict:
    streams_of = jax.random.split(jax.random.key(seed), 18)
    return {
        "tokens": bell_draw(streams_of[0], (SEQUENCES, LENGTH, D), 1.0, 6.0, ((0, 4), (1, 32))),
        "cotangent": bell_draw(streams_of[1], (SEQUENCES, LENGTH, D), 1.0, 6.0, ((0, 4), (1, 32))),
        "w_query": bell_draw(streams_of[2], (D, D), D ** -0.5, 0.21875, ((0, 2),)),
        "w_key": bell_draw(streams_of[3], (D, D), D ** -0.5, 0.21875, ((0, 2),)),
        "w_value": bell_draw(streams_of[4], (D, D), D ** -0.5, 0.21875, ((0, 2),)),
        "w_output": bell_draw(streams_of[5], (D, D), ((LENGTH * 1000 // (27 * D)) ** 0.5 * 0.1), 6.0, ((0, 2),)),
        "b_query": bell_draw(streams_of[6], (D,), 0.1, 1.5, ((0, 2),)),
        "b_value": bell_draw(streams_of[7], (D,), 0.01, 0.15625, ((0, 2),)),
        "b_output": bell_draw(streams_of[8], (D,), 0.1, 1.5, ((0, 2),)),
        "first_gain": jnp.clip(1.0 + 0.1 * jax.random.normal(streams_of[9], (D,), jnp.float32), 0.5, 1.5).astype(jnp.bfloat16),
        "first_shift": bell_draw(streams_of[10], (D,), 0.1, 1.5, ((0, 2),)),
        "w_inner": bell_draw(streams_of[11], (D, FF), D ** -0.5, 0.21875, ((0, 2),)),
        "b_inner": bell_draw(streams_of[12], (FF,), 0.1, 1.5, ((0, 2),)),
        "w_outer": bell_draw(streams_of[13], (FF, D), FF ** -0.5, 0.109375, ((0, 2),)),
        "b_outer": bell_draw(streams_of[14], (D,), 0.1, 1.5, ((0, 2),)),
        "second_gain": jnp.clip(1.0 + 0.1 * jax.random.normal(streams_of[15], (D,), jnp.float32), 0.5, 1.5).astype(jnp.bfloat16),
        "second_shift": bell_draw(streams_of[16], (D,), 0.1, 1.5, ((0, 2),)),
    }


@jax.custom_vjp
def low(v):
    return lax.optimization_barrier(v.astype(jnp.bfloat16)).astype(jnp.float32)

@jax.custom_vjp
def low_back(v):
    return v

def low_keep(v):
    return (low(v), None)

def low_pass(kept, grad):
    return (grad,)

def back_keep(v):
    return (v, None)

def back_low(kept, grad):
    return (low(grad),)
low.defvjp(low_keep, low_pass)
low_back.defvjp(back_keep, back_low)

def product(left, right):
    return jnp.dot(left, right, precision=lax.Precision.HIGHEST)

def layer_norm(hidden, gain, shift):
    centred = hidden - lax.optimization_barrier(jnp.mean(hidden, axis=-1, keepdims=True))
    variance = lax.optimization_barrier(jnp.mean(centred * centred, axis=-1, keepdims=True))
    return centred * lax.rsqrt(variance + 1e-12) * gain + shift

def attend(query, keys, values):
    scores = low_back(jnp.einsum('qhd,khd->hqk', query, keys, precision=lax.Precision.HIGHEST) * HEAD_DIM ** (-0.5))
    probs = jax.nn.softmax(scores, axis=-1)
    return jnp.einsum('hqk,khd->qhd', low(probs), values, precision=lax.Precision.HIGHEST)

def forward(seq_tokens, w_query, w_key, w_value, w_output, b_query, b_value, b_output, first_gain, first_shift, w_inner, b_inner, w_outer, b_outer, second_gain, second_shift):
    count = seq_tokens.shape[0]
    query = low_back(low(product(seq_tokens, w_query) + b_query)).reshape(count, HEADS, HEAD_DIM)
    keys = low_back(low(product(seq_tokens, w_key))).reshape(count, HEADS, HEAD_DIM)
    values = low_back(low(product(seq_tokens, w_value) + b_value)).reshape(count, HEADS, HEAD_DIM)
    query_rows = math.gcd(count, 512)
    blocks = query.reshape(count // query_rows, query_rows, HEADS, HEAD_DIM)
    mixed = lax.map(jax.checkpoint(lambda piece: attend(piece, keys, values)), blocks)
    attended = low_back(low(mixed.reshape(count, HEADS * HEAD_DIM)))
    branch = low_back(product(attended, w_output) + b_output)
    normed = layer_norm(seq_tokens + branch, first_gain, first_shift)
    inner = low_back(product(low(normed), w_inner) + b_inner)
    active = low(jax.nn.gelu(inner, approximate=False))
    second = low_back(product(active, w_outer) + b_outer)
    return layer_norm(normed + second, second_gain, second_shift)

def reference(tokens, cotangent, w_query, w_key, w_value, w_output, b_query, b_value, b_output, first_gain, first_shift, w_inner, b_inner, w_outer, b_outer, second_gain, second_shift):
    params = tuple((p.astype(jnp.float32) for p in (w_query, w_key, w_value, w_output, b_query, b_value, b_output, first_gain, first_shift, w_inner, b_inner, w_outer, b_outer, second_gain, second_shift)))

    def one_sequence(totals, pair):
        seq_tokens, seq_grad = pair
        result, pullback = jax.vjp(forward, seq_tokens.astype(jnp.float32), *params)
        grads = pullback(seq_grad.astype(jnp.float32))
        summed = tuple((t + g for t, g in zip(totals, grads[1:])))
        return (summed, (result.astype(jnp.bfloat16), grads[0]))
    zeros = tuple((jnp.zeros(p.shape, jnp.float32) for p in params))
    totals, (layer_out, tokens_grad) = lax.scan(one_sequence, zeros, (tokens, cotangent))
    return (layer_out, tokens_grad) + totals
```

```python
import functools

import jax
import jax.numpy as jnp
from jax import lax
from jax.experimental import pallas as pl
from jax.experimental.pallas import tpu as pltpu
from jax.sharding import PartitionSpec as P

AXES = ("ctx", "seq", "fsdp")
MESH = pl.DeviceIdType.MESH
BF = jnp.bfloat16
F32 = jnp.float32
D = 768
FF = 3072
HALF = 384
GROUP = 192
HD = 64
ROWS = 128
EPS = 1e-12
LIMIT = 56 << 20
VM = pl.BlockSpec(memory_space=pltpu.VMEM)
ANY = pl.BlockSpec(memory_space=pl.ANY)


def shape(*dims, dtype=BF):
    return jax.ShapeDtypeStruct(dims, dtype)


def nn(left, right):
    return jnp.dot(left, right, preferred_element_type=F32)


def nt(left, right):
    return lax.dot_general(left, right, (((1,), (1,)), ((), ())), preferred_element_type=F32)


def tn(left, right):
    return lax.dot_general(left, right, (((0,), (0,)), ((), ())), preferred_element_type=F32)


def wrap(value, size):
    return lax.rem(value + size, size)


def place():
    ctx = lax.axis_index("ctx")
    y = lax.div(ctx, 8)
    z = lax.rem(lax.div(ctx, 2), 4)
    return y, z, lax.rem(ctx, 2), lax.axis_index("seq"), lax.axis_index("fsdp")


def device(y, z, xl, core, half):
    return ((y * 4 + z) * 2 + xl, core, half)


def send(src, dst, out_sem, in_sem, where):
    pltpu.make_async_remote_copy(
        src_ref=src, dst_ref=dst, send_sem=out_sem, recv_sem=in_sem,
        device_id=where, device_id_type=MESH,
    ).start()


def finish(src, dst, out_sem, in_sem, where):
    copy = pltpu.make_async_remote_copy(
        src_ref=src, dst_ref=dst, send_sem=out_sem, recv_sem=in_sem,
        device_id=where, device_id_type=MESH,
    )
    copy.wait_send()
    copy.wait_recv()


def greet(barrier, where):
    pl.semaphore_signal(barrier, inc=1, device_id=where, device_id_type=MESH)


def parts(k):
    return lax.div(k, 8), lax.rem(lax.div(k, 2), 4), lax.rem(k, 2)


def spread_kernel(q_ref, kv_ref, qo_ref, kvo_ref, local_sem, qs, qr, ks, kr):
    y, z, xl, core, half = place()
    me = lax.axis_index("ctx")
    barrier = pltpu.get_barrier_semaphore()

    def other(k):
        dy, dz, dx = parts(k)
        return wrap(y + dy, 4), wrap(z + dz, 4), wrap(xl + dx, 2)

    def source(k):
        dy, dz, dx = parts(k)
        return (wrap(y - dy, 4) * 4 + wrap(z - dz, 4)) * 2 + wrap(xl - dx, 2)

    def hello(k, carry):
        ey, ez, ex = other(k)
        greet(barrier, device(ey, ez, ex, core, half))
        return carry

    lax.fori_loop(1, 32, hello, 0)
    pl.semaphore_wait(barrier, 31)

    def push_q(k, carry):
        ez = wrap(z + k, 4)
        send(q_ref.at[ez], qo_ref.at[z], qs.at[k], qr.at[k], device(y, ez, xl, core, half))
        return carry

    def push(k, carry):
        ey, ez, ex = other(k)
        send(kv_ref.at[ez], kvo_ref.at[me], ks.at[k], kr.at[k], device(ey, ez, ex, core, half))
        return carry

    lax.fori_loop(1, 4, push_q, 0)
    lax.fori_loop(1, 32, push, 0)
    mine = pltpu.make_async_copy(kv_ref.at[z], kvo_ref.at[me], local_sem.at[0])
    mine.start()
    mine_q = pltpu.make_async_copy(q_ref.at[z], qo_ref.at[z], local_sem.at[1])
    mine_q.start()

    def done_q(k, carry):
        finish(q_ref.at[0], qo_ref.at[wrap(z - k, 4)], qs.at[k], qr.at[k], device(y, z, xl, core, half))
        return carry

    def done(k, carry):
        finish(kv_ref.at[0], kvo_ref.at[source(k)], ks.at[k], kr.at[k], device(y, z, xl, core, half))
        return carry

    lax.fori_loop(1, 4, done_q, 0)
    lax.fori_loop(1, 32, done, 0)
    mine.wait()
    mine_q.wait()


def collect_kernel(q_ref, kv_ref, qo_ref, kvo_ref, local_sem, qs, qr, ks, kr):
    y, z, xl, core, half = place()
    me = lax.axis_index("ctx")
    barrier = pltpu.get_barrier_semaphore()

    def other(k):
        dy, dz, dx = parts(k)
        return wrap(y + dy, 4), wrap(z + dz, 4), wrap(xl + dx, 2)

    def source(k):
        dy, dz, dx = parts(k)
        return (wrap(y - dy, 4) * 4 + wrap(z - dz, 4)) * 2 + wrap(xl - dx, 2)

    def hello(k, carry):
        ey, ez, ex = other(k)
        greet(barrier, device(ey, ez, ex, core, half))
        return carry

    lax.fori_loop(1, 32, hello, 0)
    pl.semaphore_wait(barrier, 31)

    def push_q(k, carry):
        ez = wrap(z + k, 4)
        send(q_ref.at[ez], qo_ref.at[z], qs.at[k], qr.at[k], device(y, ez, xl, core, half))
        return carry

    def push(k, carry):
        ey, ez, ex = other(k)
        to = (ey * 4 + ez) * 2 + ex
        send(kv_ref.at[to], kvo_ref.at[me], ks.at[k], kr.at[k], device(ey, ez, ex, core, half))
        return carry

    lax.fori_loop(1, 4, push_q, 0)
    lax.fori_loop(1, 32, push, 0)
    mine = pltpu.make_async_copy(kv_ref.at[me], kvo_ref.at[me], local_sem.at[0])
    mine.start()
    mine_q = pltpu.make_async_copy(q_ref.at[z], qo_ref.at[z], local_sem.at[1])
    mine_q.start()

    def done_q(k, carry):
        finish(q_ref.at[0], qo_ref.at[wrap(z - k, 4)], qs.at[k], qr.at[k], device(y, z, xl, core, half))
        return carry

    def done(k, carry):
        finish(kv_ref.at[0], kvo_ref.at[source(k)], ks.at[k], kr.at[k], device(y, z, xl, core, half))
        return carry

    lax.fori_loop(1, 4, done_q, 0)
    lax.fori_loop(1, 32, done, 0)
    mine.wait()
    mine_q.wait()


def mates_kernel(q_ref, qo_ref, local_sem, qs, qr):
    y, z, xl, core, half = place()
    barrier = pltpu.get_barrier_semaphore()

    def hello(k, carry):
        greet(barrier, device(y, wrap(z + k, 4), xl, core, half))
        return carry

    lax.fori_loop(1, 4, hello, 0)
    pl.semaphore_wait(barrier, 3)

    def push(k, carry):
        ez = wrap(z + k, 4)
        send(q_ref.at[ez], qo_ref.at[z], qs.at[k], qr.at[k], device(y, ez, xl, core, half))
        return carry

    lax.fori_loop(1, 4, push, 0)
    mine = pltpu.make_async_copy(q_ref.at[z], qo_ref.at[z], local_sem)
    mine.start()

    def done(k, carry):
        finish(q_ref.at[0], qo_ref.at[wrap(z - k, 4)], qs.at[k], qr.at[k], device(y, z, xl, core, half))
        return carry

    lax.fori_loop(1, 4, done, 0)
    mine.wait()


def exchange(kernel, name, number, pieces, blocks):
    dma = pltpu.SemaphoreType.DMA
    return pl.pallas_call(
        kernel,
        name=name,
        out_shape=(shape(4, ROWS, 256), shape(32, ROWS, HALF)),
        in_specs=[VM, VM],
        out_specs=(VM, VM),
        scratch_shapes=[dma((2,)), dma((4,)), dma((4,)), dma((32,)), dma((32,))],
        compiler_params=pltpu.CompilerParams(
            collective_id=number, has_side_effects=True, vmem_limit_bytes=LIMIT
        ),
    )(pieces, blocks)


def mates(name, number, pieces):
    dma = pltpu.SemaphoreType.DMA
    return pl.pallas_call(
        mates_kernel,
        name=name,
        out_shape=shape(4, ROWS, 256),
        in_specs=[VM],
        out_specs=VM,
        scratch_shapes=[dma, dma((4,)), dma((4,))],
        compiler_params=pltpu.CompilerParams(
            collective_id=number, has_side_effects=True, vmem_limit_bytes=LIMIT
        ),
    )(pieces)


def project_kernel(x_ref, wq, wk, wv, ra, rb, bias_ref, q_ref, kv_ref, w_ref, sems):
    core = lax.axis_index("seq")
    half = lax.axis_index("fsdp")
    own = pl.multiple_of(half * HALF, HALF)
    first = pl.multiple_of((1 - half) * HALF + core * GROUP, GROUP)
    second = pl.multiple_of((1 - half) * HALF + (1 - core) * GROUP, GROUP)
    copies = []
    for i, w in enumerate((wq, wk, wv)):
        copies.append(pltpu.make_async_copy(w, w_ref.at[i, pl.ds(own, HALF)], sems.at[i]))
    for i in range(3):
        copies.append(pltpu.make_async_copy(ra.at[i], w_ref.at[i, pl.ds(first, GROUP)], sems.at[3 + i]))
        copies.append(pltpu.make_async_copy(rb.at[i], w_ref.at[i, pl.ds(second, GROUP)], sems.at[6 + i]))
    for copy in copies:
        copy.start()
    for copy in copies:
        copy.wait()
    x = x_ref[...]
    pad = jnp.zeros((ROWS, 64), BF)
    query = (nn(x, w_ref[0]) + bias_ref[0:1, :]).astype(BF) * BF(0.125)
    for g in range(4):
        q_ref[g] = jnp.concatenate([query[:, g * GROUP : (g + 1) * GROUP], pad], axis=1)
    keys = nn(x, w_ref[1]).astype(BF)
    values = (nn(x, w_ref[2]) + bias_ref[1:2, :]).astype(BF)
    for g in range(4):
        cut = slice(g * GROUP, (g + 1) * GROUP)
        kv_ref[g] = jnp.concatenate([keys[:, cut], values[:, cut]], axis=1)


def project(x, wq, wk, wv, ra, rb, bias):
    return pl.pallas_call(
        project_kernel,
        name="project",
        out_shape=(shape(4, ROWS, 256), shape(4, ROWS, HALF), shape(3, D, D)),
        in_specs=[VM, ANY, ANY, ANY, ANY, ANY, VM],
        out_specs=(VM, VM, VM),
        scratch_shapes=[pltpu.SemaphoreType.DMA((9,))],
        compiler_params=pltpu.CompilerParams(vmem_limit_bytes=LIMIT),
    )(x, wq, wk, wv, ra, rb, bias)


CHUNK = 256


def load_chunk(ref, i):
    n = CHUNK // ROWS
    return ref[pl.ds(i * n, n)].reshape(CHUNK, HALF)


def stack_head(ref, h):
    return jnp.concatenate([ref[i][:, h * HD : (h + 1) * HD] for i in range(4)], axis=0)


def turned(rows):
    return rows.astype(F32).T.astype(BF)


def attend_kernel(q_ref, kv_ref, o_ref, ot_ref, lse_ref, qt, top, total):
    for h in range(3):
        qt[h] = turned(stack_head(q_ref, h))
    top[...] = jnp.full_like(top, -jnp.inf)
    total[...] = jnp.zeros_like(total)
    ot_ref[...] = jnp.zeros_like(ot_ref)

    def body(i, carry):
        kv = load_chunk(kv_ref, i)
        for h in range(3):
            scores = nn(kv[:, h * HD : (h + 1) * HD], qt[h])
            old = top[h]
            new = jnp.maximum(old, jnp.max(scores, axis=0, keepdims=True))
            shrink = jnp.exp(old - new)
            weights = jnp.exp(scores - new)
            total[h] = total[h] * shrink + jnp.sum(weights, axis=0, keepdims=True)
            mixed = tn(kv[:, GROUP + h * HD : GROUP + (h + 1) * HD], weights.astype(BF))
            ot_ref[h] = ot_ref[h] * shrink + mixed
            top[h] = new
        return carry

    lax.fori_loop(0, 4096 // CHUNK, body, 0)
    heads = []
    for h in range(3):
        lse_ref[h] = top[h] + jnp.log(total[h])
        normal = ot_ref[h] / total[h]
        ot_ref[h] = normal
        heads.append(normal.T.astype(BF))
    heads.append(jnp.zeros((512, 64), BF))
    out = jnp.concatenate(heads, axis=1)
    for i in range(4):
        o_ref[i] = out[i * ROWS : (i + 1) * ROWS]


def attend(q, kv):
    return pl.pallas_call(
        attend_kernel,
        name="attend",
        out_shape=(shape(4, ROWS, 256), shape(3, HD, 512, dtype=F32), shape(3, 1, 512, dtype=F32)),
        in_specs=[VM, VM],
        out_specs=(VM, VM, VM),
        scratch_shapes=[
            pltpu.VMEM((3, HD, 512), BF), pltpu.VMEM((3, 1, 512), F32), pltpu.VMEM((3, 1, 512), F32),
        ],
        compiler_params=pltpu.CompilerParams(vmem_limit_bytes=LIMIT),
    )(q, kv)


def attend_back_kernel(q_ref, kv_ref, da_ref, ot_ref, lse_ref, dq_ref, dkv_ref, qs, qt, ds, dt, delta, acc):
    for h in range(3):
        rows = stack_head(q_ref, h)
        qs[h] = rows
        qt[h] = turned(rows)
        rows = stack_head(da_ref, h)
        ds[h] = rows
        flipped = rows.astype(F32).T
        dt[h] = flipped.astype(BF)
        delta[h] = jnp.sum(flipped * ot_ref[h], axis=0, keepdims=True)
    acc[...] = jnp.zeros_like(acc)

    def body(i, carry):
        kv = load_chunk(kv_ref, i)
        keys, values = [], []
        for h in range(3):
            k = kv[:, h * HD : (h + 1) * HD]
            v = kv[:, GROUP + h * HD : GROUP + (h + 1) * HD]
            probs = jnp.exp(nn(k, qt[h]) - lse_ref[h])
            slopes = (probs * (nn(v, dt[h]) - delta[h])).astype(BF)
            keys.append(nn(slopes, qs[h]).astype(BF))
            values.append(nn(probs.astype(BF), ds[h]).astype(BF))
            acc[h] += tn(k, slopes)
        n = CHUNK // ROWS
        dkv_ref[pl.ds(i * n, n)] = jnp.concatenate(keys + values, axis=1).reshape(n, ROWS, HALF)
        return carry

    lax.fori_loop(0, 4096 // CHUNK, body, 0)
    heads = [(acc[h] * 0.125).T.astype(BF) for h in range(3)]
    heads.append(jnp.zeros((512, 64), BF))
    out = jnp.concatenate(heads, axis=1)
    for i in range(4):
        dq_ref[i] = out[i * ROWS : (i + 1) * ROWS]


def attend_back(q, kv, da, ot, lse):
    return pl.pallas_call(
        attend_back_kernel,
        name="attend_back",
        out_shape=(shape(4, ROWS, 256), shape(32, ROWS, HALF)),
        in_specs=[VM] * 5,
        out_specs=(VM, VM),
        scratch_shapes=[
            pltpu.VMEM((3, 512, HD), BF), pltpu.VMEM((3, HD, 512), BF),
            pltpu.VMEM((3, 512, HD), BF), pltpu.VMEM((3, HD, 512), BF),
            pltpu.VMEM((3, 1, 512), F32), pltpu.VMEM((3, HD, 512), F32),
        ],
        compiler_params=pltpu.CompilerParams(vmem_limit_bytes=LIMIT),
    )(q, kv, da, ot, lse)


def norm(hidden):
    centred = hidden - jnp.mean(hidden, axis=-1, keepdims=True)
    inverse = lax.rsqrt(jnp.mean(centred * centred, axis=-1, keepdims=True) + EPS)
    return centred * inverse, inverse


def norm_back(scaled, normal, inverse):
    centre = jnp.mean(scaled, axis=-1, keepdims=True)
    along = jnp.mean(scaled * normal, axis=-1, keepdims=True)
    return inverse * (scaled - centre - normal * along)


def column(value):
    return jnp.sum(value, axis=0, keepdims=True)


def block_kernel(
    x_ref, ct_ref, a_ref, wo, wo_a, wo_b, wi, wi_a, wi_b, wu, wu_a, wu_b, vec_ref, bi_ref,
    out_ref, dh1_ref, da_ref, af_ref, yb_ref, g_ref, df_ref, du_ref, dz_ref, vg_ref, big_ref,
    w_o, w_i, w_u, slope, sems,
):
    core = lax.axis_index("seq")
    half = lax.axis_index("fsdp")
    copies = []
    for i, (own, first, second, full, size) in enumerate(
        ((wo, wo_a, wo_b, w_o, HALF), (wi, wi_a, wi_b, w_i, HALF), (wu, wu_a, wu_b, w_u, FF // 2))
    ):
        q = size // 2
        at = pl.multiple_of(half * size, size)
        at_a = pl.multiple_of((1 - half) * size + core * q, q)
        at_b = pl.multiple_of((1 - half) * size + (1 - core) * q, q)
        copies.append(
            (
                pltpu.make_async_copy(own, full.at[pl.ds(at, size)], sems.at[3 * i]),
                pltpu.make_async_copy(first, full.at[pl.ds(at_a, q)], sems.at[3 * i + 1]),
                pltpu.make_async_copy(second, full.at[pl.ds(at_b, q)], sems.at[3 * i + 2]),
            )
        )
    for group in copies:
        for copy in group:
            copy.start()
    b_output, first_gain, first_shift = vec_ref[2:3, :], vec_ref[3:4, :], vec_ref[4:5, :]
    b_outer, second_gain, second_shift = vec_ref[5:6, :], vec_ref[6:7, :], vec_ref[7:8, :]
    mixed = jnp.concatenate([a_ref[g][:, :GROUP] for g in range(4)], axis=1)
    af_ref[...] = mixed
    for copy in copies[0]:
        copy.wait()
    hidden = x_ref[...].astype(F32) + nn(mixed, w_o[...]) + b_output
    normal1, inverse1 = norm(hidden)
    normed = normal1 * first_gain + first_shift
    low = normed.astype(BF)
    yb_ref[...] = low
    for group in copies[1:]:
        for copy in group:
            copy.wait()
    second_in = normed + b_outer
    for j in range(4):
        cut = slice(j * D, (j + 1) * D)
        inner = nn(low, w_i[:, cut]) + bi_ref[:, cut]
        cdf = 0.5 * (1.0 + lax.erf(inner * (0.5**0.5)))
        active = (inner * cdf).astype(BF)
        slope[:, cut] = cdf + inner * jnp.exp(inner * inner * -0.5) * 0.3989422804014327
        g_ref[:, cut] = active
        second_in = second_in + nn(active, w_u[cut, :])
    normal2, inverse2 = norm(second_in)
    out_ref[...] = (normal2 * second_gain + second_shift).astype(BF)
    upper = ct_ref[...].astype(F32)
    vg_ref[6:7, :] = column(upper * normal2)
    vg_ref[7:8, :] = column(upper)
    dh2 = norm_back(upper * second_gain, normal2, inverse2)
    df = dh2.astype(BF)
    df_ref[...] = df
    vg_ref[5:6, :] = column(df.astype(F32))
    dy1 = dh2
    for j in range(4):
        cut = slice(j * D, (j + 1) * D)
        du = (slope[:, cut] * nt(df, w_u[cut, :])).astype(BF)
        du_ref[:, cut] = du
        big_ref[:, cut] = column(du.astype(F32))
        dy1 = dy1 + nt(du, w_i[:, cut])
    vg_ref[3:4, :] = column(dy1 * normal1)
    vg_ref[4:5, :] = column(dy1)
    dh1 = norm_back(dy1 * first_gain, normal1, inverse1)
    dh1_ref[...] = dh1
    dz = dh1.astype(BF)
    dz_ref[...] = dz
    vg_ref[2:3, :] = column(dz.astype(F32))
    vg_ref[0:2, :] = jnp.zeros((2, D), F32)
    da = nt(dz, w_o[...]).astype(BF)
    pad = jnp.zeros((ROWS, 64), BF)
    for g in range(4):
        da_ref[g] = jnp.concatenate([da[:, g * GROUP : (g + 1) * GROUP], pad], axis=1)


def block(x, ct, a, weights, vec, b_inner):
    return pl.pallas_call(
        block_kernel,
        name="block",
        out_shape=(
            shape(ROWS, D), shape(ROWS, D, dtype=F32), shape(4, ROWS, 256), shape(ROWS, D), shape(ROWS, D),
            shape(ROWS, FF), shape(ROWS, D), shape(ROWS, FF), shape(ROWS, D), shape(8, D, dtype=F32),
            shape(1, FF, dtype=F32),
        ),
        in_specs=[VM, VM, VM] + [ANY] * 9 + [VM, VM],
        out_specs=(VM,) * 11,
        scratch_shapes=[
            pltpu.VMEM((D, D), BF), pltpu.VMEM((D, FF), BF), pltpu.VMEM((FF, D), BF),
            pltpu.VMEM((ROWS, FF), F32), pltpu.SemaphoreType.DMA((9,)),
        ],
        compiler_params=pltpu.CompilerParams(vmem_limit_bytes=LIMIT),
    )(x, ct, a, *weights, vec, b_inner)


def put(ref, at, value):
    ref[at] = value.astype(BF).reshape(4, 2, 48, HALF)


def wide_kernel(yb, yb_o, g, g_o, a, a_o, df, df_o, du, du_o, dz, dz_o, one_ref, two_ref, zero_ref):
    core = lax.axis_index("seq")

    def right(ref, other, start):
        cols = pl.ds(pl.multiple_of(start + core * HALF, HALF), HALF)
        return jnp.concatenate([ref[:, cols], other[:, cols]], axis=0)

    def left(ref, other, start):
        return jnp.concatenate([ref[:, start : start + HALF], other[:, start : start + HALF]], axis=0)

    outer = right(df, df_o, 0)
    attn = right(dz, dz_o, 0)
    for half in range(2):
        for m in range(4):
            put(one_ref, (half, m), tn(left(g, g_o, half * 1536 + m * HALF), outer))
        rows = left(yb, yb_o, half * HALF)
        for m in range(4):
            put(two_ref, (half, m), tn(rows, right(du, du_o, m * D)))
        put(zero_ref, half, tn(left(a, a_o, half * HALF), attn))


def wide(*arrays):
    return pl.pallas_call(
        wide_kernel,
        name="wide",
        out_shape=(shape(2, 4, 4, 2, 48, HALF), shape(2, 4, 4, 2, 48, HALF), shape(2, 4, 2, 48, HALF)),
        in_specs=[VM] * 12,
        out_specs=(VM, VM, VM),
        compiler_params=pltpu.CompilerParams(vmem_limit_bytes=LIMIT),
    )(*arrays)


def tail_kernel(dq_ref, dkv_ref, dh1_ref, w_ref, grad_ref, low_ref, vg_ref):
    low_ref[0] = jnp.concatenate([dq_ref[g][:, :GROUP] for g in range(4)], axis=1)
    sums = []
    for g in range(4):
        total = dkv_ref[2 * g].astype(F32)
        for k in range(1, 8):
            total = total + dkv_ref[(k // 2) * 8 + 2 * g + k % 2].astype(F32)
        sums.append(total.astype(BF))
    low_ref[1] = jnp.concatenate([s[:, :GROUP] for s in sums], axis=1)
    low_ref[2] = jnp.concatenate([s[:, GROUP:] for s in sums], axis=1)
    grad = dh1_ref[...]
    for i in range(3):
        grad = grad + nt(low_ref[i], w_ref[i])
    grad_ref[...] = grad
    vg_ref[...] = jnp.concatenate(
        [column(low_ref[0].astype(F32)), column(low_ref[2].astype(F32)), jnp.zeros((6, D), F32)], axis=0
    )


def tail(dq, dkv, dh1, w):
    return pl.pallas_call(
        tail_kernel,
        name="tail",
        out_shape=(shape(ROWS, D, dtype=F32), shape(3, ROWS, D), shape(8, D, dtype=F32)),
        in_specs=[VM] * 4,
        out_specs=(VM,) * 3,
        compiler_params=pltpu.CompilerParams(vmem_limit_bytes=LIMIT),
    )(dq, dkv, dh1, w)


def narrow_kernel(x, x_o, low, low_o, attn_ref, zero_ref):
    core = lax.axis_index("seq")
    cols = pl.ds(pl.multiple_of(core * HALF, HALF), HALF)
    for half in range(2):
        cut = slice(half * HALF, (half + 1) * HALF)
        rows = jnp.concatenate([x[:, cut], x_o[:, cut]], axis=0)
        for m in range(3):
            put(zero_ref, (half, m), tn(rows, jnp.concatenate([low[m, :, cols], low_o[m, :, cols]], axis=0)))
        zero_ref[half, 3] = attn_ref[half]


def narrow(*arrays):
    return pl.pallas_call(
        narrow_kernel,
        name="narrow",
        out_shape=shape(2, 4, 4, 2, 48, HALF),
        in_specs=[VM] * 5,
        out_specs=VM,
        compiler_params=pltpu.CompilerParams(vmem_limit_bytes=LIMIT),
    )(*arrays)


def reduce_kernel(
    g0, g1, g2, out, r0, r1, r2, s0, s1, s2, t0, t1, t2,
    a_out, a_in, b_out, b_in, c_out, c_in, d_out, d_in, e_out, e_in,
):
    y, z, xl, core, half = place()
    x = half * 2 + xl
    barrier = pltpu.get_barrier_semaphore()

    def along_x(k):
        e = wrap(x + k, 4)
        return device(y, z, lax.rem(e, 2), core, lax.div(e, 2))

    def pair(k):
        return lax.div(k, 4), lax.rem(k, 4)

    def at_yz(k):
        i, j = pair(k)
        return device(wrap(y + i, 4), wrap(z + j, 4), xl, core, half)

    def at_xz(k):
        i, j = pair(k)
        e = wrap(x + i, 4)
        return device(y, wrap(z + j, 4), lax.rem(e, 2), core, lax.div(e, 2))

    def at_xy(k):
        i, j = pair(k)
        e = wrap(x + i, 4)
        return device(wrap(y + j, 4), z, lax.rem(e, 2), core, lax.div(e, 2))

    def hello_yz(k, carry):
        greet(barrier, at_yz(k))
        return carry

    def hello_x(k, carry):
        i = lax.div(k - 1, 3) + 1
        j = lax.rem(k - 1, 3) + 1
        greet(barrier, at_xz(i * 4 + j))
        greet(barrier, at_xy(i * 4 + j))
        return carry

    def hello_row(k, carry):
        greet(barrier, along_x(k))
        return carry

    lax.fori_loop(1, 16, hello_yz, 0)
    lax.fori_loop(1, 10, hello_x, 0)
    lax.fori_loop(1, 4, hello_row, 0)
    greet(barrier, device(y, z, xl, 1 - core, half))
    pl.semaphore_wait(barrier, 37)

    def first(k, carry):
        e = wrap(x + k, 4)
        send(g0.at[lax.div(e, 2), :, :, lax.rem(e, 2)], r0.at[k - 1], a_out.at[0, k], a_in.at[0, k], along_x(k))
        send(g1.at[:, wrap(y + k, 4)], r1.at[k - 1], a_out.at[1, k], a_in.at[1, k], at_yz(k * 4))
        send(g2.at[:, :, wrap(z + k, 4)], r2.at[k - 1], a_out.at[2, k], a_in.at[2, k], at_yz(k))
        return carry

    lax.fori_loop(1, 4, first, 0)
    here = device(y, z, xl, core, half)

    def sum1(own, got, to, sem):
        for k in range(1, 4):
            finish(got.at[k - 1], got.at[k - 1], a_out.at[sem, k], a_in.at[sem, k], here)

        def add(i, carry):
            p, q, o = own(i)
            total = o.astype(F32)
            for k in range(3):
                total = total + got[(k,) + p].astype(F32)
            to[q] = total.astype(BF)
            return carry

        lax.fori_loop(0, 16, add, 0)

    def own0(i):
        p, q = pair(i)
        return (p, q), (p, q), g0[half, p, q, xl]

    def own1(i):
        f, q, r = lax.div(i, 8), lax.rem(lax.div(i, 2), 4), lax.rem(i, 2)
        return (f, q, r), (f, q, r), g1[f, y, q, r]

    def own2(i):
        f, q, r = lax.div(i, 8), lax.rem(lax.div(i, 2), 4), lax.rem(i, 2)
        return (f, q, r), (f, q, r), g2[f, q, z, r]

    sum1(own1, r1, s1, 1)

    def second1(k, carry):
        i, j = pair(k)
        e = wrap(x + i, 4)
        send(s1.at[lax.div(e, 2), wrap(z + j, 4), lax.rem(e, 2)], t1.at[k], b_out.at[1, k], b_in.at[1, k], at_xz(k))
        return carry

    lax.fori_loop(1, 16, second1, 0)
    sum1(own2, r2, s2, 2)

    def second2(k, carry):
        i, j = pair(k)
        e = wrap(x + i, 4)
        send(s2.at[lax.div(e, 2), wrap(y + j, 4), lax.rem(e, 2)], t2.at[k], b_out.at[2, k], b_in.at[2, k], at_xy(k))
        return carry

    lax.fori_loop(1, 16, second2, 0)
    sum1(own0, r0, s0, 0)

    def second0(k, carry):
        i, j = pair(k)
        send(s0.at[wrap(y + i, 4), wrap(z + j, 4)], t0.at[k], b_out.at[0, k], b_in.at[0, k], at_yz(k))
        return carry

    lax.fori_loop(1, 16, second0, 0)

    def sum2(own, got, slab):
        def done(k, carry):
            finish(got.at[k], got.at[k], b_out.at[slab, k], b_in.at[slab, k], here)
            return carry

        lax.fori_loop(1, 16, done, 0)

        def add(k, total):
            return total + got[k].astype(F32)

        total = lax.fori_loop(1, 16, add, own.astype(F32))
        out[core, slab, y, z, xl] = total.astype(BF)

    sum2(s1[half, z, xl], t1, 1)

    def third1(k, carry):
        i, j = lax.rem(k, 2), lax.div(k, 2)
        mine = out.at[core, 1, y, z, xl]
        send(mine, mine, c_out.at[1, k], c_in.at[1, k], device(y, wrap(z + j, 4), wrap(xl + i, 2), core, half))
        return carry

    lax.fori_loop(1, 8, third1, 0)
    sum2(s2[half, y, xl], t2, 2)

    def third2(k, carry):
        i, j = lax.rem(k, 2), lax.div(k, 2)
        mine = out.at[core, 2, y, z, xl]
        send(mine, mine, c_out.at[2, k], c_in.at[2, k], device(wrap(y + j, 4), z, wrap(xl + i, 2), core, half))
        return carry

    lax.fori_loop(1, 8, third2, 0)
    sum2(s0[y, z], t0, 0)

    def third0(k, carry):
        mine = out.at[core, 0, y, z, xl]
        send(mine, mine, c_out.at[0, k], c_in.at[0, k], at_yz(k))
        return carry

    lax.fori_loop(1, 16, third0, 0)

    def got1(k, carry):
        i, j = lax.rem(k, 2), lax.div(k, 2)
        piece = out.at[core, 1, y, wrap(z - j, 4), wrap(xl - i, 2)]
        finish(piece, piece, c_out.at[1, k], c_in.at[1, k], here)
        return carry

    lax.fori_loop(1, 8, got1, 0)

    def fourth1(k, carry):
        mine = out.at[core, 1, y]
        send(mine, mine, d_out.at[1, k], d_in.at[1, k], at_yz(k * 4))
        return carry

    lax.fori_loop(1, 4, fourth1, 0)

    def got2(k, carry):
        i, j = lax.rem(k, 2), lax.div(k, 2)
        piece = out.at[core, 2, wrap(y - j, 4), z, wrap(xl - i, 2)]
        finish(piece, piece, c_out.at[2, k], c_in.at[2, k], here)
        return carry

    lax.fori_loop(1, 8, got2, 0)

    def fourth2(k, carry):
        mine = out.at[core, 2, :, z]
        send(mine, mine, d_out.at[2, k], d_in.at[2, k], at_yz(k))
        return carry

    lax.fori_loop(1, 4, fourth2, 0)

    def got0(k, carry):
        i, j = pair(k)
        piece = out.at[core, 0, wrap(y - i, 4), wrap(z - j, 4), xl]
        finish(piece, piece, c_out.at[0, k], c_in.at[0, k], here)
        return carry

    lax.fori_loop(1, 16, got0, 0)
    mine0 = out.at[core, 0, :, :, xl]
    send(mine0, mine0, d_out.at[0, 1], d_in.at[0, 1], device(y, z, 1 - xl, core, half))

    def last1(k, carry):
        piece = out.at[core, 1, wrap(y - k, 4)]
        finish(piece, piece, d_out.at[1, k], d_in.at[1, k], here)
        return carry

    def last2(k, carry):
        piece = out.at[core, 2, :, wrap(z - k, 4)]
        finish(piece, piece, d_out.at[2, k], d_in.at[2, k], here)
        return carry

    sibling = device(y, z, xl, 1 - core, half)
    lax.fori_loop(1, 4, last1, 0)
    send(out.at[core, 1], out.at[core, 1], e_out.at[1], e_in.at[1], sibling)
    lax.fori_loop(1, 4, last2, 0)
    send(out.at[core, 2], out.at[core, 2], e_out.at[2], e_in.at[2], sibling)
    piece0 = out.at[core, 0, :, :, 1 - xl]
    finish(piece0, piece0, d_out.at[0, 1], d_in.at[0, 1], here)
    send(out.at[core, 0], out.at[core, 0], e_out.at[0], e_in.at[0], sibling)
    for slab in (1, 2, 0):
        piece = out.at[1 - core, slab]
        finish(piece, piece, e_out.at[slab], e_in.at[slab], here)


def reduce(g0, g1, g2):
    dma = pltpu.SemaphoreType.DMA
    blk = (48, HALF)
    return pl.pallas_call(
        reduce_kernel,
        name="reduce",
        out_shape=shape(2, 3, 4, 4, 2, *blk),
        in_specs=[VM] * 3,
        out_specs=VM,
        scratch_shapes=[
            pltpu.VMEM((3, 4, 4, *blk), BF), pltpu.VMEM((3, 2, 4, 2, *blk), BF), pltpu.VMEM((3, 2, 4, 2, *blk), BF),
            pltpu.VMEM((4, 4, *blk), BF), pltpu.VMEM((2, 4, 2, *blk), BF), pltpu.VMEM((2, 4, 2, *blk), BF),
            pltpu.VMEM((16, *blk), BF), pltpu.VMEM((16, *blk), BF), pltpu.VMEM((16, *blk), BF),
            dma((3, 4)), dma((3, 4)), dma((3, 16)), dma((3, 16)), dma((3, 16)), dma((3, 16)),
            dma((3, 4)), dma((3, 4)), dma((3,)), dma((3,)),
        ],
        compiler_params=pltpu.CompilerParams(
            collective_id=5, has_side_effects=True, vmem_limit_bytes=LIMIT
        ),
    )(g0, g1, g2)


def swap_halves(array):
    pairs = []
    for ctx in range(32):
        for core in range(2):
            for half in range(2):
                there = (ctx // 2) * 2 + (1 - ctx % 2)
                pairs.append(((ctx * 2 + core) * 2 + half, (there * 2 + core) * 2 + 1 - half))
    return lax.ppermute(array, AXES, pairs)


def swap_cores(array):
    return lax.ppermute(array, "seq", [(0, 1), (1, 0)])


def local(
    tokens, cotangent, w_query, w_key, w_value, w_output, b_query, b_value, b_output,
    first_gain, first_shift, w_inner, b_inner, w_outer, b_outer, second_gain, second_shift,
):
    core = lax.axis_index("seq")
    half = lax.axis_index("fsdp")
    x = tokens[0]

    def share(w):
        return lax.dynamic_slice_in_dim(w, core * (w.shape[0] // 2), w.shape[0] // 2, 0)

    small = jnp.concatenate(
        [b_query, b_value, b_output, first_gain, first_shift, b_outer, second_gain, second_shift, b_inner]
    ).reshape(12, HALF)
    small_o = swap_halves(small)
    qkv_a = swap_halves(jnp.stack([share(w) for w in (w_query, w_key, w_value)]))
    qkv_b = swap_cores(qkv_a)
    later, qkv_a = lax.optimization_barrier((tuple(share(w) for w in (w_output, w_inner, w_outer)), qkv_a))
    later_a = [swap_halves(w) for w in later]
    later_b = [swap_cores(w) for w in later_a]

    low_first = half == 0
    ahead = jnp.where(low_first, small, small_o).astype(F32)
    behind = jnp.where(low_first, small_o, small).astype(F32)
    vec = jnp.concatenate([ahead[:8], behind[:8]], axis=1)
    bi = jnp.concatenate([ahead[8:].reshape(1, 1536), behind[8:].reshape(1, 1536)], axis=1)

    q, kv, w_qkv = project(x, w_query, w_key, w_value, qkv_a, qkv_b, vec)
    q_all, kv_all = exchange(spread_kernel, "spread", 1, q, kv)
    mixed, mixed_t, lse = attend(q_all, kv_all)
    mixed = mates("mates_out", 2, mixed)
    weights = []
    for own, a, b in zip((w_output, w_inner, w_outer), later_a, later_b):
        weights += [own, a, b]
    layer_out, dh1, da, a_full, yb, g, df, du, dz, vg, big = block(x, cotangent[0], mixed, weights, vec, bi)
    da_all = mates("mates_in", 3, da)
    acts = (yb, g, a_full, df, du, dz)
    acts_o = [swap_cores(v) for v in acts]
    x_o = swap_cores(x)
    g1, g2, g0o = wide(*[v for pair in zip(acts, acts_o) for v in pair])
    dq, dkv = attend_back(q_all, kv_all, da_all, mixed_t, lse)
    dq, dkv = exchange(collect_kernel, "collect", 4, dq, dkv)
    tokens_grad, low, vg2 = tail(dq, dkv, dh1, w_qkv)
    low_o = swap_cores(low)
    g0 = narrow(x, x_o, low, low_o, g0o)
    summed = reduce(g0, g1, g2)

    vectors = jnp.concatenate([vg + vg2, big.reshape(4, D)], axis=0)
    vectors = lax.psum(vectors, AXES)
    vecs = lax.dynamic_slice_in_dim(vectors[:8], half * HALF, HALF, 1)
    b_inner_grad = lax.dynamic_slice_in_dim(vectors[8:].reshape(FF), half * 1536, 1536, 0)

    full = jnp.concatenate(
        [summed[0].reshape(3, 1536, HALF), summed[1].reshape(3, 1536, HALF)], axis=2
    ).astype(F32)
    inner = full[2].reshape(4, HALF, D).transpose(1, 0, 2).reshape(HALF, FF)
    return (
        layer_out[None], tokens_grad[None],
        full[0, :HALF], full[0, HALF : 2 * HALF], full[0, 2 * HALF : 3 * HALF], full[0, 3 * HALF :],
        vecs[0], vecs[1], vecs[2], vecs[3], vecs[4], inner, b_inner_grad, full[1], vecs[5], vecs[6], vecs[7],
    )


def solution(mesh):
    rows = P(("seq", "fsdp"), "ctx", None)
    mat = P("fsdp", None)
    vec = P("fsdp")
    return jax.shard_map(
        local,
        mesh=mesh,
        in_specs=(rows, rows, mat, mat, mat, mat, vec, vec, vec, vec, vec, mat, vec, mat, vec, vec, vec),
        out_specs=(rows, rows, mat, mat, mat, mat, vec, vec, vec, vec, vec, mat, vec, mat, vec, vec, vec),
        check_vma=False,
    )
```

```python
import functools

import jax
import jax.numpy as jnp
from jax import lax
from jax.experimental import pallas as pl
from jax.experimental.pallas import tpu as pltpu
from jax.sharding import PartitionSpec as P

AXES = ("ctx", "seq", "fsdp")
MESH = pl.DeviceIdType.MESH
BF = jnp.bfloat16
F32 = jnp.float32
D = 768
FF = 3072
HALF = 384
GROUP = 192
HD = 64
ROWS = 128
EPS = 1e-12
LIMIT = 56 << 20
VM = pl.BlockSpec(memory_space=pltpu.VMEM)
ANY = pl.BlockSpec(memory_space=pl.ANY)


def shape(*dims, dtype=BF):
    return jax.ShapeDtypeStruct(dims, dtype)


def nn(left, right):
    return jnp.dot(left, right, preferred_element_type=F32)


def nt(left, right):
    return lax.dot_general(left, right, (((1,), (1,)), ((), ())), preferred_element_type=F32)


def tn(left, right):
    return lax.dot_general(left, right, (((0,), (0,)), ((), ())), preferred_element_type=F32)


def wrap(value, size):
    return lax.rem(value + size, size)


def place():
    ctx = lax.axis_index("ctx")
    y = lax.div(ctx, 8)
    z = lax.rem(lax.div(ctx, 2), 4)
    return y, z, lax.rem(ctx, 2), lax.axis_index("seq"), lax.axis_index("fsdp")


def device(y, z, xl, core, half):
    return ((y * 4 + z) * 2 + xl, core, half)


def send(src, dst, out_sem, in_sem, where):
    pltpu.make_async_remote_copy(
        src_ref=src, dst_ref=dst, send_sem=out_sem, recv_sem=in_sem,
        device_id=where, device_id_type=MESH,
    ).start()


def finish(src, dst, out_sem, in_sem, where):
    copy = pltpu.make_async_remote_copy(
        src_ref=src, dst_ref=dst, send_sem=out_sem, recv_sem=in_sem,
        device_id=where, device_id_type=MESH,
    )
    copy.wait_send()
    copy.wait_recv()


def greet(barrier, where):
    pl.semaphore_signal(barrier, inc=1, device_id=where, device_id_type=MESH)


def pair(k):
    return lax.div(k, 4), lax.rem(k, 4)


class Turn:
    def __init__(self):
        self.y, self.z, self.xl, self.core, self.half = place()
        self.stays = self.xl == self.core

    def partner(self, k):
        i, j = pair(k)
        return device(wrap(self.y + i, 4), wrap(self.z + j, 4), self.core, self.xl, self.half)

    def ahead(self, k):
        i, j = pair(k)
        return wrap(self.y + i, 4), wrap(self.z + j, 4)

    def behind(self, k):
        i, j = pair(k)
        return wrap(self.y - i, 4), wrap(self.z - j, 4)

    def sibling(self):
        return device(self.y, self.z, self.xl, 1 - self.core, self.half)

    def greet(self, count, others=()):
        barrier = pltpu.get_barrier_semaphore()

        def hello(k, carry):
            greet(barrier, self.partner(k))
            return carry

        lax.fori_loop(1, count, hello, 0)
        for where in others:
            greet(barrier, where)

        @pl.when(jnp.logical_not(self.stays))
        def _():
            greet(barrier, self.partner(0))

        pl.semaphore_wait(barrier, count - 1 + len(others) + lax.rem(self.xl + self.core, 2))

    def start(self, count, src, dst, outs, ins):
        def push(k, carry):
            send(src(k), dst, outs.at[k], ins.at[k], self.partner(k))
            return carry

        @pl.when(self.stays)
        def _():
            pltpu.make_async_copy(src(0), dst, ins.at[0]).start()

        @pl.when(jnp.logical_not(self.stays))
        def _():
            push(0, 0)

        lax.fori_loop(1, count, push, 0)

    def end(self, k, got, outs, ins):
        finish(got, got, outs.at[k], ins.at[k], self.partner(k))

    def end_first(self, got, outs, ins):
        @pl.when(self.stays)
        def _():
            pltpu.make_async_copy(got, got, ins.at[0]).wait()

        @pl.when(jnp.logical_not(self.stays))
        def _():
            self.end(0, got, outs, ins)


def spread_kernel(q_ref, kv_ref, qo_ref, kvo_ref, qs, qr, ks, kr, fs, fr):
    turn = Turn()
    y, z, xl, core = turn.y, turn.z, turn.xl, turn.core
    turn.greet(16, (turn.sibling(),))
    turn.start(4, lambda k: q_ref.at[turn.ahead(k)[1]], qo_ref.at[z], qs, qr)
    turn.start(16, lambda k: kv_ref.at[turn.ahead(k)[1]], kvo_ref.at[y, z, xl], ks, kr)

    def onward(k):
        i, j = turn.behind(k)
        piece = kvo_ref.at[i, j, core]
        send(piece, piece, fs.at[k], fr.at[k], turn.sibling())

    turn.end_first(kvo_ref.at[y, z, core], ks, kr)
    onward(0)

    def relay(k, carry):
        i, j = turn.behind(k)
        turn.end(k, kvo_ref.at[i, j, core], ks, kr)
        onward(k)
        return carry

    lax.fori_loop(1, 16, relay, 0)
    turn.end_first(qo_ref.at[z], qs, qr)

    def done_q(k, carry):
        turn.end(k, qo_ref.at[turn.behind(k)[1]], qs, qr)
        return carry

    lax.fori_loop(1, 4, done_q, 0)

    def done(k, carry):
        i, j = turn.behind(k)
        piece = kvo_ref.at[i, j, 1 - core]
        finish(piece, piece, fs.at[k], fr.at[k], turn.sibling())
        return carry

    lax.fori_loop(0, 16, done, 0)


def collect_kernel(q_ref, kv_ref, qo_ref, kvo_ref, other, both, qs, qr, ks, kr, fs, fr):
    turn = Turn()
    y, z, xl, core = turn.y, turn.z, turn.xl, turn.core
    turn.greet(16, (turn.sibling(),))
    for i in range(4):
        send(kv_ref.at[i, :, 1 - core], other.at[i], fs.at[i], fr.at[i], turn.sibling())
    turn.start(4, lambda k: q_ref.at[turn.ahead(k)[1]], qo_ref.at[z], qs, qr)
    for i in range(4):
        finish(other.at[i], other.at[i], fs.at[i], fr.at[i], turn.sibling())

    def add(k, carry):
        i, j = pair(k)
        both[i, j] = (kv_ref[i, j, core].astype(F32) + other[i, j].astype(F32)).astype(BF)
        return carry

    lax.fori_loop(0, 16, add, 0)
    turn.start(16, lambda k: both.at[turn.ahead(k)], kvo_ref.at[y, z], ks, kr)
    turn.end_first(qo_ref.at[z], qs, qr)

    def done_q(k, carry):
        turn.end(k, qo_ref.at[turn.behind(k)[1]], qs, qr)
        return carry

    lax.fori_loop(1, 4, done_q, 0)
    turn.end_first(kvo_ref.at[y, z], ks, kr)

    def done(k, carry):
        turn.end(k, kvo_ref.at[turn.behind(k)], ks, kr)
        return carry

    lax.fori_loop(1, 16, done, 0)


def mates_kernel(q_ref, qo_ref, qs, qr):
    turn = Turn()
    turn.greet(4)
    turn.start(4, lambda k: q_ref.at[turn.ahead(k)[1]], qo_ref.at[turn.z], qs, qr)
    turn.end_first(qo_ref.at[turn.z], qs, qr)

    def done_q(k, carry):
        turn.end(k, qo_ref.at[turn.behind(k)[1]], qs, qr)
        return carry

    lax.fori_loop(1, 4, done_q, 0)


def cost(us):
    return pl.CostEstimate(flops=0, transcendentals=0, bytes_accessed=int(us * 3e6))


def remote(number):
    return pltpu.CompilerParams(collective_id=number, has_side_effects=True, vmem_limit_bytes=LIMIT)


def plain():
    return pltpu.CompilerParams(vmem_limit_bytes=LIMIT)


DMA = pltpu.SemaphoreType.DMA


def spread(q, kv):
    return pl.pallas_call(
        spread_kernel,
        name="spread",
        out_shape=(shape(4, ROWS, 256), shape(4, 4, 2, ROWS, HALF)),
        in_specs=[VM, VM],
        out_specs=(VM, VM),
        scratch_shapes=[DMA((4,)), DMA((4,)), DMA((16,)), DMA((16,)), DMA((16,)), DMA((16,))],
        compiler_params=remote(1),
        cost_estimate=cost(30),
    )(q, kv)


def collect(q, kv):
    return pl.pallas_call(
        collect_kernel,
        name="collect",
        out_shape=(shape(4, ROWS, 256), shape(4, 4, ROWS, HALF)),
        in_specs=[VM, VM],
        out_specs=(VM, VM),
        scratch_shapes=[
            pltpu.VMEM((4, 4, ROWS, HALF), BF), pltpu.VMEM((4, 4, ROWS, HALF), BF),
            DMA((4,)), DMA((4,)), DMA((16,)), DMA((16,)), DMA((4,)), DMA((4,)),
        ],
        compiler_params=remote(4),
        cost_estimate=cost(30),
    )(q, kv)


def mates(name, number, pieces):
    return pl.pallas_call(
        mates_kernel,
        name=name,
        out_shape=shape(4, ROWS, 256),
        in_specs=[VM],
        out_specs=VM,
        scratch_shapes=[DMA((4,)), DMA((4,))],
        compiler_params=remote(number),
        cost_estimate=cost(6),
    )(pieces)


def project_kernel(x_ref, wq, wk, wv, small, q_ref, kv_ref, w_ref, vec_ref, bi_ref, small_o, own_sem, a_out, a_in, b_out, b_in):
    y, z, xl, core, half = place()
    across = device(y, z, 1 - xl, core, 1 - half)
    sibling = device(y, z, xl, 1 - core, half)
    barrier = pltpu.get_barrier_semaphore()
    greet(barrier, across)
    greet(barrier, sibling)
    pl.semaphore_wait(barrier, 2)
    start = pl.multiple_of(core * GROUP, GROUP)
    own = pl.multiple_of(half * HALF, HALF)
    give = pl.ds(pl.multiple_of(half * HALF + core * GROUP, GROUP), GROUP)
    take = pl.ds(pl.multiple_of((1 - half) * HALF + core * GROUP, GROUP), GROUP)
    last = pl.ds(pl.multiple_of((1 - half) * HALF + (1 - core) * GROUP, GROUP), GROUP)
    send(small, small_o, a_out.at[3], a_in.at[3], across)
    for i, w in enumerate((wq, wk, wv)):
        send(w.at[pl.ds(start, GROUP)], w_ref.at[i, give], a_out.at[i], a_in.at[i], across)
    mine = [
        pltpu.make_async_copy(w, w_ref.at[i, pl.ds(own, HALF)], own_sem.at[i]) for i, w in enumerate((wq, wk, wv))
    ]
    for copy in mine:
        copy.start()
    finish(small_o, small_o, a_out.at[3], a_in.at[3], across)
    near, far = small[...].astype(F32), small_o[...].astype(F32)
    ahead = jnp.where(half == 0, near, far)
    behind = jnp.where(half == 0, far, near)
    vec_ref[:, :HALF] = ahead[:8]
    vec_ref[:, HALF:] = behind[:8]
    for i in range(4):
        bi_ref[:, i * HALF : (i + 1) * HALF] = ahead[8 + i : 9 + i]
        bi_ref[:, 1536 + i * HALF : 1536 + (i + 1) * HALF] = behind[8 + i : 9 + i]
    x = x_ref[...]
    for i in range(3):
        piece = w_ref.at[i, take]
        finish(piece, piece, a_out.at[i], a_in.at[i], across)
        send(piece, piece, b_out.at[i], b_in.at[i], sibling)
    done = []
    for i in range(3):
        piece = w_ref.at[i, last]
        finish(piece, piece, b_out.at[i], b_in.at[i], sibling)
        mine[i].wait()
        done.append(nn(x, w_ref[i]))
    pad = jnp.zeros((ROWS, 64), BF)
    query = (done[0] + vec_ref[0:1, :]).astype(BF) * BF(0.125)
    keys = done[1].astype(BF)
    values = (done[2] + vec_ref[1:2, :]).astype(BF)
    for g in range(4):
        cut = slice(g * GROUP, (g + 1) * GROUP)
        q_ref[g] = jnp.concatenate([query[:, cut], pad], axis=1)
        kv_ref[g] = jnp.concatenate([keys[:, cut], values[:, cut]], axis=1)


def project(x, wq, wk, wv, small):
    return pl.pallas_call(
        project_kernel,
        name="project",
        out_shape=(
            shape(4, ROWS, 256), shape(4, ROWS, HALF), shape(3, D, D), shape(8, D, dtype=F32), shape(1, FF, dtype=F32),
        ),
        in_specs=[VM, ANY, ANY, ANY, VM],
        out_specs=(VM,) * 5,
        scratch_shapes=[pltpu.VMEM((16, HALF), BF), DMA((3,)), DMA((4,)), DMA((4,)), DMA((3,)), DMA((3,))],
        compiler_params=remote(6),
        cost_estimate=cost(25),
    )(x, wq, wk, wv, small)


CHUNK = 256


def load_chunk(ref, i):
    y, z = pair(i)
    return ref[y, z].reshape(CHUNK, HALF)


def stack_head(ref, h):
    return jnp.concatenate([ref[i][:, h * HD : (h + 1) * HD] for i in range(4)], axis=0)


def turned(rows):
    return rows.astype(F32).T.astype(BF)


def attend_kernel(q_ref, kv_ref, o_ref, ot_ref, lse_ref, qt, top, total):
    for h in range(3):
        qt[h] = turned(stack_head(q_ref, h))
    top[...] = jnp.full_like(top, -jnp.inf)
    total[...] = jnp.zeros_like(total)
    ot_ref[...] = jnp.zeros_like(ot_ref)

    def body(i, carry):
        kv = load_chunk(kv_ref, i)
        for h in range(3):
            scores = nn(kv[:, h * HD : (h + 1) * HD], qt[h])
            old = top[h]
            new = jnp.maximum(old, jnp.max(scores, axis=0, keepdims=True))
            shrink = jnp.exp(old - new)
            weights = jnp.exp(scores - new)
            total[h] = total[h] * shrink + jnp.sum(weights, axis=0, keepdims=True)
            mixed = tn(kv[:, GROUP + h * HD : GROUP + (h + 1) * HD], weights.astype(BF))
            ot_ref[h] = ot_ref[h] * shrink + mixed
            top[h] = new
        return carry

    lax.fori_loop(0, 4096 // CHUNK, body, 0)
    heads = []
    for h in range(3):
        lse_ref[h] = top[h] + jnp.log(total[h])
        normal = ot_ref[h] / total[h]
        ot_ref[h] = normal
        heads.append(normal.T.astype(BF))
    heads.append(jnp.zeros((512, 64), BF))
    out = jnp.concatenate(heads, axis=1)
    for i in range(4):
        o_ref[i] = out[i * ROWS : (i + 1) * ROWS]


def attend(q, kv):
    return pl.pallas_call(
        attend_kernel,
        name="attend",
        cost_estimate=cost(20),
        out_shape=(shape(4, ROWS, 256), shape(3, HD, 512, dtype=F32), shape(3, 1, 512, dtype=F32)),
        in_specs=[VM, VM],
        out_specs=(VM, VM, VM),
        scratch_shapes=[
            pltpu.VMEM((3, HD, 512), BF), pltpu.VMEM((3, 1, 512), F32), pltpu.VMEM((3, 1, 512), F32),
        ],
        compiler_params=plain(),
    )(q, kv)


def attend_back_kernel(q_ref, kv_ref, da_ref, ot_ref, lse_ref, dq_ref, dkv_ref, qs, qt, ds, dt, delta, acc):
    for h in range(3):
        rows = stack_head(q_ref, h)
        qs[h] = rows
        qt[h] = turned(rows)
        rows = stack_head(da_ref, h)
        ds[h] = rows
        flipped = rows.astype(F32).T
        dt[h] = flipped.astype(BF)
        delta[h] = jnp.sum(flipped * ot_ref[h], axis=0, keepdims=True)
    acc[...] = jnp.zeros_like(acc)

    def body(i, carry):
        kv = load_chunk(kv_ref, i)
        keys, values = [], []
        for h in range(3):
            k = kv[:, h * HD : (h + 1) * HD]
            v = kv[:, GROUP + h * HD : GROUP + (h + 1) * HD]
            probs = jnp.exp(nn(k, qt[h]) - lse_ref[h])
            slopes = (probs * (nn(v, dt[h]) - delta[h])).astype(BF)
            keys.append(nn(slopes, qs[h]).astype(BF))
            values.append(nn(probs.astype(BF), ds[h]).astype(BF))
            acc[h] += tn(k, slopes)
        y, z = pair(i)
        dkv_ref[y, z] = jnp.concatenate(keys + values, axis=1).reshape(2, ROWS, HALF)
        return carry

    lax.fori_loop(0, 4096 // CHUNK, body, 0)
    heads = [(acc[h] * 0.125).T.astype(BF) for h in range(3)]
    heads.append(jnp.zeros((512, 64), BF))
    out = jnp.concatenate(heads, axis=1)
    for i in range(4):
        dq_ref[i] = out[i * ROWS : (i + 1) * ROWS]


def attend_back(q, kv, da, ot, lse):
    return pl.pallas_call(
        attend_back_kernel,
        name="attend_back",
        cost_estimate=cost(25),
        out_shape=(shape(4, ROWS, 256), shape(4, 4, 2, ROWS, HALF)),
        in_specs=[VM] * 5,
        out_specs=(VM, VM),
        scratch_shapes=[
            pltpu.VMEM((3, 512, HD), BF), pltpu.VMEM((3, HD, 512), BF),
            pltpu.VMEM((3, 512, HD), BF), pltpu.VMEM((3, HD, 512), BF),
            pltpu.VMEM((3, 1, 512), F32), pltpu.VMEM((3, HD, 512), F32),
        ],
        compiler_params=plain(),
    )(q, kv, da, ot, lse)


def norm(hidden):
    centred = hidden - jnp.mean(hidden, axis=-1, keepdims=True)
    inverse = lax.rsqrt(jnp.mean(centred * centred, axis=-1, keepdims=True) + EPS)
    return centred * inverse, inverse


def norm_back(scaled, normal, inverse):
    centre = jnp.mean(scaled, axis=-1, keepdims=True)
    along = jnp.mean(scaled * normal, axis=-1, keepdims=True)
    return inverse * (scaled - centre - normal * along)


def column(value):
    return jnp.sum(value, axis=0, keepdims=True)


def block_kernel(
    x_ref, ct_ref, a_ref, wo, wo_a, wo_b, wi, wi_a, wi_b, wu, wu_a, wu_b, vec_ref, bi_ref,
    out_ref, dh1_ref, da_ref, af_ref, yb_ref, g_ref, df_ref, du_ref, dz_ref, vg_ref,
    w_o, w_i, w_u, slope, sems,
):
    core = lax.axis_index("seq")
    half = lax.axis_index("fsdp")
    copies = []
    for i, (own, first, second, full, size) in enumerate(
        ((wo, wo_a, wo_b, w_o, HALF), (wi, wi_a, wi_b, w_i, HALF), (wu, wu_a, wu_b, w_u, FF // 2))
    ):
        q = size // 2
        at = pl.multiple_of(half * size, size)
        at_a = pl.multiple_of((1 - half) * size + core * q, q)
        at_b = pl.multiple_of((1 - half) * size + (1 - core) * q, q)
        copies.append(
            (
                pltpu.make_async_copy(own, full.at[pl.ds(at, size)], sems.at[3 * i]),
                pltpu.make_async_copy(first, full.at[pl.ds(at_a, q)], sems.at[3 * i + 1]),
                pltpu.make_async_copy(second, full.at[pl.ds(at_b, q)], sems.at[3 * i + 2]),
            )
        )
    for group in copies:
        for copy in group:
            copy.start()
    b_output, first_gain, first_shift = vec_ref[2:3, :], vec_ref[3:4, :], vec_ref[4:5, :]
    b_outer, second_gain, second_shift = vec_ref[5:6, :], vec_ref[6:7, :], vec_ref[7:8, :]
    mixed = jnp.concatenate([a_ref[g][:, :GROUP] for g in range(4)], axis=1)
    af_ref[...] = mixed
    for copy in copies[0]:
        copy.wait()
    hidden = x_ref[...].astype(F32) + nn(mixed, w_o[...]) + b_output
    normal1, inverse1 = norm(hidden)
    normed = normal1 * first_gain + first_shift
    low = normed.astype(BF)
    yb_ref[...] = low
    for group in copies[1:]:
        for copy in group:
            copy.wait()
    second_in = normed + b_outer
    for j in range(4):
        cut = slice(j * D, (j + 1) * D)
        inner = nn(low, w_i[:, cut]) + bi_ref[:, cut]
        cdf = 0.5 * (1.0 + lax.erf(inner * (0.5**0.5)))
        active = (inner * cdf).astype(BF)
        slope[:, cut] = cdf + inner * jnp.exp(inner * inner * -0.5) * 0.3989422804014327
        g_ref[:, cut] = active
        second_in = second_in + nn(active, w_u[cut, :])
    normal2, inverse2 = norm(second_in)
    out_ref[...] = (normal2 * second_gain + second_shift).astype(BF)
    upper = ct_ref[...].astype(F32)


    def note(row, value):
        for h in range(2):
            vg_ref[h, row : row + 1, :] = value[:, h * HALF : (h + 1) * HALF]

    vg_ref[...] = jnp.zeros_like(vg_ref)
    note(6, column(upper * normal2))
    note(7, column(upper))
    dh2 = norm_back(upper * second_gain, normal2, inverse2)
    df = dh2.astype(BF)
    df_ref[...] = df
    note(5, column(df.astype(F32)))
    dy1 = dh2
    for j in range(4):
        cut = slice(j * D, (j + 1) * D)
        du = (slope[:, cut] * nt(df, w_u[cut, :])).astype(BF)
        du_ref[:, cut] = du
        sums = column(du.astype(F32))
        for i in range(2):
            n = 2 * j + i
            vg_ref[n // 4, 8 + n % 4 : 9 + n % 4, :] = sums[:, i * HALF : (i + 1) * HALF]
        dy1 = dy1 + nt(du, w_i[:, cut])
    note(3, column(dy1 * normal1))
    note(4, column(dy1))
    dh1 = norm_back(dy1 * first_gain, normal1, inverse1)
    dh1_ref[...] = dh1
    dz = dh1.astype(BF)
    dz_ref[...] = dz
    note(2, column(dz.astype(F32)))
    da = nt(dz, w_o[...]).astype(BF)
    pad = jnp.zeros((ROWS, 64), BF)
    for g in range(4):
        da_ref[g] = jnp.concatenate([da[:, g * GROUP : (g + 1) * GROUP], pad], axis=1)


def block(x, ct, a, weights, vec, b_inner):
    return pl.pallas_call(
        block_kernel,
        name="block",
        cost_estimate=cost(12),
        out_shape=(
            shape(ROWS, D), shape(ROWS, D, dtype=F32), shape(4, ROWS, 256), shape(ROWS, D), shape(ROWS, D),
            shape(ROWS, FF), shape(ROWS, D), shape(ROWS, FF), shape(ROWS, D),
            shape(2, 16, HALF, dtype=F32),
        ),
        in_specs=[VM, VM, VM] + [ANY] * 9 + [VM, VM],
        out_specs=(VM,) * 10,
        scratch_shapes=[
            pltpu.VMEM((D, D), BF), pltpu.VMEM((D, FF), BF), pltpu.VMEM((FF, D), BF),
            pltpu.VMEM((ROWS, FF), F32), pltpu.SemaphoreType.DMA((9,)),
        ],
        compiler_params=plain(),
    )(x, ct, a, *weights, vec, b_inner)


def put(ref, at, value):
    ref[at] = value.astype(BF).reshape(4, 2, 48, HALF)


def wide_kernel(yb, yb_o, g, g_o, a, a_o, df, df_o, du, du_o, dz, dz_o, one_ref, two_ref, zero_ref):
    core = lax.axis_index("seq")

    def right(ref, other, start):
        cols = pl.ds(pl.multiple_of(start + core * HALF, HALF), HALF)
        return jnp.concatenate([ref[:, cols], other[:, cols]], axis=0)

    def left(ref, other, start):
        return jnp.concatenate([ref[:, start : start + HALF], other[:, start : start + HALF]], axis=0)

    outer = right(df, df_o, 0)
    attn = right(dz, dz_o, 0)
    for half in range(2):
        for m in range(4):
            put(one_ref, (half, m), tn(left(g, g_o, half * 1536 + m * HALF), outer))
        rows = left(yb, yb_o, half * HALF)
        for m in range(4):
            put(two_ref, (half, m), tn(rows, right(du, du_o, m * D)))
        put(zero_ref, half, tn(left(a, a_o, half * HALF), attn))


def wide(*arrays):
    return pl.pallas_call(
        wide_kernel,
        name="wide",
        cost_estimate=cost(6),
        out_shape=(shape(2, 4, 4, 2, 48, HALF), shape(2, 4, 4, 2, 48, HALF), shape(2, 4, 2, 48, HALF)),
        in_specs=[VM] * 12,
        out_specs=(VM, VM, VM),
        compiler_params=plain(),
    )(*arrays)


def tail_kernel(dq_ref, dkv_ref, dh1_ref, w_ref, vg_ref, grad_ref, low_ref, vo_ref):
    low_ref[0] = jnp.concatenate([dq_ref[g][:, :GROUP] for g in range(4)], axis=1)
    sums = []
    for g in range(4):
        total = dkv_ref[0, g].astype(F32)
        for k in range(1, 4):
            total = total + dkv_ref[k, g].astype(F32)
        sums.append(total.astype(BF))
    low_ref[1] = jnp.concatenate([s[:, :GROUP] for s in sums], axis=1)
    low_ref[2] = jnp.concatenate([s[:, GROUP:] for s in sums], axis=1)
    grad = dh1_ref[...]
    for i in range(3):
        grad = grad + nt(low_ref[i], w_ref[i])
    grad_ref[...] = grad
    vo_ref[...] = vg_ref[...]
    for row, i in ((0, 0), (1, 2)):
        value = column(low_ref[i].astype(F32))
        for h in range(2):
            vo_ref[h, row : row + 1, :] = value[:, h * HALF : (h + 1) * HALF]


def tail(*arrays):
    return pl.pallas_call(
        tail_kernel,
        name="tail",
        out_shape=(shape(ROWS, D, dtype=F32), shape(3, ROWS, D), shape(2, 16, HALF, dtype=F32)),
        in_specs=[VM] * 5,
        out_specs=(VM,) * 3,
        compiler_params=plain(),
        cost_estimate=cost(6),
    )(*arrays)


def narrow_kernel(x, x_o, low, low_o, attn_ref, zero_ref):
    core = lax.axis_index("seq")
    cols = pl.ds(pl.multiple_of(core * HALF, HALF), HALF)
    for half in range(2):
        cut = slice(half * HALF, (half + 1) * HALF)
        rows = jnp.concatenate([x[:, cut], x_o[:, cut]], axis=0)
        for m in range(3):
            put(zero_ref, (half, m), tn(rows, jnp.concatenate([low[m, :, cols], low_o[m, :, cols]], axis=0)))
        zero_ref[half, 3] = attn_ref[half]


def narrow(*arrays):
    return pl.pallas_call(
        narrow_kernel,
        name="narrow",
        cost_estimate=cost(4),
        out_shape=shape(2, 4, 4, 2, 48, HALF),
        in_specs=[VM] * 5,
        out_specs=VM,
        compiler_params=plain(),
    )(*arrays)


def reduce_kernel(
    g0, g1, g2, vg, out, vo, r0, r1, r2, s0, s1, s2, t0, t1, t2, rv, sv, tv, uv,
    a_out, a_in, b_out, b_in, c_out, c_in, d_out, d_in, e_out, e_in,
):
    y, z, xl, core, half = place()
    x = half * 2 + xl
    barrier = pltpu.get_barrier_semaphore()

    def along_x(k):
        e = wrap(x + k, 4)
        return device(y, z, lax.rem(e, 2), core, lax.div(e, 2))

    def at_yz(k):
        i, j = pair(k)
        return device(wrap(y + i, 4), wrap(z + j, 4), xl, core, half)

    def at_xz(k):
        i, j = pair(k)
        e = wrap(x + i, 4)
        return device(y, wrap(z + j, 4), lax.rem(e, 2), core, lax.div(e, 2))

    def at_xy(k):
        i, j = pair(k)
        e = wrap(x + i, 4)
        return device(wrap(y + j, 4), z, lax.rem(e, 2), core, lax.div(e, 2))

    def hello_yz(k, carry):
        greet(barrier, at_yz(k))
        return carry

    def hello_x(k, carry):
        i = lax.div(k - 1, 3) + 1
        j = lax.rem(k - 1, 3) + 1
        greet(barrier, at_xz(i * 4 + j))
        greet(barrier, at_xy(i * 4 + j))
        return carry

    def hello_row(k, carry):
        greet(barrier, along_x(k))
        return carry

    lax.fori_loop(1, 16, hello_yz, 0)
    lax.fori_loop(1, 10, hello_x, 0)
    lax.fori_loop(1, 4, hello_row, 0)
    greet(barrier, device(y, z, xl, 1 - core, half))
    pl.semaphore_wait(barrier, 37)

    def first(k, carry):
        e = wrap(x + k, 4)
        send(g0.at[lax.div(e, 2), :, :, lax.rem(e, 2)], r0.at[k - 1], a_out.at[0, k], a_in.at[0, k], along_x(k))
        send(g1.at[:, wrap(y + k, 4)], r1.at[k - 1], a_out.at[1, k], a_in.at[1, k], at_yz(k * 4))
        send(g2.at[:, :, wrap(z + k, 4)], r2.at[k - 1], a_out.at[2, k], a_in.at[2, k], at_yz(k))
        send(vg.at[lax.div(e, 2)], rv.at[k - 1], a_out.at[3, k], a_in.at[3, k], along_x(k))
        return carry

    lax.fori_loop(1, 4, first, 0)
    here = device(y, z, xl, core, half)

    def sum1(own, got, to, sem):
        for k in range(1, 4):
            finish(got.at[k - 1], got.at[k - 1], a_out.at[sem, k], a_in.at[sem, k], here)

        def add(i, carry):
            p, q, o = own(i)
            total = o.astype(F32)
            for k in range(3):
                total = total + got[(k,) + p].astype(F32)
            to[q] = total.astype(BF)
            return carry

        lax.fori_loop(0, 16, add, 0)

    def own0(i):
        p, q = pair(i)
        return (p, q), (p, q), g0[half, p, q, xl]

    def own1(i):
        f, q, r = lax.div(i, 8), lax.rem(lax.div(i, 2), 4), lax.rem(i, 2)
        return (f, q, r), (f, q, r), g1[f, y, q, r]

    def own2(i):
        f, q, r = lax.div(i, 8), lax.rem(lax.div(i, 2), 4), lax.rem(i, 2)
        return (f, q, r), (f, q, r), g2[f, q, z, r]

    for k in range(1, 4):
        finish(rv.at[k - 1], rv.at[k - 1], a_out.at[3, k], a_in.at[3, k], here)
    part = vg[half] + rv[0] + rv[1] + rv[2]
    sv[...] = part.astype(BF)

    def second3(k, carry):
        send(sv, tv.at[k], b_out.at[3, k], b_in.at[3, k], at_yz(k))
        return carry

    lax.fori_loop(1, 16, second3, 0)
    sum1(own1, r1, s1, 1)

    def second1(k, carry):
        i, j = pair(k)
        e = wrap(x + i, 4)
        send(s1.at[lax.div(e, 2), wrap(z + j, 4), lax.rem(e, 2)], t1.at[k], b_out.at[1, k], b_in.at[1, k], at_xz(k))
        return carry

    lax.fori_loop(1, 16, second1, 0)
    sum1(own2, r2, s2, 2)

    def second2(k, carry):
        i, j = pair(k)
        e = wrap(x + i, 4)
        send(s2.at[lax.div(e, 2), wrap(y + j, 4), lax.rem(e, 2)], t2.at[k], b_out.at[2, k], b_in.at[2, k], at_xy(k))
        return carry

    lax.fori_loop(1, 16, second2, 0)
    sum1(own0, r0, s0, 0)

    def second0(k, carry):
        i, j = pair(k)
        send(s0.at[wrap(y + i, 4), wrap(z + j, 4)], t0.at[k], b_out.at[0, k], b_in.at[0, k], at_yz(k))
        return carry

    lax.fori_loop(1, 16, second0, 0)

    def sum2(own, got, slab):
        def done(k, carry):
            finish(got.at[k], got.at[k], b_out.at[slab, k], b_in.at[slab, k], here)
            return carry

        lax.fori_loop(1, 16, done, 0)

        def add(k, total):
            return total + got[k].astype(F32)

        total = lax.fori_loop(1, 16, add, own.astype(F32))
        out[core, slab, y, z, xl] = total.astype(BF)

    def done3(k, total):
        finish(tv.at[k], tv.at[k], b_out.at[3, k], b_in.at[3, k], here)
        return total + tv[k].astype(F32)

    vo[...] = lax.fori_loop(1, 16, done3, part)
    sibling = device(y, z, xl, 1 - core, half)
    send(vo, uv, e_out.at[3], e_in.at[3], sibling)

    sum2(s1[half, z, xl], t1, 1)

    def third1(k, carry):
        i, j = lax.rem(k, 2), lax.div(k, 2)
        mine = out.at[core, 1, y, z, xl]
        send(mine, mine, c_out.at[1, k], c_in.at[1, k], device(y, wrap(z + j, 4), wrap(xl + i, 2), core, half))
        return carry

    lax.fori_loop(1, 8, third1, 0)
    sum2(s2[half, y, xl], t2, 2)

    def third2(k, carry):
        i, j = lax.rem(k, 2), lax.div(k, 2)
        mine = out.at[core, 2, y, z, xl]
        send(mine, mine, c_out.at[2, k], c_in.at[2, k], device(wrap(y + j, 4), z, wrap(xl + i, 2), core, half))
        return carry

    lax.fori_loop(1, 8, third2, 0)
    sum2(s0[y, z], t0, 0)

    def third0(k, carry):
        mine = out.at[core, 0, y, z, xl]
        send(mine, mine, c_out.at[0, k], c_in.at[0, k], at_yz(k))
        return carry

    lax.fori_loop(1, 16, third0, 0)

    def got1(k, carry):
        i, j = lax.rem(k, 2), lax.div(k, 2)
        piece = out.at[core, 1, y, wrap(z - j, 4), wrap(xl - i, 2)]
        finish(piece, piece, c_out.at[1, k], c_in.at[1, k], here)
        return carry

    lax.fori_loop(1, 8, got1, 0)

    def fourth1(k, carry):
        mine = out.at[core, 1, y]
        send(mine, mine, d_out.at[1, k], d_in.at[1, k], at_yz(k * 4))
        return carry

    lax.fori_loop(1, 4, fourth1, 0)

    def got2(k, carry):
        i, j = lax.rem(k, 2), lax.div(k, 2)
        piece = out.at[core, 2, wrap(y - j, 4), z, wrap(xl - i, 2)]
        finish(piece, piece, c_out.at[2, k], c_in.at[2, k], here)
        return carry

    lax.fori_loop(1, 8, got2, 0)

    def fourth2(k, carry):
        mine = out.at[core, 2, :, z]
        send(mine, mine, d_out.at[2, k], d_in.at[2, k], at_yz(k))
        return carry

    lax.fori_loop(1, 4, fourth2, 0)

    def got0(k, carry):
        i, j = pair(k)
        piece = out.at[core, 0, wrap(y - i, 4), wrap(z - j, 4), xl]
        finish(piece, piece, c_out.at[0, k], c_in.at[0, k], here)
        return carry

    lax.fori_loop(1, 16, got0, 0)
    mine0 = out.at[core, 0, :, :, xl]
    send(mine0, mine0, d_out.at[0, 1], d_in.at[0, 1], device(y, z, 1 - xl, core, half))

    def last1(k, carry):
        piece = out.at[core, 1, wrap(y - k, 4)]
        finish(piece, piece, d_out.at[1, k], d_in.at[1, k], here)
        return carry

    def last2(k, carry):
        piece = out.at[core, 2, :, wrap(z - k, 4)]
        finish(piece, piece, d_out.at[2, k], d_in.at[2, k], here)
        return carry

    lax.fori_loop(1, 4, last1, 0)
    send(out.at[core, 1], out.at[core, 1], e_out.at[1], e_in.at[1], sibling)
    lax.fori_loop(1, 4, last2, 0)
    send(out.at[core, 2], out.at[core, 2], e_out.at[2], e_in.at[2], sibling)
    piece0 = out.at[core, 0, :, :, 1 - xl]
    finish(piece0, piece0, d_out.at[0, 1], d_in.at[0, 1], here)
    send(out.at[core, 0], out.at[core, 0], e_out.at[0], e_in.at[0], sibling)
    for slab in (1, 2, 0):
        piece = out.at[1 - core, slab]
        finish(piece, piece, e_out.at[slab], e_in.at[slab], here)
    finish(uv, uv, e_out.at[3], e_in.at[3], here)
    vo[...] = vo[...] + uv[...]


def reduce(g0, g1, g2, vg):
    dma = pltpu.SemaphoreType.DMA
    blk = (48, HALF)
    return pl.pallas_call(
        reduce_kernel,
        name="reduce",
        out_shape=(shape(2, 3, 4, 4, 2, *blk), shape(16, HALF, dtype=F32)),
        in_specs=[VM] * 4,
        out_specs=(VM, VM),
        scratch_shapes=[
            pltpu.VMEM((3, 4, 4, *blk), BF), pltpu.VMEM((3, 2, 4, 2, *blk), BF), pltpu.VMEM((3, 2, 4, 2, *blk), BF),
            pltpu.VMEM((4, 4, *blk), BF), pltpu.VMEM((2, 4, 2, *blk), BF), pltpu.VMEM((2, 4, 2, *blk), BF),
            pltpu.VMEM((16, *blk), BF), pltpu.VMEM((16, *blk), BF), pltpu.VMEM((16, *blk), BF),
            pltpu.VMEM((3, 16, HALF), F32), pltpu.VMEM((16, HALF), BF), pltpu.VMEM((16, 16, HALF), BF),
            pltpu.VMEM((16, HALF), F32),
            dma((4, 4)), dma((4, 4)), dma((4, 16)), dma((4, 16)), dma((3, 16)), dma((3, 16)),
            dma((3, 4)), dma((3, 4)), dma((4,)), dma((4,)),
        ],
        compiler_params=pltpu.CompilerParams(
            collective_id=5, has_side_effects=True, vmem_limit_bytes=LIMIT
        ),
        cost_estimate=cost(80),
    )(g0, g1, g2, vg)


def spell_kernel(zero, one, two, q_ref, k_ref, v_ref, o_ref, i_ref, u_ref):
    for c in range(2):
        cols = slice(c * HALF, (c + 1) * HALF)
        for m, ref in enumerate((q_ref, k_ref, v_ref, o_ref)):
            ref[:, cols] = zero[c, 0, m, 0].astype(F32)
            i_ref[:, m * D + c * HALF : m * D + (c + 1) * HALF] = two[c, 0, m, 0].astype(F32)
            u_ref[m * 48 : (m + 1) * 48, cols] = one[c, 0, 0, m].astype(F32)


def spell(summed):
    summed = summed.reshape(2, 3, 4, 8, 48, HALF)
    part = pl.BlockSpec((48, D), lambda i: (i, 0))
    return pl.pallas_call(
        spell_kernel,
        name="spell",
        grid=(8,),
        out_shape=tuple(
            shape(*dims, dtype=F32) for dims in ((HALF, D), (HALF, D), (HALF, D), (HALF, D), (HALF, FF), (1536, D))
        ),
        in_specs=[
            pl.BlockSpec((2, 1, 4, 1, 48, HALF), lambda i: (0, 0, 0, i, 0, 0)),
            pl.BlockSpec((2, 1, 1, 4, 48, HALF), lambda i: (0, 1, i // 2, i % 2, 0, 0)),
            pl.BlockSpec((2, 1, 4, 1, 48, HALF), lambda i: (0, 2, 0, i, 0, 0)),
        ],
        out_specs=(part, part, part, part, pl.BlockSpec((48, FF), lambda i: (i, 0)), pl.BlockSpec((192, D), lambda i: (i, 0))),
        compiler_params=plain(),
        cost_estimate=cost(6),
    )(summed, summed, summed)


def swap_halves(array):
    pairs = []
    for ctx in range(32):
        for core in range(2):
            for half in range(2):
                there = (ctx // 2) * 2 + (1 - ctx % 2)
                pairs.append(((ctx * 2 + core) * 2 + half, (there * 2 + core) * 2 + 1 - half))
    return lax.ppermute(array, AXES, pairs)


def swap_cores(array):
    return lax.ppermute(array, "seq", [(0, 1), (1, 0)])


def local(
    tokens, cotangent, w_query, w_key, w_value, w_output, b_query, b_value, b_output,
    first_gain, first_shift, w_inner, b_inner, w_outer, b_outer, second_gain, second_shift,
):
    core = lax.axis_index("seq")
    half = lax.axis_index("fsdp")
    x = tokens[0]

    def share(w):
        return lax.dynamic_slice_in_dim(w, core * (w.shape[0] // 2), w.shape[0] // 2, 0)

    rows = [b_query, b_value, b_output, first_gain, first_shift, b_outer, second_gain, second_shift]
    small = jnp.concatenate(
        [v.reshape(1, HALF) for v in rows] + [b_inner.reshape(4, HALF), jnp.zeros((4, HALF), BF)], axis=0
    )
    q, kv, w_qkv, vec, bi = project(x, w_query, w_key, w_value, small)
    later = tuple(share(w) for w in (w_output, w_inner, w_outer))
    later, q = lax.optimization_barrier((later, q))
    later = [swap_halves(w) for w in later]
    q_all, kv_all = spread(q, kv)
    mixed, mixed_t, lse = attend(q_all, kv_all)
    mixed, later = lax.optimization_barrier((mixed, later))
    others = [swap_cores(w) for w in later]
    mixed = mates("mates_out", 2, mixed)
    weights = []
    for own, a, b in zip((w_output, w_inner, w_outer), later, others):
        weights += [own, a, b]
    layer_out, dh1, da, a_full, yb, g, df, du, dz, vg = block(x, cotangent[0], mixed, weights, vec, bi)
    da_all = mates("mates_in", 3, da)
    acts = (yb, g, a_full, df, du, dz)
    acts_o = [swap_cores(v) for v in acts]
    x_o = swap_cores(x)
    g1, g2, g0o = wide(*[v for pair in zip(acts, acts_o) for v in pair])
    dq, dkv = attend_back(q_all, kv_all, da_all, mixed_t, lse)
    dq, dkv = collect(dq, dkv)
    tokens_grad, low, vg = tail(dq, dkv, dh1, w_qkv, vg)
    low_o = swap_cores(low)
    g0 = narrow(x, x_o, low, low_o, g0o)
    summed, vecs = reduce(g0, g1, g2, vg)
    gq, gk, gv, go, gi, gu = spell(summed)
    return (
        layer_out[None], tokens_grad[None], gq, gk, gv, go,
        vecs[0], vecs[1], vecs[2], vecs[3], vecs[4], gi, vecs[8:12].reshape(1536), gu, vecs[5], vecs[6], vecs[7],
    )


def solution(mesh):
    rows = P(("seq", "fsdp"), "ctx", None)
    mat = P("fsdp", None)
    vec = P("fsdp")
    return jax.shard_map(
        local,
        mesh=mesh,
        in_specs=(rows, rows, mat, mat, mat, mat, vec, vec, vec, vec, vec, mat, vec, mat, vec, vec, vec),
        out_specs=(rows, rows, mat, mat, mat, mat, vec, vec, vec, vec, vec, mat, vec, mat, vec, vec, vec),
        check_vma=False,
    )
```

```python
import functools

import jax
import jax.numpy as jnp
from jax import lax
from jax.experimental import pallas as pl
from jax.experimental.pallas import tpu as pltpu
from jax.sharding import PartitionSpec as P

AXES = ("ctx", "seq", "fsdp")
MESH = pl.DeviceIdType.MESH
BF = jnp.bfloat16
F32 = jnp.float32
D = 768
FF = 3072
HALF = 384
GROUP = 192
HD = 64
ROWS = 128
EPS = 1e-12
LIMIT = 24 << 20
VM = pl.BlockSpec(memory_space=pltpu.VMEM)
ANY = pl.BlockSpec(memory_space=pltpu.HBM)


def plain_shape(*dims, dtype=BF):
    return jax.ShapeDtypeStruct(dims, dtype)


def shape(*dims, dtype=BF):
    return pltpu.VMEM(dims, dtype)


def hbm(array):
    return pltpu.with_memory_space_constraint(array, pltpu.HBM)


def vm(array):
    return pltpu.with_memory_space_constraint(array, pltpu.VMEM)


def nn(left, right):
    return jnp.dot(left, right, preferred_element_type=F32)


def nt(left, right):
    return lax.dot_general(left, right, (((1,), (1,)), ((), ())), preferred_element_type=F32)


def tn(left, right):
    return lax.dot_general(left, right, (((0,), (0,)), ((), ())), preferred_element_type=F32)


def wrap(value, size):
    return lax.rem(value + size, size)


def place():
    ctx = lax.axis_index("ctx")
    y = lax.div(ctx, 8)
    z = lax.rem(lax.div(ctx, 2), 4)
    return y, z, lax.rem(ctx, 2), lax.axis_index("seq"), lax.axis_index("fsdp")


def device(y, z, xl, core, half):
    return ((y * 4 + z) * 2 + xl, core, half)


def send(src, dst, out_sem, in_sem, where):
    pltpu.make_async_remote_copy(
        src_ref=src, dst_ref=dst, send_sem=out_sem, recv_sem=in_sem,
        device_id=where, device_id_type=MESH,
    ).start()


def finish(src, dst, out_sem, in_sem, where):
    copy = pltpu.make_async_remote_copy(
        src_ref=src, dst_ref=dst, send_sem=out_sem, recv_sem=in_sem,
        device_id=where, device_id_type=MESH,
    )
    copy.wait_send()
    copy.wait_recv()


def greet(barrier, where):
    pl.semaphore_signal(barrier, inc=1, device_id=where, device_id_type=MESH)


def pair(k):
    return lax.div(k, 4), lax.rem(k, 4)


class Turn:
    def __init__(self):
        self.y, self.z, self.xl, self.core, self.half = place()
        self.stays = self.xl == self.core

    def partner(self, k):
        i, j = pair(k)
        return device(wrap(self.y + i, 4), wrap(self.z + j, 4), self.core, self.xl, self.half)

    def ahead(self, k):
        i, j = pair(k)
        return wrap(self.y + i, 4), wrap(self.z + j, 4)

    def behind(self, k):
        i, j = pair(k)
        return wrap(self.y - i, 4), wrap(self.z - j, 4)

    def sibling(self):
        return device(self.y, self.z, self.xl, 1 - self.core, self.half)

    def hello(self, count, others=()):
        barrier = pltpu.get_barrier_semaphore()

        def one(k, carry):
            greet(barrier, self.partner(k))
            return carry

        lax.fori_loop(1, count, one, 0)
        for where in others:
            greet(barrier, where)

        @pl.when(jnp.logical_not(self.stays))
        def _():
            greet(barrier, self.partner(0))

    def ready(self, count, others=0):
        barrier = pltpu.get_barrier_semaphore()
        pl.semaphore_wait(barrier, count - 1 + others + lax.rem(self.xl + self.core, 2))

    def start(self, count, src, dst, outs, ins):
        def push(k, carry):
            send(src(k), dst, outs.at[k], ins.at[k], self.partner(k))
            return carry

        @pl.when(self.stays)
        def _():
            pltpu.make_async_copy(src(0), dst, ins.at[0]).start()

        @pl.when(jnp.logical_not(self.stays))
        def _():
            push(0, 0)

        lax.fori_loop(1, count, push, 0)

    def end(self, k, got, outs, ins):
        finish(got, got, outs.at[k], ins.at[k], self.partner(k))

    def end_first(self, got, outs, ins):
        @pl.when(self.stays)
        def _():
            pltpu.make_async_copy(got, got, ins.at[0]).wait()

        @pl.when(jnp.logical_not(self.stays))
        def _():
            self.end(0, got, outs, ins)


def collect_kernel(q_ref, kv_ref, qo_ref, kvo_ref, other, both, qs, qr, ks, kr, fs, fr):
    turn = Turn()
    y, z, xl, core = turn.y, turn.z, turn.xl, turn.core
    turn.hello(16, (turn.sibling(),))
    turn.ready(16, 1)
    for i in range(4):
        send(kv_ref.at[i, :, 1 - core], other.at[i], fs.at[i], fr.at[i], turn.sibling())
    turn.start(4, lambda k: q_ref.at[turn.ahead(k)[1]], qo_ref.at[z], qs, qr)
    for i in range(4):
        finish(other.at[i], other.at[i], fs.at[i], fr.at[i], turn.sibling())

    def add(k, carry):
        i, j = pair(k)
        both[i, j] = (kv_ref[i, j, core].astype(F32) + other[i, j].astype(F32)).astype(BF)
        return carry

    lax.fori_loop(0, 16, add, 0)
    turn.start(16, lambda k: both.at[turn.ahead(k)], kvo_ref.at[y, z], ks, kr)
    turn.end_first(qo_ref.at[z], qs, qr)

    def done_q(k, carry):
        turn.end(k, qo_ref.at[turn.behind(k)[1]], qs, qr)
        return carry

    lax.fori_loop(1, 4, done_q, 0)
    turn.end_first(kvo_ref.at[y, z], ks, kr)

    def done(k, carry):
        turn.end(k, kvo_ref.at[turn.behind(k)], ks, kr)
        return carry

    lax.fori_loop(1, 16, done, 0)


def cost(us):
    return pl.CostEstimate(flops=0, transcendentals=0, bytes_accessed=int(us * 3e6))


def remote(number):
    return pltpu.CompilerParams(collective_id=number, has_side_effects=True, vmem_limit_bytes=LIMIT)


def plain():
    return pltpu.CompilerParams(vmem_limit_bytes=LIMIT)


DMA = pltpu.SemaphoreType.DMA


def collect(q, kv):
    return pl.pallas_call(
        collect_kernel,
        name="collect",
        out_shape=(shape(4, ROWS, 256), shape(4, 4, ROWS, HALF)),
        in_specs=[VM, VM],
        out_specs=(VM, VM),
        scratch_shapes=[
            pltpu.VMEM((4, 4, ROWS, HALF), BF), pltpu.VMEM((4, 4, ROWS, HALF), BF),
            DMA((4,)), DMA((4,)), DMA((16,)), DMA((16,)), DMA((4,)), DMA((4,)),
        ],
        compiler_params=remote(4),
        cost_estimate=cost(30),
    )(vm(q), vm(kv))


CHUNK = 256


def load_chunk(ref, at):
    return ref[at].reshape(CHUNK, HALF)


def stack_head(ref, h):
    return jnp.concatenate([ref[i][:, h * HD : (h + 1) * HD] for i in range(4)], axis=0)


def turned(rows):
    return rows.astype(F32).T.astype(BF)


class Fetch:
    def __init__(self, turn, sources, fulls, own, sems):
        self.core, self.half = turn.core, turn.half
        y, z, xl = turn.y, turn.z, turn.xl
        self.odd = (lax.rem(y, 2), lax.rem(z, 2), xl)
        self.across = device(y, z, 1 - xl, turn.core, 1 - turn.half)
        self.beside = (
            device(y + 1 - 2 * self.odd[0], z, xl, turn.core, turn.half),
            device(y, z + 1 - 2 * self.odd[1], xl, turn.core, turn.half),
            device(y, z, 1 - xl, turn.core, turn.half),
        )
        self.sibling = turn.sibling()
        self.sources, self.fulls, self.own = sources, fulls, own
        self.sizes = (HALF, FF // 2, HALF)
        self.xs, self.xr, self.ys, self.yr, self.ds, self.dr, self.es, self.er = sems

    def rows(self, n, c, odd):
        size = self.sizes[n]
        if n == 2:
            return odd * (size // 2), size // 2
        return c * (size // 6) + odd * (size // 12), size // 12

    def piece(self, n, half, c, odd):
        start, size = self.rows(n, c, odd)
        return self.fulls[n].at[pl.ds(pl.multiple_of(half * self.sizes[n] + start, 32), size)]

    def each(self, act, flip=False):
        pl.when(self.core == (1 if flip else 0))(lambda: act(0))
        pl.when(self.core == (0 if flip else 1))(lambda: act(1))

    def keep(self):
        for n in range(3):
            rows = self.fulls[n].at[pl.ds(pl.multiple_of(self.half * self.sizes[n], 32), self.sizes[n])]
            yield pltpu.make_async_copy(self.sources[n], rows, self.own.at[n])

    def give(self, n, c, slot):
        odd = 1 - self.odd[2] if c % 3 == 2 else self.odd[c % 3]
        start, size = self.rows(n, c, odd)
        src = self.sources[n].at[pl.ds(pl.multiple_of(start, 32), size)]
        send(src, self.piece(n, self.half, c, odd), self.xs.at[slot], self.xr.at[slot], self.across)

    def own_rows(self):
        for copy in self.keep():
            copy.start()

    def issue(self, c):
        if c == 0:
            pl.when(self.core == 1)(lambda: self.give(2, 1, 6))
        if c < 6:
            self.each(lambda n: self.give(n, c, c))

    def pass_x(self, n, c, slot):
        piece = self.piece(n, 1 - self.half, c, self.odd[c % 3])
        finish(piece, piece, self.xs.at[slot], self.xr.at[slot], self.across)
        send(piece, piece, self.ys.at[slot], self.yr.at[slot], self.beside[c % 3])
        send(piece, piece, self.ds.at[slot], self.dr.at[slot], self.sibling)

    def pass_y(self, n, c, slot):
        piece = self.piece(n, 1 - self.half, c, 1 - self.odd[c % 3])
        finish(piece, piece, self.ys.at[slot], self.yr.at[slot], self.beside[c % 3])
        send(piece, piece, self.es.at[slot], self.er.at[slot], self.sibling)

    def step_x(self, c):
        self.each(lambda n: self.pass_x(n, c, c))
        if c == 0:
            pl.when(self.core == 1)(lambda: self.pass_x(2, 1, 6))

    def step_y(self, c):
        self.each(lambda n: self.pass_y(n, c, c))
        if c == 0:
            pl.when(self.core == 1)(lambda: self.pass_y(2, 1, 6))

    def between(self, n, c, odd, out_sem, in_sem):
        piece = self.piece(n, 1 - self.half, c, odd)
        return pltpu.make_async_remote_copy(
            src_ref=piece, dst_ref=piece, send_sem=out_sem, recv_sem=in_sem,
            device_id=self.sibling, device_id_type=MESH,
        )

    def end(self):
        def sent(n, c, slot):
            odd = self.odd[c % 3]
            self.between(n, c, odd, self.ds.at[slot], self.dr.at[slot]).wait_send()
            self.between(n, c, 1 - odd, self.es.at[slot], self.er.at[slot]).wait_send()

        def came(n, c, slot):
            odd = self.odd[c % 3]
            self.between(n, c, odd, self.ds.at[slot], self.dr.at[slot]).wait_recv()
            self.between(n, c, 1 - odd, self.es.at[slot], self.er.at[slot]).wait_recv()

        def act(n):
            for c in range(6):
                sent(n, c, c)
                came(1 - n, c, c)

        self.each(act)
        pl.when(self.core == 1)(lambda: sent(2, 1, 6))
        pl.when(self.core == 0)(lambda: came(2, 1, 6))
        for copy in self.keep():
            copy.wait()


def front_kernel(
    x_ref, wq, wk, wv, v0, v1, v2, v3, v4, v5, v6, v7, v8, wi, wu, wo,
    a_ref, qo_ref, kvo_ref, ot_ref, lse_ref, w_ref, w_i, w_u, w_o, vec_ref, bi_ref,
    q_ref, kv_ref, small, small_o, o_ref, qt, top, total,
    own_sem, a_out, a_in, b_out, b_in, qs, qr, ks, kr, fs, fr, os, om, own, *sems,
):
    turn = Turn()
    y, z, xl, core, half = turn.y, turn.z, turn.xl, turn.core, turn.half
    fetch = Fetch(turn, (wi, wu, wo), (w_i, w_u, w_o), own, sems)
    across, sibling = fetch.across, fetch.sibling
    barrier = pltpu.get_barrier_semaphore()
    greet(barrier, across)
    greet(barrier, sibling)
    greet(barrier, fetch.beside[2])

    def hello(k, carry):
        greet(barrier, turn.partner(k))
        return carry

    lax.fori_loop(1, 16, hello, 0)

    @pl.when(jnp.logical_not(turn.stays))
    def _():
        greet(barrier, turn.partner(0))
        greet(barrier, fetch.beside[0])
        greet(barrier, fetch.beside[1])

    start = pl.multiple_of(core * GROUP, GROUP)
    rows = pl.multiple_of(half * HALF, HALF)
    give = pl.ds(pl.multiple_of(half * HALF + core * GROUP, GROUP), GROUP)
    take = pl.ds(pl.multiple_of((1 - half) * HALF + core * GROUP, GROUP), GROUP)
    last = pl.ds(pl.multiple_of((1 - half) * HALF + (1 - core) * GROUP, GROUP), GROUP)
    mine = [
        pltpu.make_async_copy(w, w_ref.at[i, pl.ds(rows, HALF)], own_sem.at[i]) for i, w in enumerate((wq, wk, wv))
    ]
    for copy in mine:
        copy.start()
    fetch.own_rows()
    small[...] = jnp.zeros_like(small)
    for i, v in enumerate((v0, v1, v2, v3, v4, v5, v6, v7)):
        small[i : i + 1, :] = v[...].astype(F32).reshape(1, HALF)
    for i in range(4):
        small[8 + i : 9 + i, :] = v8[i * HALF : (i + 1) * HALF].astype(F32).reshape(1, HALF)
    pl.semaphore_wait(barrier, 18 + 3 * lax.rem(xl + core, 2))
    send(small, small_o, a_out.at[3], a_in.at[3], across)
    for i, w in enumerate((wk, wv, wq)):
        i = (1, 2, 0)[i]
        send(w.at[pl.ds(start, GROUP)], w_ref.at[i, give], a_out.at[i], a_in.at[i], across)
    finish(small_o, small_o, a_out.at[3], a_in.at[3], across)
    near, far = small[...], small_o[...]
    ahead = jnp.where(half == 0, near, far)
    behind = jnp.where(half == 0, far, near)
    vec_ref[:, :HALF] = ahead[:8]
    vec_ref[:, HALF:] = behind[:8]
    for i in range(4):
        bi_ref[:, i * HALF : (i + 1) * HALF] = ahead[8 + i : 9 + i]
        bi_ref[:, 1536 + i * HALF : 1536 + (i + 1) * HALF] = behind[8 + i : 9 + i]
    x = x_ref[...]
    for i in (1, 2, 0):
        piece = w_ref.at[i, take]
        finish(piece, piece, a_out.at[i], a_in.at[i], across)
        send(piece, piece, b_out.at[i], b_in.at[i], sibling)
    for c in range(6):
        fetch.issue(c)
    done = {}
    for i in (1, 2, 0):
        piece = w_ref.at[i, last]
        finish(piece, piece, b_out.at[i], b_in.at[i], sibling)
        mine[i].wait()
        done[i] = nn(x, w_ref[i])
        if i == 2:
            keys = done[1].astype(BF)
            values = (done[2] + vec_ref[1:2, :]).astype(BF)
            for g in range(4):
                cut = slice(g * GROUP, (g + 1) * GROUP)
                kv_ref[g] = jnp.concatenate([keys[:, cut], values[:, cut]], axis=1)
            turn.start(16, lambda k: kv_ref.at[turn.ahead(k)[1]], kvo_ref.at[y, z, xl], ks, kr)
    pad = jnp.zeros((ROWS, 64), BF)
    query = (done[0] + vec_ref[0:1, :]).astype(BF) * BF(0.125)
    for g in range(4):
        q_ref[g] = jnp.concatenate([query[:, g * GROUP : (g + 1) * GROUP], pad], axis=1)
    turn.start(4, lambda k: q_ref.at[turn.ahead(k)[1]], qo_ref.at[z], qs, qr)

    def onward(k):
        i, j = turn.behind(k)
        piece = kvo_ref.at[i, j, core]
        send(piece, piece, fs.at[k], fr.at[k], turn.sibling())

    turn.end_first(qo_ref.at[z], qs, qr)

    def done_q(k, carry):
        turn.end(k, qo_ref.at[turn.behind(k)[1]], qs, qr)
        return carry

    lax.fori_loop(1, 4, done_q, 0)
    turn.end_first(kvo_ref.at[y, z, core], ks, kr)
    onward(0)
    for h in range(3):
        qt[h] = turned(stack_head(qo_ref, h))
    top[...] = jnp.full_like(top, -jnp.inf)
    total[...] = jnp.zeros_like(total)
    ot_ref[...] = jnp.zeros_like(ot_ref)

    def work(k):
        i, j = turn.behind(k)
        piece = kvo_ref.at[i, j, 1 - core]
        finish(piece, piece, fs.at[k], fr.at[k], turn.sibling())
        kv = load_chunk(kvo_ref, (i, j))
        for h in range(3):
            scores = nn(kv[:, h * HD : (h + 1) * HD], qt[h])
            old = top[h]
            new = jnp.maximum(old, jnp.max(scores, axis=0, keepdims=True))
            shrink = jnp.exp(old - new)
            weights = jnp.exp(scores - new)
            total[h] = total[h] * shrink + jnp.sum(weights, axis=0, keepdims=True)
            mixed = tn(kv[:, GROUP + h * HD : GROUP + (h + 1) * HD], weights.astype(BF))
            ot_ref[h] = ot_ref[h] * shrink + mixed
            top[h] = new

    def relay(k, carry):
        i, j = turn.behind(k)
        turn.end(k, kvo_ref.at[i, j, core], ks, kr)
        onward(k)
        work(k - 1)

        for c in range(6):
            pl.when(k == c + 10)(functools.partial(fetch.step_x, c))
        return carry

    lax.fori_loop(1, 16, relay, 0)
    work(15)
    heads = []
    for h in range(3):
        lse_ref[h] = top[h] + jnp.log(total[h])
        normal = ot_ref[h] / total[h]
        ot_ref[h] = normal
        heads.append(normal.T.astype(BF))
    heads.append(jnp.zeros((512, 64), BF))
    out = jnp.concatenate(heads, axis=1)
    for i in range(4):
        o_ref[i] = out[i * ROWS : (i + 1) * ROWS]
    turn.start(4, lambda k: o_ref.at[turn.ahead(k)[1]], a_ref.at[z], os, om)
    for c in range(6):
        fetch.step_y(c)
    turn.end_first(a_ref.at[z], os, om)

    def done_o(k, carry):
        turn.end(k, a_ref.at[turn.behind(k)[1]], os, om)
        return carry

    lax.fori_loop(1, 4, done_o, 0)
    fetch.end()


def front(*arrays):
    return pl.pallas_call(
        front_kernel,
        name="front",
        cost_estimate=cost(70),
        out_shape=(
            shape(4, ROWS, 256), shape(4, ROWS, 256), shape(4, 4, 2, ROWS, HALF),
            shape(3, HD, 512, dtype=F32), shape(3, 1, 512, dtype=F32),
            shape(3, D, D), shape(D, FF), shape(FF, D), shape(D, D), shape(8, D, dtype=F32), shape(1, FF, dtype=F32),
        ),
        in_specs=[VM, ANY, ANY, ANY] + [VM] * 9 + [ANY] * 3,
        out_specs=(VM,) * 11,
        scratch_shapes=[
            pltpu.VMEM((4, ROWS, 256), BF), pltpu.VMEM((4, ROWS, HALF), BF),
            pltpu.VMEM((16, HALF), F32), pltpu.VMEM((16, HALF), F32),
            pltpu.VMEM((4, ROWS, 256), BF),
            pltpu.VMEM((3, HD, 512), BF), pltpu.VMEM((3, 1, 512), F32), pltpu.VMEM((3, 1, 512), F32),
            DMA((3,)), DMA((4,)), DMA((4,)), DMA((3,)), DMA((3,)),
            DMA((4,)), DMA((4,)), DMA((16,)), DMA((16,)), DMA((16,)), DMA((16,)), DMA((4,)), DMA((4,)), DMA((3,)),
        ] + [DMA((7,))] * 8,
        compiler_params=remote(1),
    )(arrays[0], *map(hbm, arrays[1:4]), *arrays[4:13], *map(hbm, arrays[13:]))


def attend_back_kernel(q_ref, kv_ref, da_ref, ot_ref, lse_ref, dq_ref, dkv_ref, qs, qt, ds, dt, delta, acc):
    for h in range(3):
        rows = stack_head(q_ref, h)
        qs[h] = rows
        qt[h] = turned(rows)
        rows = stack_head(da_ref, h)
        ds[h] = rows
        flipped = rows.astype(F32).T
        dt[h] = flipped.astype(BF)
        delta[h] = jnp.sum(flipped * ot_ref[h], axis=0, keepdims=True)
    acc[...] = jnp.zeros_like(acc)

    def body(i, carry):
        kv = load_chunk(kv_ref, pair(i))
        keys, values = [], []
        for h in range(3):
            k = kv[:, h * HD : (h + 1) * HD]
            v = kv[:, GROUP + h * HD : GROUP + (h + 1) * HD]
            probs = jnp.exp(nn(k, qt[h]) - lse_ref[h])
            slopes = (probs * (nn(v, dt[h]) - delta[h])).astype(BF)
            keys.append(nn(slopes, qs[h]).astype(BF))
            values.append(nn(probs.astype(BF), ds[h]).astype(BF))
            acc[h] += tn(k, slopes)
        y, z = pair(i)
        dkv_ref[y, z] = jnp.concatenate(keys + values, axis=1).reshape(2, ROWS, HALF)
        return carry

    lax.fori_loop(0, 4096 // CHUNK, body, 0)
    heads = [(acc[h] * 0.125).T.astype(BF) for h in range(3)]
    heads.append(jnp.zeros((512, 64), BF))
    out = jnp.concatenate(heads, axis=1)
    for i in range(4):
        dq_ref[i] = out[i * ROWS : (i + 1) * ROWS]


def attend_back(q, kv, da, ot, lse):
    return pl.pallas_call(
        attend_back_kernel,
        name="attend_back",
        cost_estimate=cost(25),
        out_shape=(shape(4, ROWS, 256), shape(4, 4, 2, ROWS, HALF)),
        in_specs=[VM] * 5,
        out_specs=(VM, VM),
        scratch_shapes=[
            pltpu.VMEM((3, 512, HD), BF), pltpu.VMEM((3, HD, 512), BF),
            pltpu.VMEM((3, 512, HD), BF), pltpu.VMEM((3, HD, 512), BF),
            pltpu.VMEM((3, 1, 512), F32), pltpu.VMEM((3, HD, 512), F32),
        ],
        compiler_params=plain(),
    )(*map(vm, (q, kv, da, ot, lse)))


def norm(hidden):
    centred = hidden - jnp.mean(hidden, axis=-1, keepdims=True)
    inverse = lax.rsqrt(jnp.mean(centred * centred, axis=-1, keepdims=True) + EPS)
    return centred * inverse, inverse


def norm_back(scaled, normal, inverse):
    centre = jnp.mean(scaled, axis=-1, keepdims=True)
    along = jnp.mean(scaled * normal, axis=-1, keepdims=True)
    return inverse * (scaled - centre - normal * along)


def column(value):
    return jnp.sum(value, axis=0, keepdims=True)


def block_kernel(
    x_ref, ct_ref, a_ref, w_i, w_u, w_o, vec_ref, bi_ref,
    out_ref, dh1_ref, da_ref, af_ref, yb_ref, g_ref, df_ref, du_ref, dz_ref, vg_ref,
    slope, da_out, outs, ins,
):
    turn = Turn()
    turn.hello(4)
    b_output, first_gain, first_shift = vec_ref[2:3, :], vec_ref[3:4, :], vec_ref[4:5, :]
    b_outer, second_gain, second_shift = vec_ref[5:6, :], vec_ref[6:7, :], vec_ref[7:8, :]
    mixed = jnp.concatenate([a_ref[g][:, :GROUP] for g in range(4)], axis=1)
    af_ref[...] = mixed
    hidden = x_ref[...].astype(F32) + nn(mixed, w_o[...]) + b_output
    normal1, inverse1 = norm(hidden)
    normed = normal1 * first_gain + first_shift
    low = normed.astype(BF)
    yb_ref[...] = low
    second_in = normed + b_outer
    for j in range(4):
        cut = slice(j * D, (j + 1) * D)
        inner = nn(low, w_i[:, cut]) + bi_ref[:, cut]
        cdf = 0.5 * (1.0 + lax.erf(inner * (0.5**0.5)))
        active = (inner * cdf).astype(BF)
        slope[:, cut] = cdf + inner * jnp.exp(inner * inner * -0.5) * 0.3989422804014327
        g_ref[:, cut] = active
        second_in = second_in + nn(active, w_u[cut, :])
    normal2, inverse2 = norm(second_in)
    out_ref[...] = (normal2 * second_gain + second_shift).astype(BF)
    upper = ct_ref[...].astype(F32)


    def note(row, value):
        for h in range(2):
            vg_ref[h, row : row + 1, :] = value[:, h * HALF : (h + 1) * HALF]

    vg_ref[...] = jnp.zeros_like(vg_ref)
    note(6, column(upper * normal2))
    note(7, column(upper))
    dh2 = norm_back(upper * second_gain, normal2, inverse2)
    df = dh2.astype(BF)
    df_ref[...] = df
    note(5, column(df.astype(F32)))
    dy1 = dh2
    for j in range(4):
        cut = slice(j * D, (j + 1) * D)
        du = (slope[:, cut] * nt(df, w_u[cut, :])).astype(BF)
        du_ref[:, cut] = du
        sums = column(du.astype(F32))
        for i in range(2):
            n = 2 * j + i
            vg_ref[n // 4, 8 + n % 4 : 9 + n % 4, :] = sums[:, i * HALF : (i + 1) * HALF]
        dy1 = dy1 + nt(du, w_i[:, cut])
    note(3, column(dy1 * normal1))
    note(4, column(dy1))
    dh1 = norm_back(dy1 * first_gain, normal1, inverse1)
    dh1_ref[...] = dh1
    dz = dh1.astype(BF)
    dz_ref[...] = dz
    note(2, column(dz.astype(F32)))
    da = nt(dz, w_o[...]).astype(BF)
    pad = jnp.zeros((ROWS, 64), BF)
    for g in range(4):
        da_out[g] = jnp.concatenate([da[:, g * GROUP : (g + 1) * GROUP], pad], axis=1)
    turn.ready(4)
    turn.start(4, lambda k: da_out.at[turn.ahead(k)[1]], da_ref.at[turn.z], outs, ins)
    turn.end_first(da_ref.at[turn.z], outs, ins)

    def done(k, carry):
        turn.end(k, da_ref.at[turn.behind(k)[1]], outs, ins)
        return carry

    lax.fori_loop(1, 4, done, 0)


def block(*arrays):
    return pl.pallas_call(
        block_kernel,
        name="block",
        cost_estimate=cost(12),
        out_shape=(
            plain_shape(ROWS, D), shape(ROWS, D, dtype=F32), shape(4, ROWS, 256), shape(ROWS, D), shape(ROWS, D),
            shape(ROWS, FF), shape(ROWS, D), shape(ROWS, FF), shape(ROWS, D),
            shape(2, 16, HALF, dtype=F32),
        ),
        in_specs=[VM] * 8,
        out_specs=(VM,) * 10,
        scratch_shapes=[
            pltpu.VMEM((ROWS, FF), F32), pltpu.VMEM((4, ROWS, 256), BF), DMA((4,)), DMA((4,)),
        ],
        compiler_params=remote(2),
    )(arrays[0], arrays[1], *map(vm, arrays[2:]))


def put(ref, at, value):
    ref[at] = value.astype(BF).reshape(4, 2, 48, HALF)


def wide_kernel(yb, yb_o, g, g_o, a, a_o, df, df_o, du, du_o, dz, dz_o, one_ref, two_ref, zero_ref):
    core = lax.axis_index("seq")

    def right(ref, other, start):
        cols = pl.ds(pl.multiple_of(start + core * HALF, HALF), HALF)
        return jnp.concatenate([ref[:, cols], other[:, cols]], axis=0)

    def left(ref, other, start):
        return jnp.concatenate([ref[:, start : start + HALF], other[:, start : start + HALF]], axis=0)

    outer = right(df, df_o, 0)
    attn = right(dz, dz_o, 0)
    for half in range(2):
        for m in range(4):
            put(one_ref, (half, m), tn(left(g, g_o, half * 1536 + m * HALF), outer))
        rows = left(yb, yb_o, half * HALF)
        for m in range(4):
            put(two_ref, (half, m), tn(rows, right(du, du_o, m * D)))
        put(zero_ref, half, tn(left(a, a_o, half * HALF), attn))


def wide(*arrays):
    return pl.pallas_call(
        wide_kernel,
        name="wide",
        cost_estimate=cost(6),
        out_shape=(shape(2, 4, 4, 2, 48, HALF), shape(2, 4, 4, 2, 48, HALF), shape(2, 4, 2, 48, HALF)),
        in_specs=[VM] * 12,
        out_specs=(VM, VM, VM),
        compiler_params=plain(),
    )(*arrays)


def tail_kernel(dq_ref, dkv_ref, dh1_ref, w_ref, vg_ref, grad_ref, low_ref, vo_ref):
    low_ref[0] = jnp.concatenate([dq_ref[g][:, :GROUP] for g in range(4)], axis=1)
    sums = []
    for g in range(4):
        total = dkv_ref[0, g].astype(F32)
        for k in range(1, 4):
            total = total + dkv_ref[k, g].astype(F32)
        sums.append(total.astype(BF))
    low_ref[1] = jnp.concatenate([s[:, :GROUP] for s in sums], axis=1)
    low_ref[2] = jnp.concatenate([s[:, GROUP:] for s in sums], axis=1)
    grad = dh1_ref[...]
    for i in range(3):
        grad = grad + nt(low_ref[i], w_ref[i])
    grad_ref[...] = grad
    vo_ref[...] = vg_ref[...]
    for row, i in ((0, 0), (1, 2)):
        value = column(low_ref[i].astype(F32))
        for h in range(2):
            vo_ref[h, row : row + 1, :] = value[:, h * HALF : (h + 1) * HALF]


def tail(*arrays):
    return pl.pallas_call(
        tail_kernel,
        name="tail",
        out_shape=(plain_shape(ROWS, D, dtype=F32), shape(3, ROWS, D), shape(2, 16, HALF, dtype=F32)),
        in_specs=[VM] * 5,
        out_specs=(VM,) * 3,
        compiler_params=plain(),
        cost_estimate=cost(6),
    )(*map(vm, arrays))


def narrow_kernel(x, x_o, low, low_o, attn_ref, zero_ref):
    core = lax.axis_index("seq")
    cols = pl.ds(pl.multiple_of(core * HALF, HALF), HALF)
    for half in range(2):
        cut = slice(half * HALF, (half + 1) * HALF)
        rows = jnp.concatenate([x[:, cut], x_o[:, cut]], axis=0)
        for m in range(3):
            put(zero_ref, (half, m), tn(rows, jnp.concatenate([low[m, :, cols], low_o[m, :, cols]], axis=0)))
        zero_ref[half, 3] = attn_ref[half]


def narrow(*arrays):
    return pl.pallas_call(
        narrow_kernel,
        name="narrow",
        cost_estimate=cost(4),
        out_shape=shape(2, 4, 4, 2, 48, HALF),
        in_specs=[VM] * 5,
        out_specs=VM,
        compiler_params=plain(),
    )(*arrays)


def reduce_kernel(
    g0, g1, g2, vg, out, vo, r0, r1, r2, s0, s1, s2, t0, t1, t2, rv, sv, tv, uv,
    a_out, a_in, b_out, b_in, c_out, c_in, d_out, d_in, e_out, e_in,
):
    y, z, xl, core, half = place()
    x = half * 2 + xl
    barrier = pltpu.get_barrier_semaphore()

    def along_x(k):
        e = wrap(x + k, 4)
        return device(y, z, lax.rem(e, 2), core, lax.div(e, 2))

    def at_yz(k):
        i, j = pair(k)
        return device(wrap(y + i, 4), wrap(z + j, 4), xl, core, half)

    def at_xz(k):
        i, j = pair(k)
        e = wrap(x + i, 4)
        return device(y, wrap(z + j, 4), lax.rem(e, 2), core, lax.div(e, 2))

    def at_xy(k):
        i, j = pair(k)
        e = wrap(x + i, 4)
        return device(wrap(y + j, 4), z, lax.rem(e, 2), core, lax.div(e, 2))

    def hello_yz(k, carry):
        greet(barrier, at_yz(k))
        return carry

    def hello_x(k, carry):
        i = lax.div(k - 1, 3) + 1
        j = lax.rem(k - 1, 3) + 1
        greet(barrier, at_xz(i * 4 + j))
        greet(barrier, at_xy(i * 4 + j))
        return carry

    def hello_row(k, carry):
        greet(barrier, along_x(k))
        return carry

    lax.fori_loop(1, 16, hello_yz, 0)
    lax.fori_loop(1, 10, hello_x, 0)
    lax.fori_loop(1, 4, hello_row, 0)
    greet(barrier, device(y, z, xl, 1 - core, half))
    pl.semaphore_wait(barrier, 37)

    def first(k, carry):
        e = wrap(x + k, 4)
        send(g0.at[lax.div(e, 2), :, :, lax.rem(e, 2)], r0.at[k - 1], a_out.at[0, k], a_in.at[0, k], along_x(k))
        send(g1.at[:, wrap(y + k, 4)], r1.at[k - 1], a_out.at[1, k], a_in.at[1, k], at_yz(k * 4))
        send(g2.at[:, :, wrap(z + k, 4)], r2.at[k - 1], a_out.at[2, k], a_in.at[2, k], at_yz(k))
        send(vg.at[lax.div(e, 2)], rv.at[k - 1], a_out.at[3, k], a_in.at[3, k], along_x(k))
        return carry

    lax.fori_loop(1, 4, first, 0)
    here = device(y, z, xl, core, half)

    def sum1(own, got, to, sem):
        for k in range(1, 4):
            finish(got.at[k - 1], got.at[k - 1], a_out.at[sem, k], a_in.at[sem, k], here)

        def add(i, carry):
            p, q, o = own(i)
            total = o.astype(F32)
            for k in range(3):
                total = total + got[(k,) + p].astype(F32)
            to[q] = total.astype(BF)
            return carry

        lax.fori_loop(0, 16, add, 0)

    def own0(i):
        p, q = pair(i)
        return (p, q), (p, q), g0[half, p, q, xl]

    def own1(i):
        f, q, r = lax.div(i, 8), lax.rem(lax.div(i, 2), 4), lax.rem(i, 2)
        return (f, q, r), (f, q, r), g1[f, y, q, r]

    def own2(i):
        f, q, r = lax.div(i, 8), lax.rem(lax.div(i, 2), 4), lax.rem(i, 2)
        return (f, q, r), (f, q, r), g2[f, q, z, r]

    for k in range(1, 4):
        finish(rv.at[k - 1], rv.at[k - 1], a_out.at[3, k], a_in.at[3, k], here)
    part = vg[half] + rv[0] + rv[1] + rv[2]
    sv[...] = part.astype(BF)

    def second3(k, carry):
        send(sv, tv.at[k], b_out.at[3, k], b_in.at[3, k], at_yz(k))
        return carry

    lax.fori_loop(1, 16, second3, 0)
    sum1(own1, r1, s1, 1)

    def second1(k, carry):
        i, j = pair(k)
        e = wrap(x + i, 4)
        send(s1.at[lax.div(e, 2), wrap(z + j, 4), lax.rem(e, 2)], t1.at[k], b_out.at[1, k], b_in.at[1, k], at_xz(k))
        return carry

    lax.fori_loop(1, 16, second1, 0)
    sum1(own2, r2, s2, 2)

    def second2(k, carry):
        i, j = pair(k)
        e = wrap(x + i, 4)
        send(s2.at[lax.div(e, 2), wrap(y + j, 4), lax.rem(e, 2)], t2.at[k], b_out.at[2, k], b_in.at[2, k], at_xy(k))
        return carry

    lax.fori_loop(1, 16, second2, 0)
    sum1(own0, r0, s0, 0)

    def second0(k, carry):
        i, j = pair(k)
        send(s0.at[wrap(y + i, 4), wrap(z + j, 4)], t0.at[k], b_out.at[0, k], b_in.at[0, k], at_yz(k))
        return carry

    lax.fori_loop(1, 16, second0, 0)

    def sum2(own, got, slab):
        def done(k, carry):
            finish(got.at[k], got.at[k], b_out.at[slab, k], b_in.at[slab, k], here)
            return carry

        lax.fori_loop(1, 16, done, 0)

        def add(k, total):
            return total + got[k].astype(F32)

        total = lax.fori_loop(1, 16, add, own.astype(F32))
        out[core, slab, y, z, xl] = total.astype(BF)

    def done3(k, total):
        finish(tv.at[k], tv.at[k], b_out.at[3, k], b_in.at[3, k], here)
        return total + tv[k].astype(F32)

    vo[...] = lax.fori_loop(1, 16, done3, part)
    sibling = device(y, z, xl, 1 - core, half)
    send(vo, uv, e_out.at[3], e_in.at[3], sibling)

    sum2(s1[half, z, xl], t1, 1)

    def third1(k, carry):
        i, j = lax.rem(k, 2), lax.div(k, 2)
        mine = out.at[core, 1, y, z, xl]
        send(mine, mine, c_out.at[1, k], c_in.at[1, k], device(y, wrap(z + j, 4), wrap(xl + i, 2), core, half))
        return carry

    lax.fori_loop(1, 8, third1, 0)
    sum2(s2[half, y, xl], t2, 2)

    def third2(k, carry):
        i, j = lax.rem(k, 2), lax.div(k, 2)
        mine = out.at[core, 2, y, z, xl]
        send(mine, mine, c_out.at[2, k], c_in.at[2, k], device(wrap(y + j, 4), z, wrap(xl + i, 2), core, half))
        return carry

    lax.fori_loop(1, 8, third2, 0)
    sum2(s0[y, z], t0, 0)

    def third0(k, carry):
        mine = out.at[core, 0, y, z, xl]
        send(mine, mine, c_out.at[0, k], c_in.at[0, k], at_yz(k))
        return carry

    lax.fori_loop(1, 16, third0, 0)

    def got1(k, carry):
        i, j = lax.rem(k, 2), lax.div(k, 2)
        piece = out.at[core, 1, y, wrap(z - j, 4), wrap(xl - i, 2)]
        finish(piece, piece, c_out.at[1, k], c_in.at[1, k], here)
        return carry

    lax.fori_loop(1, 8, got1, 0)

    def fourth1(k, carry):
        mine = out.at[core, 1, y]
        send(mine, mine, d_out.at[1, k], d_in.at[1, k], at_yz(k * 4))
        return carry

    lax.fori_loop(1, 4, fourth1, 0)

    def got2(k, carry):
        i, j = lax.rem(k, 2), lax.div(k, 2)
        piece = out.at[core, 2, wrap(y - j, 4), z, wrap(xl - i, 2)]
        finish(piece, piece, c_out.at[2, k], c_in.at[2, k], here)
        return carry

    lax.fori_loop(1, 8, got2, 0)

    def fourth2(k, carry):
        mine = out.at[core, 2, :, z]
        send(mine, mine, d_out.at[2, k], d_in.at[2, k], at_yz(k))
        return carry

    lax.fori_loop(1, 4, fourth2, 0)

    def got0(k, carry):
        i, j = pair(k)
        piece = out.at[core, 0, wrap(y - i, 4), wrap(z - j, 4), xl]
        finish(piece, piece, c_out.at[0, k], c_in.at[0, k], here)
        return carry

    lax.fori_loop(1, 16, got0, 0)
    mine0 = out.at[core, 0, :, :, xl]
    send(mine0, mine0, d_out.at[0, 1], d_in.at[0, 1], device(y, z, 1 - xl, core, half))

    def last1(k, carry):
        piece = out.at[core, 1, wrap(y - k, 4)]
        finish(piece, piece, d_out.at[1, k], d_in.at[1, k], here)
        return carry

    def last2(k, carry):
        piece = out.at[core, 2, :, wrap(z - k, 4)]
        finish(piece, piece, d_out.at[2, k], d_in.at[2, k], here)
        return carry

    lax.fori_loop(1, 4, last1, 0)
    send(out.at[core, 1], out.at[core, 1], e_out.at[1], e_in.at[1], sibling)
    lax.fori_loop(1, 4, last2, 0)
    send(out.at[core, 2], out.at[core, 2], e_out.at[2], e_in.at[2], sibling)
    piece0 = out.at[core, 0, :, :, 1 - xl]
    finish(piece0, piece0, d_out.at[0, 1], d_in.at[0, 1], here)
    send(out.at[core, 0], out.at[core, 0], e_out.at[0], e_in.at[0], sibling)
    for slab in (1, 2, 0):
        piece = out.at[1 - core, slab]
        finish(piece, piece, e_out.at[slab], e_in.at[slab], here)
    finish(uv, uv, e_out.at[3], e_in.at[3], here)
    vo[...] = vo[...] + uv[...]


def reduce(g0, g1, g2, vg):
    dma = pltpu.SemaphoreType.DMA
    blk = (48, HALF)
    return pl.pallas_call(
        reduce_kernel,
        name="reduce",
        out_shape=(shape(2, 3, 4, 4, 2, *blk), shape(16, HALF, dtype=F32)),
        in_specs=[VM] * 4,
        out_specs=(VM, VM),
        scratch_shapes=[
            pltpu.VMEM((3, 4, 4, *blk), BF), pltpu.VMEM((3, 2, 4, 2, *blk), BF), pltpu.VMEM((3, 2, 4, 2, *blk), BF),
            pltpu.VMEM((4, 4, *blk), BF), pltpu.VMEM((2, 4, 2, *blk), BF), pltpu.VMEM((2, 4, 2, *blk), BF),
            pltpu.VMEM((16, *blk), BF), pltpu.VMEM((16, *blk), BF), pltpu.VMEM((16, *blk), BF),
            pltpu.VMEM((3, 16, HALF), F32), pltpu.VMEM((16, HALF), BF), pltpu.VMEM((16, 16, HALF), BF),
            pltpu.VMEM((16, HALF), F32),
            dma((4, 4)), dma((4, 4)), dma((4, 16)), dma((4, 16)), dma((3, 16)), dma((3, 16)),
            dma((3, 4)), dma((3, 4)), dma((4,)), dma((4,)),
        ],
        compiler_params=pltpu.CompilerParams(
            collective_id=5, has_side_effects=True, vmem_limit_bytes=LIMIT
        ),
        cost_estimate=cost(80),
    )(*map(vm, (g0, g1, g2, vg)))


def spell_kernel(zero, one, two, q_ref, k_ref, v_ref, o_ref, i_ref, u_ref):
    for c in range(2):
        cols = slice(c * HALF, (c + 1) * HALF)
        for m, ref in enumerate((q_ref, k_ref, v_ref, o_ref)):
            ref[:, cols] = zero[c, 0, m, 0].astype(F32)
            i_ref[:, m * D + c * HALF : m * D + (c + 1) * HALF] = two[c, 0, m, 0].astype(F32)
            u_ref[m * 48 : (m + 1) * 48, cols] = one[c, 0, 0, m].astype(F32)


def spell(summed):
    summed = summed.reshape(2, 3, 4, 8, 48, HALF)
    part = pl.BlockSpec((48, D), lambda i: (i, 0))
    return pl.pallas_call(
        spell_kernel,
        name="spell",
        grid=(8,),
        out_shape=tuple(
            plain_shape(*dims, dtype=F32) for dims in ((HALF, D), (HALF, D), (HALF, D), (HALF, D), (HALF, FF), (1536, D))
        ),
        in_specs=[
            pl.BlockSpec((2, 1, 4, 1, 48, HALF), lambda i: (0, 0, 0, i, 0, 0)),
            pl.BlockSpec((2, 1, 1, 4, 48, HALF), lambda i: (0, 1, i // 2, i % 2, 0, 0)),
            pl.BlockSpec((2, 1, 4, 1, 48, HALF), lambda i: (0, 2, 0, i, 0, 0)),
        ],
        out_specs=(part, part, part, part, pl.BlockSpec((48, FF), lambda i: (i, 0)), pl.BlockSpec((192, D), lambda i: (i, 0))),
        compiler_params=plain(),
        cost_estimate=cost(6),
    )(summed, summed, summed)


def swap_cores(array):
    return lax.ppermute(array, "seq", [(0, 1), (1, 0)])


def local(
    tokens, cotangent, w_query, w_key, w_value, w_output, b_query, b_value, b_output,
    first_gain, first_shift, w_inner, b_inner, w_outer, b_outer, second_gain, second_shift,
):
    x = tokens[0]
    mixed, q_all, kv_all, mixed_t, lse, w_qkv, w_i, w_u, w_o, vec, bi = front(
        x, w_query, w_key, w_value, b_query, b_value, b_output, first_gain, first_shift, b_outer, second_gain,
        second_shift, b_inner, w_inner, w_outer, w_output,
    )
    layer_out, dh1, da_all, a_full, yb, g, df, du, dz, vg = block(x, cotangent[0], mixed, w_i, w_u, w_o, vec, bi)
    acts = (yb, g, a_full, df, du, dz)
    acts_o = [swap_cores(v) for v in acts]
    x_o = swap_cores(x)
    g1, g2, g0o = wide(*[v for pair in zip(acts, acts_o) for v in pair])
    dq, dkv = attend_back(q_all, kv_all, da_all, mixed_t, lse)
    dq, dkv = collect(dq, dkv)
    tokens_grad, low, vg = tail(dq, dkv, dh1, w_qkv, vg)
    low_o = swap_cores(low)
    g0 = narrow(x, x_o, low, low_o, g0o)
    summed, vecs = reduce(g0, g1, g2, vg)
    gq, gk, gv, go, gi, gu = spell(summed)
    return (
        layer_out[None], tokens_grad[None], gq, gk, gv, go,
        vecs[0], vecs[1], vecs[2], vecs[3], vecs[4], gi, vecs[8:12].reshape(1536), gu, vecs[5], vecs[6], vecs[7],
    )


def solution(mesh):
    rows = P(("seq", "fsdp"), "ctx", None)
    mat = P("fsdp", None)
    vec = P("fsdp")
    return jax.shard_map(
        local,
        mesh=mesh,
        in_specs=(rows, rows, mat, mat, mat, mat, vec, vec, vec, vec, vec, mat, vec, mat, vec, vec, vec),
        out_specs=(rows, rows, mat, mat, mat, mat, vec, vec, vec, vec, vec, mat, vec, mat, vec, vec, vec),
        check_vma=False,
    )
```

```python
import functools

import jax
import jax.numpy as jnp
from jax import lax
from jax.experimental import pallas as pl
from jax.experimental.pallas import tpu as pltpu
from jax.sharding import PartitionSpec as P

AXES = ("ctx", "seq", "fsdp")
MESH = pl.DeviceIdType.MESH
BF = jnp.bfloat16
F32 = jnp.float32
D = 768
FF = 3072
HALF = 384
GROUP = 192
HD = 64
ROWS = 128
EPS = 1e-12
LIMIT = 12 << 20
VM = pl.BlockSpec(memory_space=pltpu.VMEM)
ANY = pl.BlockSpec(memory_space=pltpu.HBM)


def plain_shape(*dims, dtype=BF):
    return jax.ShapeDtypeStruct(dims, dtype)


def shape(*dims, dtype=BF):
    return pltpu.VMEM(dims, dtype)


def hbm(array):
    return pltpu.with_memory_space_constraint(array, pltpu.HBM)


def vm(array):
    return pltpu.with_memory_space_constraint(array, pltpu.VMEM)


def nn(left, right):
    return jnp.dot(left, right, preferred_element_type=F32)


def nt(left, right):
    return lax.dot_general(left, right, (((1,), (1,)), ((), ())), preferred_element_type=F32)


def tn(left, right):
    return lax.dot_general(left, right, (((0,), (0,)), ((), ())), preferred_element_type=F32)


def wrap(value, size):
    return lax.rem(value + size, size)


def place():
    ctx = lax.axis_index("ctx")
    y = lax.div(ctx, 8)
    z = lax.rem(lax.div(ctx, 2), 4)
    return y, z, lax.rem(ctx, 2), lax.axis_index("seq"), lax.axis_index("fsdp")


def device(y, z, xl, core, half):
    return ((y * 4 + z) * 2 + xl, core, half)


def send(src, dst, out_sem, in_sem, where):
    pltpu.make_async_remote_copy(
        src_ref=src, dst_ref=dst, send_sem=out_sem, recv_sem=in_sem,
        device_id=where, device_id_type=MESH,
    ).start()


def finish(src, dst, out_sem, in_sem, where):
    copy = pltpu.make_async_remote_copy(
        src_ref=src, dst_ref=dst, send_sem=out_sem, recv_sem=in_sem,
        device_id=where, device_id_type=MESH,
    )
    copy.wait_send()
    copy.wait_recv()


def arrived(got, in_sem, where):
    pltpu.make_async_remote_copy(
        src_ref=got, dst_ref=got, send_sem=in_sem, recv_sem=in_sem, device_id=where, device_id_type=MESH
    ).wait_recv()


def left_here(src, out_sem, where):
    pltpu.make_async_remote_copy(
        src_ref=src, dst_ref=src, send_sem=out_sem, recv_sem=out_sem, device_id=where, device_id_type=MESH
    ).wait_send()


def greet(barrier, where):
    pl.semaphore_signal(barrier, inc=1, device_id=where, device_id_type=MESH)


def pair(k):
    return lax.div(k, 4), lax.rem(k, 4)


class Turn:
    def __init__(self):
        self.y, self.z, self.xl, self.core, self.half = place()
        self.stays = self.xl == self.core

    def step(self, k, count):
        if count == 4:
            return 0, k
        return lax.rem(k + lax.div(k, 4), 4), lax.rem(k, 4)

    def partner(self, k, count):
        i, j = self.ahead(k, count)
        return device(i, j, self.core, self.xl, self.half)

    def ahead(self, k, count):
        i, j = self.step(k, count)
        return wrap(self.y + i, 4), wrap(self.z + j, 4)

    def behind(self, k, count):
        i, j = self.step(k, count)
        return wrap(self.y - i, 4), wrap(self.z - j, 4)

    def sibling(self):
        return device(self.y, self.z, self.xl, 1 - self.core, self.half)

    def hello(self, count, others=()):
        barrier = pltpu.get_barrier_semaphore()

        def one(k, carry):
            greet(barrier, self.partner(k, count))
            return carry

        lax.fori_loop(1, count, one, 0)
        for where in others:
            greet(barrier, where)

        @pl.when(jnp.logical_not(self.stays))
        def _():
            greet(barrier, self.partner(0, count))

    def ready(self, count, others=0):
        barrier = pltpu.get_barrier_semaphore()
        pl.semaphore_wait(barrier, count - 1 + others + lax.rem(self.xl + self.core, 2))

    def push(self, k, count, src, dst, outs, ins):
        send(src, dst, outs.at[k], ins.at[k], self.partner(k, count))

    def first(self, count, src, dst, outs, ins):
        @pl.when(self.stays)
        def _():
            pltpu.make_async_copy(src, dst, ins.at[0]).start()

        @pl.when(jnp.logical_not(self.stays))
        def _():
            self.push(0, count, src, dst, outs, ins)

    def start(self, count, src, dst, outs, ins):
        self.first(count, src(0), dst, outs, ins)

        def one(k, carry):
            self.push(k, count, src(k), dst, outs, ins)
            return carry

        lax.fori_loop(1, count, one, 0)

    def end(self, k, count, got, outs, ins):
        finish(got, got, outs.at[k], ins.at[k], self.partner(k, count))

    def end_first(self, count, got, outs, ins):
        @pl.when(self.stays)
        def _():
            pltpu.make_async_copy(got, got, ins.at[0]).wait()

        @pl.when(jnp.logical_not(self.stays))
        def _():
            self.end(0, count, got, outs, ins)

    def mates(self, src, dst, outs, ins):
        self.start(4, lambda k: src.at[self.ahead(k, 4)[1]], dst.at[self.z], outs, ins)

    def mates_end(self, dst, outs, ins):
        self.end_first(4, dst.at[self.z], outs, ins)

        def one(k, carry):
            self.end(k, 4, dst.at[self.behind(k, 4)[1]], outs, ins)
            return carry

        lax.fori_loop(1, 4, one, 0)


def cost(us):
    return pl.CostEstimate(flops=0, transcendentals=0, bytes_accessed=int(us * 3e6))


def remote(number):
    return pltpu.CompilerParams(collective_id=number, has_side_effects=True, vmem_limit_bytes=LIMIT)


def plain():
    return pltpu.CompilerParams(vmem_limit_bytes=LIMIT)


DMA = pltpu.SemaphoreType.DMA


CHUNK = 256
WINDOW = 6


def load_chunk(ref, at):
    return ref[at].reshape(CHUNK, HALF)


def stack_head(ref, h):
    return jnp.concatenate([ref[i][:, h * HD : (h + 1) * HD] for i in range(4)], axis=0)


def turned(rows):
    return rows.astype(F32).T.astype(BF)


class Fetch:
    def __init__(self, turn, sources, fulls, own, sems):
        self.core, self.half = turn.core, turn.half
        y, z, xl = turn.y, turn.z, turn.xl
        self.odd = (lax.rem(y, 2), lax.rem(z, 2), xl)
        self.across = device(y, z, 1 - xl, turn.core, 1 - turn.half)
        self.beside = (
            device(y + 1 - 2 * self.odd[0], z, xl, turn.core, turn.half),
            device(y, z + 1 - 2 * self.odd[1], xl, turn.core, turn.half),
            device(y, z, 1 - xl, turn.core, turn.half),
        )
        self.sibling = turn.sibling()
        self.sources, self.fulls, self.own = sources, fulls, own
        self.sizes = (HALF, FF // 2, HALF)
        self.xs, self.xr, self.ys, self.yr, self.ds, self.dr, self.es, self.er = sems

    def rows(self, n, c, odd):
        size = self.sizes[n]
        if n == 2:
            return odd * (size // 2), size // 2
        return c * (size // 6) + odd * (size // 12), size // 12

    def piece(self, n, half, c, odd):
        start, size = self.rows(n, c, odd)
        return self.fulls[n].at[pl.ds(pl.multiple_of(half * self.sizes[n] + start, 32), size)]

    def each(self, act, flip=False):
        pl.when(self.core == (1 if flip else 0))(lambda: act(0))
        pl.when(self.core == (0 if flip else 1))(lambda: act(1))

    def keep(self):
        for n in range(3):
            rows = self.fulls[n].at[pl.ds(pl.multiple_of(self.half * self.sizes[n], 32), self.sizes[n])]
            yield pltpu.make_async_copy(self.sources[n], rows, self.own.at[n])

    def give(self, n, c, slot):
        odd = 1 - self.odd[2] if c % 3 == 2 else self.odd[c % 3]
        start, size = self.rows(n, c, odd)
        src = self.sources[n].at[pl.ds(pl.multiple_of(start, 32), size)]
        send(src, self.piece(n, self.half, c, odd), self.xs.at[slot], self.xr.at[slot], self.across)

    def own_rows(self):
        for copy in self.keep():
            copy.start()

    def issue(self, c):
        if c == 0:
            pl.when(self.core == 1)(lambda: self.give(2, 1, 6))
        if c < 6:
            self.each(lambda n: self.give(n, c, c))

    def pass_x(self, n, c, slot):
        piece = self.piece(n, 1 - self.half, c, self.odd[c % 3])
        finish(piece, piece, self.xs.at[slot], self.xr.at[slot], self.across)
        send(piece, piece, self.ys.at[slot], self.yr.at[slot], self.beside[c % 3])
        send(piece, piece, self.ds.at[slot], self.dr.at[slot], self.sibling)

    def pass_y(self, n, c, slot):
        piece = self.piece(n, 1 - self.half, c, 1 - self.odd[c % 3])
        finish(piece, piece, self.ys.at[slot], self.yr.at[slot], self.beside[c % 3])
        send(piece, piece, self.es.at[slot], self.er.at[slot], self.sibling)

    def step_x(self, c):
        self.each(lambda n: self.pass_x(n, c, c))
        if c == 0:
            pl.when(self.core == 1)(lambda: self.pass_x(2, 1, 6))

    def step_y(self, c):
        self.each(lambda n: self.pass_y(n, c, c))
        if c == 0:
            pl.when(self.core == 1)(lambda: self.pass_y(2, 1, 6))

    def between(self, n, c, odd, out_sem, in_sem):
        piece = self.piece(n, 1 - self.half, c, odd)
        return pltpu.make_async_remote_copy(
            src_ref=piece, dst_ref=piece, send_sem=out_sem, recv_sem=in_sem,
            device_id=self.sibling, device_id_type=MESH,
        )

    def end(self):
        def sent(n, c, slot):
            odd = self.odd[c % 3]
            self.between(n, c, odd, self.ds.at[slot], self.dr.at[slot]).wait_send()
            self.between(n, c, 1 - odd, self.es.at[slot], self.er.at[slot]).wait_send()

        def came(n, c, slot):
            odd = self.odd[c % 3]
            self.between(n, c, odd, self.ds.at[slot], self.dr.at[slot]).wait_recv()
            self.between(n, c, 1 - odd, self.es.at[slot], self.er.at[slot]).wait_recv()

        def act(n):
            for c in range(6):
                sent(n, c, c)
                came(1 - n, c, c)

        self.each(act)
        pl.when(self.core == 1)(lambda: sent(2, 1, 6))
        pl.when(self.core == 0)(lambda: came(2, 1, 6))
        for copy in self.keep():
            copy.wait()


def front_kernel(
    x_ref, wq, wk, wv, v0, v1, v2, v3, v4, v5, v6, v7, v8, wi, wu, wo,
    a_ref, qo_ref, kvo_ref, ot_ref, lse_ref, w_ref, w_i, w_u, w_o, vec_ref, bi_ref, xo_ref,
    q_ref, kv_ref, small, small_o, o_ref, qt, top, total,
    own_sem, a_out, a_in, b_out, b_in, qs, qr, ks, kr, fs, fr, os, om, own, *rest,
):
    sems, lines = rest[:8], rest[8:]
    turn = Turn()
    y, z, xl, core, half = turn.y, turn.z, turn.xl, turn.core, turn.half
    fetch = Fetch(turn, (wi, wu, wo), (w_i, w_u, w_o), own, sems)
    across, sibling = fetch.across, fetch.sibling
    barrier = pltpu.get_barrier_semaphore()
    greet(barrier, across)
    greet(barrier, sibling)
    greet(barrier, fetch.beside[2])

    def hello(k, carry):
        greet(barrier, turn.partner(k, 16))
        return carry

    lax.fori_loop(1, 16, hello, 0)

    @pl.when(jnp.logical_not(turn.stays))
    def _():
        greet(barrier, turn.partner(0, 16))
        greet(barrier, fetch.beside[0])
        greet(barrier, fetch.beside[1])

    start = pl.multiple_of(core * GROUP, GROUP)
    rows = pl.multiple_of(half * HALF, HALF)
    give = pl.ds(pl.multiple_of(half * HALF + core * GROUP, GROUP), GROUP)
    take = pl.ds(pl.multiple_of((1 - half) * HALF + core * GROUP, GROUP), GROUP)
    last = pl.ds(pl.multiple_of((1 - half) * HALF + (1 - core) * GROUP, GROUP), GROUP)
    mine = [
        pltpu.make_async_copy(w, w_ref.at[i, pl.ds(rows, HALF)], own_sem.at[i]) for i, w in enumerate((wq, wk, wv))
    ]
    for copy in mine:
        copy.start()
    fetch.own_rows()
    vectors = (v0, v1, v2, v3, v4, v5, v6, v7, v8)
    loads = [pltpu.make_async_copy(v, line, own_sem.at[3 + i]) for i, (v, line) in enumerate(zip(vectors, lines))]
    for copy in loads:
        copy.start()
    for copy in loads:
        copy.wait()
    small[...] = jnp.zeros_like(small)
    for i in range(8):
        small[i : i + 1, :] = lines[i][...].astype(F32).reshape(1, HALF)
    for i in range(4):
        small[8 + i : 9 + i, :] = lines[8][i * HALF : (i + 1) * HALF].astype(F32).reshape(1, HALF)
    pl.semaphore_wait(barrier, 18 + 3 * lax.rem(xl + core, 2))
    send(small, small_o, a_out.at[3], a_in.at[3], across)
    for i, w in enumerate((wk, wv, wq)):
        i = (1, 2, 0)[i]
        send(w.at[pl.ds(start, GROUP)], w_ref.at[i, give], a_out.at[i], a_in.at[i], across)
    finish(small_o, small_o, a_out.at[3], a_in.at[3], across)
    near, far = small[...], small_o[...]
    ahead = jnp.where(half == 0, near, far)
    behind = jnp.where(half == 0, far, near)
    vec_ref[:, :HALF] = ahead[:8]
    vec_ref[:, HALF:] = behind[:8]
    for i in range(4):
        bi_ref[:, i * HALF : (i + 1) * HALF] = ahead[8 + i : 9 + i]
        bi_ref[:, 1536 + i * HALF : 1536 + (i + 1) * HALF] = behind[8 + i : 9 + i]
    def spread(k):
        src = kv_ref.at[turn.ahead(k, 16)[1]]
        if isinstance(k, int) and k == 0:
            turn.first(16, src, kvo_ref.at[y, z, xl], ks, kr)
        else:
            turn.push(k, 16, src, kvo_ref.at[y, z, xl], ks, kr)

    send(x_ref, xo_ref, a_out.at[4], a_in.at[4], sibling)
    x = x_ref[...]
    for i in (1, 2, 0):
        piece = w_ref.at[i, take]
        finish(piece, piece, a_out.at[i], a_in.at[i], across)
        send(piece, piece, b_out.at[i], b_in.at[i], sibling)
    for c in range(6):
        fetch.issue(c)
    done = {}
    for i in (1, 2, 0):
        piece = w_ref.at[i, last]
        finish(piece, piece, b_out.at[i], b_in.at[i], sibling)
        mine[i].wait()
        done[i] = nn(x, w_ref[i])
        if i == 2:
            keys = done[1].astype(BF)
            values = (done[2] + vec_ref[1:2, :]).astype(BF)
            for g in range(4):
                cut = slice(g * GROUP, (g + 1) * GROUP)
                kv_ref[g] = jnp.concatenate([keys[:, cut], values[:, cut]], axis=1)
            for k in range(WINDOW):
                spread(k)
    pad = jnp.zeros((ROWS, 64), BF)
    query = (done[0] + vec_ref[0:1, :]).astype(BF) * BF(0.125)
    for g in range(4):
        q_ref[g] = jnp.concatenate([query[:, g * GROUP : (g + 1) * GROUP], pad], axis=1)
    turn.mates(q_ref, qo_ref, qs, qr)

    def onward(k):
        i, j = turn.behind(k, 16)
        piece = kvo_ref.at[i, j, core]
        send(piece, piece, fs.at[k], fr.at[k], sibling)

    turn.mates_end(qo_ref, qs, qr)
    turn.end_first(16, kvo_ref.at[y, z, core], ks, kr)
    onward(0)
    for h in range(3):
        qt[h] = turned(stack_head(qo_ref, h))
    top[...] = jnp.full_like(top, -jnp.inf)
    total[...] = jnp.zeros_like(total)
    ot_ref[...] = jnp.zeros_like(ot_ref)

    def work(k):
        i, j = turn.behind(k, 16)
        piece = kvo_ref.at[i, j, 1 - core]
        finish(piece, piece, fs.at[k], fr.at[k], sibling)
        kv = load_chunk(kvo_ref, (i, j))
        for h in range(3):
            scores = nn(kv[:, h * HD : (h + 1) * HD], qt[h])
            old = top[h]
            new = jnp.maximum(old, jnp.max(scores, axis=0, keepdims=True))
            shrink = jnp.exp(old - new)
            weights = jnp.exp(scores - new)
            total[h] = total[h] * shrink + jnp.sum(weights, axis=0, keepdims=True)
            mixed = tn(kv[:, GROUP + h * HD : GROUP + (h + 1) * HD], weights.astype(BF))
            ot_ref[h] = ot_ref[h] * shrink + mixed
            top[h] = new

    def relay(k, carry):
        i, j = turn.behind(k, 16)
        turn.end(k, 16, kvo_ref.at[i, j, core], ks, kr)
        pl.when(k + WINDOW - 1 < 16)(lambda: spread(k + WINDOW - 1))
        onward(k)
        work(k - 1)

        for c in range(6):
            pl.when(k == c + 10)(functools.partial(fetch.step_x, c))
        return carry

    lax.fori_loop(1, 16, relay, 0)
    work(15)
    heads = []
    for h in range(3):
        lse_ref[h] = top[h] + jnp.log(total[h])
        normal = ot_ref[h] / total[h]
        ot_ref[h] = normal
        heads.append(normal.T.astype(BF))
    heads.append(jnp.zeros((512, 64), BF))
    out = jnp.concatenate(heads, axis=1)
    for i in range(4):
        o_ref[i] = out[i * ROWS : (i + 1) * ROWS]
    turn.mates(o_ref, a_ref, os, om)
    for c in range(6):
        fetch.step_y(c)
    turn.mates_end(a_ref, os, om)
    finish(xo_ref, xo_ref, a_out.at[4], a_in.at[4], sibling)
    fetch.end()


def front(*arrays):
    return pl.pallas_call(
        front_kernel,
        name="front",
        cost_estimate=cost(70),
        out_shape=(
            shape(4, ROWS, 256), shape(4, ROWS, 256), shape(4, 4, 2, ROWS, HALF),
            shape(3, HD, 512, dtype=F32), shape(3, 1, 512, dtype=F32),
            shape(3, D, D), shape(D, FF), shape(FF, D), shape(D, D), shape(8, D, dtype=F32), shape(1, FF, dtype=F32),
            shape(ROWS, D),
        ),
        in_specs=[VM, ANY, ANY, ANY] + [ANY] * 9 + [ANY] * 3,
        out_specs=(VM,) * 12,
        scratch_shapes=[
            pltpu.VMEM((4, ROWS, 256), BF), pltpu.VMEM((4, ROWS, HALF), BF),
            pltpu.VMEM((16, HALF), F32), pltpu.VMEM((16, HALF), F32),
            pltpu.VMEM((4, ROWS, 256), BF),
            pltpu.VMEM((3, HD, 512), BF), pltpu.VMEM((3, 1, 512), F32), pltpu.VMEM((3, 1, 512), F32),
            DMA((12,)), DMA((5,)), DMA((5,)), DMA((3,)), DMA((3,)),
            DMA((4,)), DMA((4,)), DMA((16,)), DMA((16,)), DMA((16,)), DMA((16,)), DMA((4,)), DMA((4,)), DMA((3,)),
        ] + [DMA((7,))] * 8 + [pltpu.VMEM((HALF,), BF)] * 8 + [pltpu.VMEM((1536,), BF)],
        compiler_params=remote(1),
    )(arrays[0], *map(hbm, arrays[1:]))


def norm(hidden):
    centred = hidden - jnp.mean(hidden, axis=-1, keepdims=True)
    inverse = lax.rsqrt(jnp.mean(centred * centred, axis=-1, keepdims=True) + EPS)
    return centred * inverse, inverse


def norm_back(scaled, normal, inverse):
    centre = jnp.mean(scaled, axis=-1, keepdims=True)
    along = jnp.mean(scaled * normal, axis=-1, keepdims=True)
    return inverse * (scaled - centre - normal * along)


def column(value):
    return jnp.sum(value, axis=0, keepdims=True)


def block_kernel(
    x_ref, ct_ref, a_ref, w_i, w_u, w_o, vec_ref, bi_ref,
    out_ref, dh1_ref, da_ref, af_ref, yb_ref, g_ref, df_ref, du_ref, dz_ref, vg_ref,
    af_o, yb_o, g_o, df_o, du_o, dz_o, slope, da_out, outs, ins, p_out, p_in,
):
    turn = Turn()
    turn.hello(4, (turn.sibling(),))
    passed = ((af_ref, af_o), (yb_ref, yb_o), (g_ref, g_o), (df_ref, df_o), (du_ref, du_o), (dz_ref, dz_o))

    def pass_on(n):
        send(*passed[n], p_out.at[n], p_in.at[n], turn.sibling())

    b_output, first_gain, first_shift = vec_ref[2:3, :], vec_ref[3:4, :], vec_ref[4:5, :]
    b_outer, second_gain, second_shift = vec_ref[5:6, :], vec_ref[6:7, :], vec_ref[7:8, :]
    mixed = jnp.concatenate([a_ref[g][:, :GROUP] for g in range(4)], axis=1)
    af_ref[...] = mixed
    hidden = x_ref[...].astype(F32) + nn(mixed, w_o[...]) + b_output
    normal1, inverse1 = norm(hidden)
    normed = normal1 * first_gain + first_shift
    low = normed.astype(BF)
    yb_ref[...] = low
    turn.ready(4, 1)
    pass_on(0)
    pass_on(1)
    second_in = normed + b_outer
    for j in range(4):
        cut = slice(j * D, (j + 1) * D)
        inner = nn(low, w_i[:, cut]) + bi_ref[:, cut]
        cdf = 0.5 * (1.0 + lax.erf(inner * (0.5**0.5)))
        active = (inner * cdf).astype(BF)
        slope[:, cut] = cdf + inner * jnp.exp(inner * inner * -0.5) * 0.3989422804014327
        g_ref[:, cut] = active
        second_in = second_in + nn(active, w_u[cut, :])
    pass_on(2)
    normal2, inverse2 = norm(second_in)
    out_ref[...] = (normal2 * second_gain + second_shift).astype(BF)
    upper = ct_ref[...].astype(F32)


    def note(row, value):
        for h in range(2):
            vg_ref[h, row : row + 1, :] = value[:, h * HALF : (h + 1) * HALF]

    vg_ref[...] = jnp.zeros_like(vg_ref)
    note(6, column(upper * normal2))
    note(7, column(upper))
    dh2 = norm_back(upper * second_gain, normal2, inverse2)
    df = dh2.astype(BF)
    df_ref[...] = df
    pass_on(3)
    note(5, column(df.astype(F32)))
    dy1 = dh2
    for j in range(4):
        cut = slice(j * D, (j + 1) * D)
        du = (slope[:, cut] * nt(df, w_u[cut, :])).astype(BF)
        du_ref[:, cut] = du
        sums = column(du.astype(F32))
        for i in range(2):
            n = 2 * j + i
            vg_ref[n // 4, 8 + n % 4 : 9 + n % 4, :] = sums[:, i * HALF : (i + 1) * HALF]
        dy1 = dy1 + nt(du, w_i[:, cut])
    pass_on(4)
    note(3, column(dy1 * normal1))
    note(4, column(dy1))
    dh1 = norm_back(dy1 * first_gain, normal1, inverse1)
    dh1_ref[...] = dh1
    dz = dh1.astype(BF)
    dz_ref[...] = dz
    pass_on(5)
    note(2, column(dz.astype(F32)))
    da = nt(dz, w_o[...]).astype(BF)
    pad = jnp.zeros((ROWS, 64), BF)
    for g in range(4):
        da_out[g] = jnp.concatenate([da[:, g * GROUP : (g + 1) * GROUP], pad], axis=1)
    turn.mates(da_out, da_ref, outs, ins)
    turn.mates_end(da_ref, outs, ins)
    for n, (src, got) in enumerate(passed):
        finish(src, got, p_out.at[n], p_in.at[n], turn.sibling())


def block(*arrays):
    return pl.pallas_call(
        block_kernel,
        name="block",
        cost_estimate=cost(12),
        out_shape=(
            plain_shape(ROWS, D), shape(ROWS, D, dtype=F32), shape(4, ROWS, 256), shape(ROWS, D), shape(ROWS, D),
            shape(ROWS, FF), shape(ROWS, D), shape(ROWS, FF), shape(ROWS, D),
            shape(2, 16, HALF, dtype=F32), shape(ROWS, D), shape(ROWS, D), shape(ROWS, FF), shape(ROWS, D),
            shape(ROWS, FF), shape(ROWS, D),
        ),
        in_specs=[VM] * 8,
        out_specs=(VM,) * 16,
        scratch_shapes=[
            pltpu.VMEM((ROWS, FF), F32), pltpu.VMEM((4, ROWS, 256), BF), DMA((4,)), DMA((4,)), DMA((6,)), DMA((6,)),
        ],
        compiler_params=remote(2),
    )(arrays[0], arrays[1], *map(vm, arrays[2:]))


EARLY = (0, 3)
LATE = (3, 1)


def back_kernel(
    q_ref, kv_ref, da_ref, ot_ref, lse_ref, x, x_o, yb, yb_o, g, g_o, a, a_o, df, df_o, du, du_o, dz, dz_o,
    dh1_ref, w_ref, vg_in,
    grad_ref, out, vo,
    rows_q, qt, rows_d, dt, delta, acc, dkv, other, dq, dqo, home, low, low_o, vg,
    g0, g1, g2, r0, r1, r2, s0, s1, s2, t0, t1, t2, rv, sv, tv, uv,
    fs, fr, ks, kr, qs, qr, ls, lr, a_out, a_in, b_out, b_in, c_out, c_in, d_out, d_in, e_out, e_in,
):
    turn = Turn()
    y, z, xl, core, half = turn.y, turn.z, turn.xl, turn.core, turn.half
    x_at = half * 2 + xl
    sibling = turn.sibling()
    barrier = pltpu.get_barrier_semaphore()

    def at(x_to, y_to, z_to):
        return device(y_to, z_to, lax.rem(x_to, 2), core, lax.div(x_to, 2))

    def along_x(k):
        return at(wrap(x_at + k, 4), y, z)

    def at_yz(k):
        i, j = pair(k)
        return at(x_at, wrap(y + i, 4), wrap(z + j, 4))

    def at_xz(k):
        i, j = pair(k)
        return at(wrap(x_at + i, 4), y, wrap(z + j, 4))

    def at_xy(k):
        i, j = pair(k)
        return at(wrap(x_at + i, 4), wrap(y + j, 4), z)

    def hello_yz(k, carry):
        greet(barrier, at_yz(k))
        return carry

    def hello_x(k, carry):
        i = lax.div(k - 1, 3) + 1
        j = lax.rem(k - 1, 3) + 1
        greet(barrier, at_xz(i * 4 + j))
        greet(barrier, at_xy(i * 4 + j))
        return carry

    def hello_row(k, carry):
        greet(barrier, along_x(k))
        return carry

    def hello_turn(k, carry):
        greet(barrier, turn.partner(k, 16))
        return carry

    lax.fori_loop(1, 16, hello_yz, 0)
    lax.fori_loop(1, 10, hello_x, 0)
    lax.fori_loop(1, 4, hello_row, 0)
    greet(barrier, sibling)

    @pl.when(jnp.logical_not(turn.stays))
    def _():
        lax.fori_loop(0, 16, hello_turn, 0)

    def put(slab, f, m, value):
        blocks = value.astype(BF).reshape(4, 2, 48, HALF)
        if slab == 1:
            g1[f, :, m] = blocks
        else:
            (g0 if slab == 0 else g2)[f, m] = blocks

    def right(ref, second, start):
        cols = pl.ds(pl.multiple_of(start + core * HALF, HALF), HALF)
        return jnp.concatenate([ref[:, cols], second[:, cols]], axis=0)

    def left(ref, second, start):
        return jnp.concatenate([ref[:, start : start + HALF], second[:, start : start + HALF]], axis=0)

    outer = right(df, df_o, 0)
    attn = right(dz, dz_o, 0)
    for f in range(2):
        for m in range(4):
            put(*((1, f, m) if m < 3 else (0, f, 0)), tn(left(g, g_o, f * 1536 + m * HALF), outer))
        rows = left(yb, yb_o, f * HALF)
        for m in range(4):
            put(*((2, f, m) if m < 3 else (0, f, 1)), tn(rows, right(du, du_o, m * D)))
        put(0, f, 2, tn(left(a, a_o, f * HALF), attn))
    pl.semaphore_wait(barrier, 37 + 16 * lax.rem(xl + core, 2))

    def first(part):
        m, n = part
        late = 0 if part is EARLY else 4

        def one(k, carry):
            e = wrap(x_at + k, 4)
            send(
                g1.at[:, wrap(y + k, 4), pl.ds(m, n)], r1.at[k - 1, :, pl.ds(m, n)],
                a_out.at[late + 1, k], a_in.at[late + 1, k], at_yz(k * 4),
            )
            send(
                g2.at[:, pl.ds(m, n), wrap(z + k, 4)], r2.at[k - 1, :, pl.ds(m, n)],
                a_out.at[late + 2, k], a_in.at[late + 2, k], at_yz(k),
            )
            send(
                g0.at[lax.div(e, 2), pl.ds(m, n), :, lax.rem(e, 2)], r0.at[k - 1, pl.ds(m, n)],
                a_out.at[late, k], a_in.at[late, k], along_x(k),
            )
            return carry

        lax.fori_loop(1, 4, one, 0)

    first(EARLY)

    for h in range(3):
        rows = stack_head(q_ref, h)
        rows_q[h] = rows
        qt[h] = turned(rows)
        rows = stack_head(da_ref, h)
        rows_d[h] = rows
        flipped = rows.astype(F32).T
        dt[h] = flipped.astype(BF)
        delta[h] = jnp.sum(flipped * ot_ref[h], axis=0, keepdims=True)
    acc[...] = jnp.zeros_like(acc)

    def work(k):
        i, j = turn.ahead(k, 16)
        kv = load_chunk(kv_ref, (i, j))
        keys, values = [], []
        for h in range(3):
            key = kv[:, h * HD : (h + 1) * HD]
            value = kv[:, GROUP + h * HD : GROUP + (h + 1) * HD]
            probs = jnp.exp(nn(key, qt[h]) - lse_ref[h])
            slopes = (probs * (nn(value, dt[h]) - delta[h])).astype(BF)
            keys.append(nn(slopes, rows_q[h]).astype(BF))
            values.append(nn(probs.astype(BF), rows_d[h]).astype(BF))
            acc[h] += tn(key, slopes)
        dkv[i, j] = jnp.concatenate(keys + values, axis=1).reshape(2, ROWS, HALF)
        send(dkv.at[i, j, 1 - core], other.at[i, j], fs.at[k], fr.at[k], sibling)

    def join(k):
        i, j = turn.ahead(k, 16)
        finish(other.at[i, j], other.at[i, j], fs.at[k], fr.at[k], sibling)
        other[i, j] = (dkv[i, j, core].astype(F32) + other[i, j].astype(F32)).astype(BF)

    def relay(k):
        join(k)
        turn.push(k, 16, other.at[turn.ahead(k, 16)], home.at[y, z], ks, kr)

    work(0)
    work(1)
    join(0)
    turn.first(16, other.at[y, z], home.at[y, z], ks, kr)

    def step(k, carry):
        work(k)
        relay(k - 1)
        return carry

    lax.fori_loop(2, 16, step, 0)
    relay(15)
    heads = [(acc[h] * 0.125).T.astype(BF) for h in range(3)]
    heads.append(jnp.zeros((512, 64), BF))
    turned_back = jnp.concatenate(heads, axis=1)
    for i in range(4):
        dq[i] = turned_back[i * ROWS : (i + 1) * ROWS]
    turn.mates(dq, dqo, qs, qr)

    here = device(y, z, xl, core, half)

    def second(part):
        m, n = part
        late = 0 if part is EARLY else 4

        def add(slab, own, got, to, count, where):
            for k in range(1, 4):
                piece = got.at[k - 1, pl.ds(m, n)] if slab == 0 else got.at[k - 1, :, pl.ds(m, n)]
                finish(piece, piece, a_out.at[late + slab, k], a_in.at[late + slab, k], here)

            def one(i, carry):
                p = where(i)
                total = own(p).astype(F32)
                for k in range(3):
                    total = total + got[(k,) + p].astype(F32)
                to[p] = total.astype(BF)
                return carry

            lax.fori_loop(0, count, one, 0)

        def push(slab, src, got, k, where):
            @pl.when(k > 0)
            def _():
                send(src, got.at[k], b_out.at[slab, k], b_in.at[slab, k], where)

        def spot(i):
            return lax.div(i, 2 * n), m + lax.rem(lax.div(i, 2), n), lax.rem(i, 2)

        add(1, lambda p: g1[p[0], y, p[1], p[2]], r1, s1, 4 * n, spot)

        def push1(i, carry):
            e, to = wrap(x_at + lax.div(i, n), 4), m + lax.rem(i, n)
            k = lax.div(i, n) * 4 + wrap(to - z, 4)
            push(1, s1.at[lax.div(e, 2), to, lax.rem(e, 2)], t1, k, at(e, y, to))
            return carry

        lax.fori_loop(0, 4 * n, push1, 0)
        add(2, lambda p: g2[p[0], p[1], z, p[2]], r2, s2, 4 * n, spot)

        def push2(i, carry):
            e, to = wrap(x_at + lax.div(i, n), 4), m + lax.rem(i, n)
            k = lax.div(i, n) * 4 + wrap(to - y, 4)
            push(2, s2.at[lax.div(e, 2), to, lax.rem(e, 2)], t2, k, at(e, to, z))
            return carry

        lax.fori_loop(0, 4 * n, push2, 0)
        add(
            0, lambda p: g0[half, p[0], p[1], xl], r0, s0, 4 * n,
            lambda i: (m + lax.div(i, 4), lax.rem(i, 4)),
        )

        def push0(i, carry):
            e, to = wrap(z + lax.div(i, n), 4), m + lax.rem(i, n)
            k = wrap(to - y, 4) * 4 + lax.div(i, n)
            push(0, s0.at[to, e], t0, k, at(x_at, to, e))
            return carry

        lax.fori_loop(0, 4 * n, push0, 0)

    second(EARLY)

    turn.mates_end(dqo, qs, qr)
    turn.end_first(16, home.at[y, z], ks, kr)

    def done(k, carry):
        turn.end(k, 16, home.at[turn.behind(k, 16)], ks, kr)
        return carry

    lax.fori_loop(1, 16, done, 0)
    low[0] = jnp.concatenate([dqo[i][:, :GROUP] for i in range(4)], axis=1)
    sums = []
    for i in range(4):
        total = home[0, i].astype(F32)
        for k in range(1, 4):
            total = total + home[k, i].astype(F32)
        sums.append(total.astype(BF))
    low[1] = jnp.concatenate([v[:, :GROUP] for v in sums], axis=1)
    low[2] = jnp.concatenate([v[:, GROUP:] for v in sums], axis=1)
    send(low, low_o, ls, lr, sibling)
    grad = dh1_ref[...]
    for i in range(3):
        grad = grad + nt(low[i], w_ref[i])
    grad_ref[...] = grad
    vg[...] = vg_in[...]
    for row, i in ((0, 0), (1, 2)):
        value = column(low[i].astype(F32))
        for f in range(2):
            vg[f, row : row + 1, :] = value[:, f * HALF : (f + 1) * HALF]

    def first3(k, carry):
        src = vg.at[lax.div(wrap(x_at + k, 4), 2)]
        send(src, rv.at[k - 1], a_out.at[3, k], a_in.at[3, k], along_x(k))
        return carry

    lax.fori_loop(1, 4, first3, 0)
    finish(low, low_o, ls, lr, sibling)
    cols = pl.ds(pl.multiple_of(core * HALF, HALF), HALF)
    both_low = [jnp.concatenate([low[i, :, cols], low_o[i, :, cols]], axis=0) for i in range(3)]
    for f in range(2):
        rows = left(x, x_o, f * HALF)
        for i, slab in enumerate((2, 1, 0)):
            put(slab, f, 3, tn(rows, both_low[i]))
    first(LATE)

    def third(part):
        early = part is EARLY

        def whole(own, got, slab):
            def wait(k, carry):
                arrived(got.at[k], b_in.at[slab, k], here)
                return carry

            lax.fori_loop(1, 16, wait, 0)

            def one(k, total):
                return total + got[k].astype(F32)

            out[core, slab, y, z, xl] = lax.fori_loop(1, 16, one, own.astype(F32)).astype(BF)

        def spread(slab, count, where):
            mine = out.at[core, slab, y, z, xl]

            def one(k, carry):
                send(mine, mine, c_out.at[slab, k], c_in.at[slab, k], where(k))
                return carry

            lax.fori_loop(1, count, one, 0)

        @pl.when(z < 3 if early else z == 3)
        def _():
            whole(s1[half, z, xl], t1, 1)
            spread(1, 8, lambda k: device(y, wrap(z + lax.div(k, 2), 4), wrap(xl + lax.rem(k, 2), 2), core, half))

        @pl.when(y < 3 if early else y == 3)
        def _():
            whole(s2[half, y, xl], t2, 2)
            spread(2, 8, lambda k: device(wrap(y + lax.div(k, 2), 4), z, wrap(xl + lax.rem(k, 2), 2), core, half))
            whole(s0[y, z], t0, 0)
            spread(0, 16, at_yz)

    def fourth(part):
        m, n = part
        late = 0 if part is EARLY else 3

        def wait(slab, piece, k):
            @pl.when(k > 0)
            def _():
                arrived(piece, c_in.at[slab, k], here)

        def got1(i, carry):
            zz, xx = m + lax.div(i, 2), lax.rem(i, 2)
            wait(1, out.at[core, 1, y, zz, xx], wrap(z - zz, 4) * 2 + wrap(xl - xx, 2))
            return carry

        lax.fori_loop(0, 2 * n, got1, 0)

        def push1(k, carry):
            mine = out.at[core, 1, y, pl.ds(m, n)]
            send(mine, mine, d_out.at[late + 1, k], d_in.at[late + 1, k], at_yz(k * 4))
            return carry

        lax.fori_loop(1, 4, push1, 0)

        def got2(i, carry):
            yy, xx = m + lax.div(i, 2), lax.rem(i, 2)
            wait(2, out.at[core, 2, yy, z, xx], wrap(y - yy, 4) * 2 + wrap(xl - xx, 2))
            return carry

        lax.fori_loop(0, 2 * n, got2, 0)

        def push2(k, carry):
            mine = out.at[core, 2, pl.ds(m, n), z]
            send(mine, mine, d_out.at[late + 2, k], d_in.at[late + 2, k], at_yz(k))
            return carry

        lax.fori_loop(1, 4, push2, 0)

        def got0(i, carry):
            yy, zz = m + lax.div(i, 4), lax.rem(i, 4)
            wait(0, out.at[core, 0, yy, zz, xl], wrap(y - yy, 4) * 4 + wrap(z - zz, 4))
            return carry

        lax.fori_loop(0, 4 * n, got0, 0)
        mine0 = out.at[core, 0, pl.ds(m, n), :, xl]
        send(mine0, mine0, d_out.at[late, 1], d_in.at[late, 1], device(y, z, 1 - xl, core, half))

    def own_part(slab, who, part):
        m, n = part
        return out.at[who, 1, :, pl.ds(m, n)] if slab == 1 else out.at[who, slab, pl.ds(m, n)]

    def last(part):
        m, n = part
        late = 0 if part is EARLY else 3

        def got1(k, carry):
            piece = out.at[core, 1, wrap(y - k, 4), pl.ds(m, n)]
            finish(piece, piece, d_out.at[late + 1, k], d_in.at[late + 1, k], here)
            return carry

        def got2(k, carry):
            piece = out.at[core, 2, pl.ds(m, n), wrap(z - k, 4)]
            finish(piece, piece, d_out.at[late + 2, k], d_in.at[late + 2, k], here)
            return carry

        def onward(slab):
            piece = own_part(slab, core, part)
            send(piece, piece, e_out.at[late + slab], e_in.at[late + slab], sibling)

        lax.fori_loop(1, 4, got1, 0)
        onward(1)
        lax.fori_loop(1, 4, got2, 0)
        onward(2)
        piece0 = out.at[core, 0, pl.ds(m, n), :, 1 - xl]
        finish(piece0, piece0, d_out.at[late, 1], d_in.at[late, 1], here)
        onward(0)

    third(EARLY)
    for k in range(1, 4):
        finish(rv.at[k - 1], rv.at[k - 1], a_out.at[3, k], a_in.at[3, k], here)
    part_sum = vg[half] + rv[0] + rv[1] + rv[2]
    sv[...] = part_sum.astype(BF)

    def second3(k, carry):
        send(sv, tv.at[k], b_out.at[3, k], b_in.at[3, k], at_yz(k))
        return carry

    lax.fori_loop(1, 16, second3, 0)
    second(LATE)
    fourth(EARLY)
    third(LATE)

    def done3(k, total):
        finish(tv.at[k], tv.at[k], b_out.at[3, k], b_in.at[3, k], here)
        return total + tv[k].astype(F32)

    vo[...] = lax.fori_loop(1, 16, done3, part_sum)
    send(vo, uv, e_out.at[6], e_in.at[6], sibling)
    fourth(LATE)
    last(EARLY)
    last(LATE)
    for late, part in ((0, EARLY), (3, LATE)):
        for slab in range(3):
            piece = own_part(slab, 1 - core, part)
            finish(piece, piece, e_out.at[late + slab], e_in.at[late + slab], here)
    for slab, count, own, got in ((1, 8, s1, t1), (2, 8, s2, t2), (0, 16, s0, t0)):
        mine = out.at[core, slab, y, z, xl]

        def gone2(k, carry):
            left_here(got.at[k], b_out.at[slab, k], here)
            return carry

        def gone3(k, carry):
            left_here(mine, c_out.at[slab, k], here)
            return carry

        lax.fori_loop(1, 16, gone2, 0)
        lax.fori_loop(1, count, gone3, 0)
    finish(uv, uv, e_out.at[6], e_in.at[6], here)
    vo[...] = vo[...] + uv[...]


def back(*arrays):
    blk = (48, HALF)
    scratch = [
        ((3, 512, HD), BF), ((3, HD, 512), BF), ((3, 512, HD), BF), ((3, HD, 512), BF), ((3, 1, 512), F32),
        ((3, HD, 512), F32), ((4, 4, 2, ROWS, HALF), BF), ((4, 4, ROWS, HALF), BF),
        ((4, ROWS, 256), BF), ((4, ROWS, 256), BF), ((4, 4, ROWS, HALF), BF), ((3, ROWS, D), BF), ((3, ROWS, D), BF),
        ((2, 16, HALF), F32),
        ((2, 4, 4, 2, *blk), BF), ((2, 4, 4, 2, *blk), BF), ((2, 4, 4, 2, *blk), BF),
        ((3, 4, 4, *blk), BF), ((3, 2, 4, 2, *blk), BF), ((3, 2, 4, 2, *blk), BF),
        ((4, 4, *blk), BF), ((2, 4, 2, *blk), BF), ((2, 4, 2, *blk), BF),
        ((16, *blk), BF), ((16, *blk), BF), ((16, *blk), BF),
        ((3, 16, HALF), F32), ((16, HALF), BF), ((16, 16, HALF), BF), ((16, HALF), F32),
    ]
    return pl.pallas_call(
        back_kernel,
        name="back",
        cost_estimate=cost(100),
        out_shape=(
            plain_shape(ROWS, D, dtype=F32), shape(2, 3, 4, 4, 2, *blk), shape(16, HALF, dtype=F32),
        ),
        in_specs=[VM] * 22,
        out_specs=(VM,) * 3,
        scratch_shapes=[pltpu.VMEM(*v) for v in scratch] + [
            DMA((16,)), DMA((16,)), DMA((16,)), DMA((16,)), DMA((4,)), DMA((4,)), DMA, DMA,
            DMA((7, 4)), DMA((7, 4)), DMA((4, 16)), DMA((4, 16)), DMA((3, 16)), DMA((3, 16)),
            DMA((6, 4)), DMA((6, 4)), DMA((7,)), DMA((7,)),
        ],
        compiler_params=pltpu.CompilerParams(
            collective_id=3, has_side_effects=True, vmem_limit_bytes=29 << 20
        ),
    )(*map(vm, arrays))


def spell_kernel(full, q_ref, k_ref, v_ref, o_ref, i_ref, u_ref, stage, sems):
    def copies(n):
        slot = stage.at[n % 2]
        rows = slice(n * 48, (n + 1) * 48)
        made = [
            pltpu.make_async_copy(slot.at[m], ref.at[rows], sems.at[n % 2, m])
            for m, ref in enumerate((q_ref, k_ref, v_ref, o_ref))
        ]
        for m in range(4):
            made.append(pltpu.make_async_copy(
                slot.at[4 + m], i_ref.at[rows, m * D : (m + 1) * D], sems.at[n % 2, 4 + m]
            ))
            made.append(pltpu.make_async_copy(
                slot.at[8 + m], u_ref.at[m * HALF + n * 48 : m * HALF + (n + 1) * 48], sems.at[n % 2, 8 + m]
            ))
        return made

    for n in range(8):
        if n >= 2:
            for copy in copies(n - 2):
                copy.wait()
        i, xl = n // 2, n % 2
        for c in range(2):
            cols = slice(c * HALF, (c + 1) * HALF)
            units = [(2, 3), (1, 3), (0, 3), (0, 2), (2, 0), (2, 1), (2, 2), (0, 1), (1, 0), (1, 1), (1, 2), (0, 0)]
            for m, (slab, unit) in enumerate(units):
                piece = full[c, 1, i, unit, xl] if slab == 1 else full[c, slab, unit, i, xl]
                stage[n % 2, m, :, cols] = piece.astype(F32)
        for copy in copies(n):
            copy.start()
    for n in (6, 7):
        for copy in copies(n):
            copy.wait()


def spell(summed):
    return pl.pallas_call(
        spell_kernel,
        name="spell",
        out_shape=tuple(
            plain_shape(*dims, dtype=F32)
            for dims in ((HALF, D), (HALF, D), (HALF, D), (HALF, D), (HALF, FF), (1536, D))
        ),
        in_specs=[VM],
        out_specs=(ANY,) * 6,
        scratch_shapes=[pltpu.VMEM((2, 12, 48, D), F32), DMA((2, 12))],
        compiler_params=plain(),
        cost_estimate=cost(6),
    )(vm(summed))


def local(
    tokens, cotangent, w_query, w_key, w_value, w_output, b_query, b_value, b_output,
    first_gain, first_shift, w_inner, b_inner, w_outer, b_outer, second_gain, second_shift,
):
    x = tokens[0]
    mixed, q_all, kv_all, mixed_t, lse, w_qkv, w_i, w_u, w_o, vec, bi, x_o = front(
        x, w_query, w_key, w_value, b_query, b_value, b_output, first_gain, first_shift, b_outer, second_gain,
        second_shift, b_inner, w_inner, w_outer, w_output,
    )
    layer_out, dh1, da_all, a, yb, g, df, du, dz, vg, a_o, yb_o, g_o, df_o, du_o, dz_o = block(
        x, cotangent[0], mixed, w_i, w_u, w_o, vec, bi
    )
    tokens_grad, summed, vecs = back(
        q_all, kv_all, da_all, mixed_t, lse, x, x_o, yb, yb_o, g, g_o, a, a_o, df, df_o, du, du_o, dz, dz_o,
        dh1, w_qkv, vg,
    )
    gq, gk, gv, go, gi, gu = spell(summed)
    return (
        layer_out[None], tokens_grad[None], gq, gk, gv, go,
        vecs[0], vecs[1], vecs[2], vecs[3], vecs[4], gi, vecs[8:12].reshape(1536), gu, vecs[5], vecs[6], vecs[7],
    )


def solution(mesh):
    rows = P(("seq", "fsdp"), "ctx", None)
    mat = P("fsdp", None)
    vec = P("fsdp")
    return jax.shard_map(
        local,
        mesh=mesh,
        in_specs=(rows, rows, mat, mat, mat, mat, vec, vec, vec, vec, vec, mat, vec, mat, vec, vec, vec),
        out_specs=(rows, rows, mat, mat, mat, mat, vec, vec, vec, vec, vec, mat, vec, mat, vec, vec, vec),
        check_vma=False,
    )
```

```python
import functools

import jax
import jax.numpy as jnp
from jax import lax
from jax.experimental import pallas as pl
from jax.experimental.pallas import tpu as pltpu
from jax.sharding import PartitionSpec as P

AXES = ("ctx", "seq", "fsdp")
MESH = pl.DeviceIdType.MESH
BF = jnp.bfloat16
F32 = jnp.float32
D = 768
FF = 3072
HALF = 384
GROUP = 192
HD = 64
ROWS = 128
EPS = 1e-12
LIMIT = 12 << 20
VM = pl.BlockSpec(memory_space=pltpu.VMEM)
ANY = pl.BlockSpec(memory_space=pltpu.HBM)


def plain_shape(*dims, dtype=BF):
    return jax.ShapeDtypeStruct(dims, dtype)


def shape(*dims, dtype=BF):
    return pltpu.VMEM(dims, dtype)


def hbm(array):
    return pltpu.with_memory_space_constraint(array, pltpu.HBM)


def vm(array):
    return pltpu.with_memory_space_constraint(array, pltpu.VMEM)


def nn(left, right):
    return jnp.dot(left, right, preferred_element_type=F32)


def nt(left, right):
    return lax.dot_general(left, right, (((1,), (1,)), ((), ())), preferred_element_type=F32)


def tn(left, right):
    return lax.dot_general(left, right, (((0,), (0,)), ((), ())), preferred_element_type=F32)


def wrap(value, size):
    return lax.rem(value + size, size)


def place():
    ctx = lax.axis_index("ctx")
    y = lax.div(ctx, 8)
    z = lax.rem(lax.div(ctx, 2), 4)
    return y, z, lax.rem(ctx, 2), lax.axis_index("seq"), lax.axis_index("fsdp")


def device(y, z, xl, core, half):
    return ((y * 4 + z) * 2 + xl, core, half)


def send(src, dst, out_sem, in_sem, where):
    pltpu.make_async_remote_copy(
        src_ref=src, dst_ref=dst, send_sem=out_sem, recv_sem=in_sem,
        device_id=where, device_id_type=MESH,
    ).start()


def finish(src, dst, out_sem, in_sem, where):
    copy = pltpu.make_async_remote_copy(
        src_ref=src, dst_ref=dst, send_sem=out_sem, recv_sem=in_sem,
        device_id=where, device_id_type=MESH,
    )
    copy.wait_send()
    copy.wait_recv()


def arrived(got, in_sem, where):
    pltpu.make_async_remote_copy(
        src_ref=got, dst_ref=got, send_sem=in_sem, recv_sem=in_sem, device_id=where, device_id_type=MESH
    ).wait_recv()


def left_here(src, out_sem, where):
    pltpu.make_async_remote_copy(
        src_ref=src, dst_ref=src, send_sem=out_sem, recv_sem=out_sem, device_id=where, device_id_type=MESH
    ).wait_send()


def greet(barrier, where):
    pl.semaphore_signal(barrier, inc=1, device_id=where, device_id_type=MESH)


def pair(k):
    return lax.div(k, 4), lax.rem(k, 4)


class Turn:
    def __init__(self):
        self.y, self.z, self.xl, self.core, self.half = place()
        self.stays = self.xl == self.core

    def step(self, k, count):
        if count == 4:
            return 0, k
        return lax.rem(k + lax.div(k, 4), 4), lax.rem(k, 4)

    def partner(self, k, count):
        i, j = self.ahead(k, count)
        return device(i, j, self.core, self.xl, self.half)

    def ahead(self, k, count):
        i, j = self.step(k, count)
        return wrap(self.y + i, 4), wrap(self.z + j, 4)

    def behind(self, k, count):
        i, j = self.step(k, count)
        return wrap(self.y - i, 4), wrap(self.z - j, 4)

    def sibling(self):
        return device(self.y, self.z, self.xl, 1 - self.core, self.half)

    def hello(self, count, others=()):
        barrier = pltpu.get_barrier_semaphore()

        def one(k, carry):
            greet(barrier, self.partner(k, count))
            return carry

        lax.fori_loop(1, count, one, 0)
        for where in others:
            greet(barrier, where)

        @pl.when(jnp.logical_not(self.stays))
        def _():
            greet(barrier, self.partner(0, count))

    def ready(self, count, others=0):
        barrier = pltpu.get_barrier_semaphore()
        pl.semaphore_wait(barrier, count - 1 + others + lax.rem(self.xl + self.core, 2))

    def push(self, k, count, src, dst, outs, ins):
        send(src, dst, outs.at[k], ins.at[k], self.partner(k, count))

    def first(self, count, src, dst, outs, ins):
        @pl.when(self.stays)
        def _():
            pltpu.make_async_copy(src, dst, ins.at[0]).start()

        @pl.when(jnp.logical_not(self.stays))
        def _():
            self.push(0, count, src, dst, outs, ins)

    def start(self, count, src, dst, outs, ins):
        self.first(count, src(0), dst, outs, ins)

        def one(k, carry):
            self.push(k, count, src(k), dst, outs, ins)
            return carry

        lax.fori_loop(1, count, one, 0)

    def end(self, k, count, got, outs, ins):
        finish(got, got, outs.at[k], ins.at[k], self.partner(k, count))

    def end_first(self, count, got, outs, ins):
        @pl.when(self.stays)
        def _():
            pltpu.make_async_copy(got, got, ins.at[0]).wait()

        @pl.when(jnp.logical_not(self.stays))
        def _():
            self.end(0, count, got, outs, ins)

    def mates(self, src, dst, outs, ins):
        self.start(4, lambda k: src.at[self.ahead(k, 4)[1]], dst.at[self.z], outs, ins)

    def mates_end(self, dst, outs, ins):
        self.end_first(4, dst.at[self.z], outs, ins)

        def one(k, carry):
            self.end(k, 4, dst.at[self.behind(k, 4)[1]], outs, ins)
            return carry

        lax.fori_loop(1, 4, one, 0)


def cost(us):
    return pl.CostEstimate(flops=0, transcendentals=0, bytes_accessed=int(us * 3e6))


def remote(number):
    return pltpu.CompilerParams(collective_id=number, has_side_effects=True, vmem_limit_bytes=LIMIT)


def plain():
    return pltpu.CompilerParams(vmem_limit_bytes=LIMIT)


DMA = pltpu.SemaphoreType.DMA


CHUNK = 256
WINDOW = 6


def load_chunk(ref, at):
    return ref[at].reshape(CHUNK, HALF)


def stack_head(ref, h):
    return jnp.concatenate([ref[i][:, h * HD : (h + 1) * HD] for i in range(4)], axis=0)


def turned(rows):
    return rows.astype(F32).T.astype(BF)


class Fetch:
    def __init__(self, turn, sources, fulls, own, sems):
        self.core, self.half = turn.core, turn.half
        y, z, xl = turn.y, turn.z, turn.xl
        self.odd = (lax.rem(y, 2), lax.rem(z, 2), xl)
        self.across = device(y, z, 1 - xl, turn.core, 1 - turn.half)
        self.beside = (
            device(y + 1 - 2 * self.odd[0], z, xl, turn.core, turn.half),
            device(y, z + 1 - 2 * self.odd[1], xl, turn.core, turn.half),
            device(y, z, 1 - xl, turn.core, turn.half),
        )
        self.sibling = turn.sibling()
        self.sources, self.fulls, self.own = sources, fulls, own
        self.sizes = (HALF, FF // 2, HALF)
        self.xs, self.xr, self.ys, self.yr, self.ds, self.dr, self.es, self.er = sems

    def rows(self, n, c, odd):
        size = self.sizes[n]
        if n == 2:
            return odd * (size // 2), size // 2
        return c * (size // 6) + odd * (size // 12), size // 12

    def piece(self, n, half, c, odd):
        start, size = self.rows(n, c, odd)
        return self.fulls[n].at[pl.ds(pl.multiple_of(half * self.sizes[n] + start, 32), size)]

    def each(self, act, flip=False):
        pl.when(self.core == (1 if flip else 0))(lambda: act(0))
        pl.when(self.core == (0 if flip else 1))(lambda: act(1))

    def keep(self):
        for n in range(3):
            rows = self.fulls[n].at[pl.ds(pl.multiple_of(self.half * self.sizes[n], 32), self.sizes[n])]
            yield pltpu.make_async_copy(self.sources[n], rows, self.own.at[n])

    def give(self, n, c, slot):
        odd = 1 - self.odd[2] if c % 3 == 2 else self.odd[c % 3]
        start, size = self.rows(n, c, odd)
        src = self.sources[n].at[pl.ds(pl.multiple_of(start, 32), size)]
        send(src, self.piece(n, self.half, c, odd), self.xs.at[slot], self.xr.at[slot], self.across)

    def own_rows(self):
        for copy in self.keep():
            copy.start()

    def issue(self, c):
        if c == 0:
            pl.when(self.core == 1)(lambda: self.give(2, 1, 6))
        if c < 6:
            self.each(lambda n: self.give(n, c, c))

    def pass_x(self, n, c, slot):
        piece = self.piece(n, 1 - self.half, c, self.odd[c % 3])
        finish(piece, piece, self.xs.at[slot], self.xr.at[slot], self.across)
        send(piece, piece, self.ys.at[slot], self.yr.at[slot], self.beside[c % 3])
        send(piece, piece, self.ds.at[slot], self.dr.at[slot], self.sibling)

    def pass_y(self, n, c, slot):
        piece = self.piece(n, 1 - self.half, c, 1 - self.odd[c % 3])
        finish(piece, piece, self.ys.at[slot], self.yr.at[slot], self.beside[c % 3])
        send(piece, piece, self.es.at[slot], self.er.at[slot], self.sibling)

    def step_x(self, c):
        self.each(lambda n: self.pass_x(n, c, c))
        if c == 0:
            pl.when(self.core == 1)(lambda: self.pass_x(2, 1, 6))

    def step_y(self, c):
        self.each(lambda n: self.pass_y(n, c, c))
        if c == 0:
            pl.when(self.core == 1)(lambda: self.pass_y(2, 1, 6))

    def between(self, n, c, odd, out_sem, in_sem):
        piece = self.piece(n, 1 - self.half, c, odd)
        return pltpu.make_async_remote_copy(
            src_ref=piece, dst_ref=piece, send_sem=out_sem, recv_sem=in_sem,
            device_id=self.sibling, device_id_type=MESH,
        )

    def end(self):
        def sent(n, c, slot):
            odd = self.odd[c % 3]
            self.between(n, c, odd, self.ds.at[slot], self.dr.at[slot]).wait_send()
            self.between(n, c, 1 - odd, self.es.at[slot], self.er.at[slot]).wait_send()

        def came(n, c, slot):
            odd = self.odd[c % 3]
            self.between(n, c, odd, self.ds.at[slot], self.dr.at[slot]).wait_recv()
            self.between(n, c, 1 - odd, self.es.at[slot], self.er.at[slot]).wait_recv()

        def act(n):
            for c in range(6):
                sent(n, c, c)
                came(1 - n, c, c)

        self.each(act)
        pl.when(self.core == 1)(lambda: sent(2, 1, 6))
        pl.when(self.core == 0)(lambda: came(2, 1, 6))
        for copy in self.keep():
            copy.wait()


def front_kernel(
    x_ref, wq, wk, wv, v0, v1, v2, v3, v4, v5, v6, v7, v8, wi, wu, wo,
    a_ref, qo_ref, kvo_ref, ot_ref, lse_ref, w_ref, w_i, w_u, w_o, vec_ref, bi_ref, xo_ref,
    q_ref, kv_ref, small, small_o, o_ref, qt, top, total,
    own_sem, a_out, a_in, b_out, b_in, p_out, p_in, qs, qr, ks, kr, fs, fr, os, om, own, *rest,
):
    sems, lines = rest[:8], rest[8:]
    turn = Turn()
    y, z, xl, core, half = turn.y, turn.z, turn.xl, turn.core, turn.half
    fetch = Fetch(turn, (wi, wu, wo), (w_i, w_u, w_o), own, sems)
    across, sibling = fetch.across, fetch.sibling
    barrier = pltpu.get_barrier_semaphore()
    greet(barrier, across)
    greet(barrier, sibling)
    greet(barrier, fetch.beside[2])

    def hello(k, carry):
        greet(barrier, turn.partner(k, 16))
        return carry

    lax.fori_loop(1, 16, hello, 0)

    @pl.when(jnp.logical_not(turn.stays))
    def _():
        greet(barrier, turn.partner(0, 16))
        greet(barrier, fetch.beside[0])
        greet(barrier, fetch.beside[1])

    rows = pl.multiple_of(half * HALF, HALF)
    quarter = GROUP // 2

    def share(i, of, odd, who):
        return w_ref.at[i, pl.ds(pl.multiple_of(of * HALF + odd * GROUP + who * quarter, quarter), quarter)]

    mine = [
        pltpu.make_async_copy(w, w_ref.at[i, pl.ds(rows, HALF)], own_sem.at[i]) for i, w in enumerate((wq, wk, wv))
    ]
    for copy in mine:
        copy.start()
    fetch.own_rows()
    vectors = (v0, v1, v2, v3, v4, v5, v6, v7, v8)
    loads = [pltpu.make_async_copy(v, line, own_sem.at[3 + i]) for i, (v, line) in enumerate(zip(vectors, lines))]
    for copy in loads:
        copy.start()
    for copy in loads:
        copy.wait()
    small[...] = jnp.zeros_like(small)
    for i in range(8):
        small[i : i + 1, :] = lines[i][...].astype(F32).reshape(1, HALF)
    for i in range(4):
        small[8 + i : 9 + i, :] = lines[8][i * HALF : (i + 1) * HALF].astype(F32).reshape(1, HALF)
    pl.semaphore_wait(barrier, 18 + 3 * lax.rem(xl + core, 2))
    send(small, small_o, a_out.at[3], a_in.at[3], across)
    for i in (1, 2, 0):
        odd = 1 - fetch.odd[2] if i == 2 else fetch.odd[i]
        src = (wq, wk, wv)[i].at[pl.ds(pl.multiple_of(odd * GROUP + core * quarter, quarter), quarter)]
        send(src, share(i, half, odd, core), a_out.at[i], a_in.at[i], across)
    finish(small_o, small_o, a_out.at[3], a_in.at[3], across)
    near, far = small[...], small_o[...]
    ahead = jnp.where(half == 0, near, far)
    behind = jnp.where(half == 0, far, near)
    vec_ref[:, :HALF] = ahead[:8]
    vec_ref[:, HALF:] = behind[:8]
    for i in range(4):
        bi_ref[:, i * HALF : (i + 1) * HALF] = ahead[8 + i : 9 + i]
        bi_ref[:, 1536 + i * HALF : 1536 + (i + 1) * HALF] = behind[8 + i : 9 + i]
    def spread(k):
        src = kv_ref.at[turn.ahead(k, 16)[1]]
        if isinstance(k, int) and k == 0:
            turn.first(16, src, kvo_ref.at[y, z, xl], ks, kr)
        else:
            turn.push(k, 16, src, kvo_ref.at[y, z, xl], ks, kr)

    send(x_ref, xo_ref, a_out.at[4], a_in.at[4], sibling)
    x = x_ref[...]
    for i in (1, 2, 0):
        piece = share(i, 1 - half, fetch.odd[i], core)
        finish(piece, piece, a_out.at[i], a_in.at[i], across)
        send(piece, piece, p_out.at[i], p_in.at[i], fetch.beside[i])
        send(piece, piece, b_out.at[i], b_in.at[i], sibling)
    for c in range(6):
        fetch.issue(c)
    for i in (1, 2, 0):
        piece = share(i, 1 - half, 1 - fetch.odd[i], core)
        finish(piece, piece, p_out.at[i], p_in.at[i], fetch.beside[i])
        send(piece, piece, b_out.at[3 + i], b_in.at[3 + i], sibling)
    done = {}
    for i in (1, 2, 0):
        for n, odd in ((i, fetch.odd[i]), (3 + i, 1 - fetch.odd[i])):
            piece = share(i, 1 - half, odd, 1 - core)
            finish(piece, piece, b_out.at[n], b_in.at[n], sibling)
        mine[i].wait()
        done[i] = nn(x, w_ref[i])
        if i == 2:
            keys = done[1].astype(BF)
            values = (done[2] + vec_ref[1:2, :]).astype(BF)
            for g in range(4):
                cut = slice(g * GROUP, (g + 1) * GROUP)
                kv_ref[g] = jnp.concatenate([keys[:, cut], values[:, cut]], axis=1)
            for k in range(WINDOW):
                spread(k)
    pad = jnp.zeros((ROWS, 64), BF)
    query = (done[0] + vec_ref[0:1, :]).astype(BF) * BF(0.125)
    for g in range(4):
        q_ref[g] = jnp.concatenate([query[:, g * GROUP : (g + 1) * GROUP], pad], axis=1)
    turn.mates(q_ref, qo_ref, qs, qr)

    def onward(k):
        i, j = turn.behind(k, 16)
        piece = kvo_ref.at[i, j, core]
        send(piece, piece, fs.at[k], fr.at[k], sibling)

    turn.mates_end(qo_ref, qs, qr)
    turn.end_first(16, kvo_ref.at[y, z, core], ks, kr)
    onward(0)
    for h in range(3):
        qt[h] = turned(stack_head(qo_ref, h))
    top[...] = jnp.full_like(top, -jnp.inf)
    total[...] = jnp.zeros_like(total)
    ot_ref[...] = jnp.zeros_like(ot_ref)

    def work(k):
        i, j = turn.behind(k, 16)
        piece = kvo_ref.at[i, j, 1 - core]
        finish(piece, piece, fs.at[k], fr.at[k], sibling)
        kv = load_chunk(kvo_ref, (i, j))
        for h in range(3):
            scores = nn(kv[:, h * HD : (h + 1) * HD], qt[h])
            old = top[h]
            new = jnp.maximum(old, jnp.max(scores, axis=0, keepdims=True))
            shrink = jnp.exp(old - new)
            weights = jnp.exp(scores - new)
            total[h] = total[h] * shrink + jnp.sum(weights, axis=0, keepdims=True)
            mixed = tn(kv[:, GROUP + h * HD : GROUP + (h + 1) * HD], weights.astype(BF))
            ot_ref[h] = ot_ref[h] * shrink + mixed
            top[h] = new

    def relay(k, carry):
        i, j = turn.behind(k, 16)
        turn.end(k, 16, kvo_ref.at[i, j, core], ks, kr)
        pl.when(k + WINDOW - 1 < 16)(lambda: spread(k + WINDOW - 1))
        onward(k)
        work(k - 1)

        for c in range(6):
            pl.when(k == c + 10)(functools.partial(fetch.step_x, c))
        return carry

    lax.fori_loop(1, 16, relay, 0)
    work(15)
    heads = []
    for h in range(3):
        lse_ref[h] = top[h] + jnp.log(total[h])
        normal = ot_ref[h] / total[h]
        ot_ref[h] = normal
        heads.append(normal.T.astype(BF))
    heads.append(jnp.zeros((512, 64), BF))
    out = jnp.concatenate(heads, axis=1)
    for i in range(4):
        o_ref[i] = out[i * ROWS : (i + 1) * ROWS]
    turn.mates(o_ref, a_ref, os, om)
    for c in range(6):
        fetch.step_y(c)
    turn.mates_end(a_ref, os, om)
    finish(xo_ref, xo_ref, a_out.at[4], a_in.at[4], sibling)
    fetch.end()


def front(*arrays):
    return pl.pallas_call(
        front_kernel,
        name="front",
        cost_estimate=cost(70),
        out_shape=(
            shape(4, ROWS, 256), shape(4, ROWS, 256), shape(4, 4, 2, ROWS, HALF),
            shape(3, HD, 512, dtype=F32), shape(3, 1, 512, dtype=F32),
            shape(3, D, D), shape(D, FF), shape(FF, D), shape(D, D), shape(8, D, dtype=F32), shape(1, FF, dtype=F32),
            shape(ROWS, D),
        ),
        in_specs=[VM, ANY, ANY, ANY] + [ANY] * 9 + [ANY] * 3,
        out_specs=(VM,) * 12,
        scratch_shapes=[
            pltpu.VMEM((4, ROWS, 256), BF), pltpu.VMEM((4, ROWS, HALF), BF),
            pltpu.VMEM((16, HALF), F32), pltpu.VMEM((16, HALF), F32),
            pltpu.VMEM((4, ROWS, 256), BF),
            pltpu.VMEM((3, HD, 512), BF), pltpu.VMEM((3, 1, 512), F32), pltpu.VMEM((3, 1, 512), F32),
            DMA((12,)), DMA((5,)), DMA((5,)), DMA((6,)), DMA((6,)), DMA((3,)), DMA((3,)),
            DMA((4,)), DMA((4,)), DMA((16,)), DMA((16,)), DMA((16,)), DMA((16,)), DMA((4,)), DMA((4,)), DMA((3,)),
        ] + [DMA((7,))] * 8 + [pltpu.VMEM((HALF,), BF)] * 8 + [pltpu.VMEM((1536,), BF)],
        compiler_params=remote(1),
    )(arrays[0], *map(hbm, arrays[1:]))


def norm(hidden):
    centred = hidden - jnp.mean(hidden, axis=-1, keepdims=True)
    inverse = lax.rsqrt(jnp.mean(centred * centred, axis=-1, keepdims=True) + EPS)
    return centred * inverse, inverse


def norm_back(scaled, normal, inverse):
    centre = jnp.mean(scaled, axis=-1, keepdims=True)
    along = jnp.mean(scaled * normal, axis=-1, keepdims=True)
    return inverse * (scaled - centre - normal * along)


def column(value):
    return jnp.sum(value, axis=0, keepdims=True)


def block_kernel(
    x_ref, ct_ref, a_ref, w_i, w_u, w_o, vec_ref, bi_ref,
    out_ref, dh1_ref, da_ref, af_ref, yb_ref, g_ref, df_ref, du_ref, dz_ref, vg_ref,
    af_o, yb_o, g_o, df_o, du_o, dz_o, slope, da_out, outs, ins, p_out, p_in,
):
    turn = Turn()
    turn.hello(4, (turn.sibling(),))
    passed = ((af_ref, af_o), (yb_ref, yb_o), (g_ref, g_o), (df_ref, df_o), (du_ref, du_o), (dz_ref, dz_o))

    def pass_on(n):
        send(*passed[n], p_out.at[n], p_in.at[n], turn.sibling())

    b_output, first_gain, first_shift = vec_ref[2:3, :], vec_ref[3:4, :], vec_ref[4:5, :]
    b_outer, second_gain, second_shift = vec_ref[5:6, :], vec_ref[6:7, :], vec_ref[7:8, :]
    mixed = jnp.concatenate([a_ref[g][:, :GROUP] for g in range(4)], axis=1)
    af_ref[...] = mixed
    hidden = x_ref[...].astype(F32) + nn(mixed, w_o[...]) + b_output
    normal1, inverse1 = norm(hidden)
    normed = normal1 * first_gain + first_shift
    low = normed.astype(BF)
    yb_ref[...] = low
    turn.ready(4, 1)
    pass_on(0)
    pass_on(1)
    second_in = normed + b_outer
    for j in range(4):
        cut = slice(j * D, (j + 1) * D)
        inner = nn(low, w_i[:, cut]) + bi_ref[:, cut]
        cdf = 0.5 * (1.0 + lax.erf(inner * (0.5**0.5)))
        active = (inner * cdf).astype(BF)
        slope[:, cut] = cdf + inner * jnp.exp(inner * inner * -0.5) * 0.3989422804014327
        g_ref[:, cut] = active
        second_in = second_in + nn(active, w_u[cut, :])
    pass_on(2)
    normal2, inverse2 = norm(second_in)
    out_ref[...] = (normal2 * second_gain + second_shift).astype(BF)
    upper = ct_ref[...].astype(F32)


    def note(row, value):
        for h in range(2):
            vg_ref[h, row : row + 1, :] = value[:, h * HALF : (h + 1) * HALF]

    vg_ref[...] = jnp.zeros_like(vg_ref)
    note(6, column(upper * normal2))
    note(7, column(upper))
    dh2 = norm_back(upper * second_gain, normal2, inverse2)
    df = dh2.astype(BF)
    df_ref[...] = df
    pass_on(3)
    note(5, column(df.astype(F32)))
    dy1 = dh2
    for j in range(4):
        cut = slice(j * D, (j + 1) * D)
        du = (slope[:, cut] * nt(df, w_u[cut, :])).astype(BF)
        du_ref[:, cut] = du
        sums = column(du.astype(F32))
        for i in range(2):
            n = 2 * j + i
            vg_ref[n // 4, 8 + n % 4 : 9 + n % 4, :] = sums[:, i * HALF : (i + 1) * HALF]
        dy1 = dy1 + nt(du, w_i[:, cut])
    pass_on(4)
    note(3, column(dy1 * normal1))
    note(4, column(dy1))
    dh1 = norm_back(dy1 * first_gain, normal1, inverse1)
    dh1_ref[...] = dh1
    dz = dh1.astype(BF)
    dz_ref[...] = dz
    pass_on(5)
    note(2, column(dz.astype(F32)))
    da = nt(dz, w_o[...]).astype(BF)
    pad = jnp.zeros((ROWS, 64), BF)
    for g in range(4):
        da_out[g] = jnp.concatenate([da[:, g * GROUP : (g + 1) * GROUP], pad], axis=1)
    turn.mates(da_out, da_ref, outs, ins)
    turn.mates_end(da_ref, outs, ins)
    for n, (src, got) in enumerate(passed):
        finish(src, got, p_out.at[n], p_in.at[n], turn.sibling())


def block(*arrays):
    return pl.pallas_call(
        block_kernel,
        name="block",
        cost_estimate=cost(12),
        out_shape=(
            shape(ROWS, D), shape(ROWS, D, dtype=F32), shape(4, ROWS, 256), shape(ROWS, D), shape(ROWS, D),
            shape(ROWS, FF), shape(ROWS, D), shape(ROWS, FF), shape(ROWS, D),
            shape(2, 16, HALF, dtype=F32), shape(ROWS, D), shape(ROWS, D), shape(ROWS, FF), shape(ROWS, D),
            shape(ROWS, FF), shape(ROWS, D),
        ),
        in_specs=[VM] * 8,
        out_specs=(VM,) * 16,
        scratch_shapes=[
            pltpu.VMEM((ROWS, FF), F32), pltpu.VMEM((4, ROWS, 256), BF), DMA((4,)), DMA((4,)), DMA((6,)), DMA((6,)),
        ],
        compiler_params=remote(2),
    )(arrays[0], arrays[1], *map(vm, arrays[2:]))


EARLY = (0, 3)
LATE = (3, 1)


def back_kernel(
    q_ref, kv_ref, da_ref, ot_ref, lse_ref, x, x_o, yb, yb_o, g, g_o, a, a_o, df, df_o, du, du_o, dz, dz_o,
    dh1_ref, w_ref, vg_in,
    grad_ref, out, vo,
    rows_q, qt, rows_d, dt, delta, acc, dkv, other, dq, dqo, home, low, low_o, vg,
    g0, g1, g2, r0, r1, r2, s0, s1, s2, t0, t1, t2, rv, sv, tv, uv,
    fs, fr, ks, kr, qs, qr, ls, lr, a_out, a_in, b_out, b_in, c_out, c_in, d_out, d_in, e_out, e_in,
):
    turn = Turn()
    y, z, xl, core, half = turn.y, turn.z, turn.xl, turn.core, turn.half
    x_at = half * 2 + xl
    sibling = turn.sibling()
    barrier = pltpu.get_barrier_semaphore()

    def at(x_to, y_to, z_to):
        return device(y_to, z_to, lax.rem(x_to, 2), core, lax.div(x_to, 2))

    def along_x(k):
        return at(wrap(x_at + k, 4), y, z)

    def at_yz(k):
        i, j = pair(k)
        return at(x_at, wrap(y + i, 4), wrap(z + j, 4))

    def at_xz(k):
        i, j = pair(k)
        return at(wrap(x_at + i, 4), y, wrap(z + j, 4))

    def at_xy(k):
        i, j = pair(k)
        return at(wrap(x_at + i, 4), wrap(y + j, 4), z)

    def hello_yz(k, carry):
        greet(barrier, at_yz(k))
        return carry

    def hello_x(k, carry):
        i = lax.div(k - 1, 3) + 1
        j = lax.rem(k - 1, 3) + 1
        greet(barrier, at_xz(i * 4 + j))
        greet(barrier, at_xy(i * 4 + j))
        return carry

    def hello_row(k, carry):
        greet(barrier, along_x(k))
        return carry

    def hello_turn(k, carry):
        greet(barrier, turn.partner(k, 16))
        return carry

    lax.fori_loop(1, 16, hello_yz, 0)
    lax.fori_loop(1, 10, hello_x, 0)
    lax.fori_loop(1, 4, hello_row, 0)
    greet(barrier, sibling)

    @pl.when(jnp.logical_not(turn.stays))
    def _():
        lax.fori_loop(0, 16, hello_turn, 0)

    for h in range(3):
        rows = stack_head(q_ref, h)
        rows_q[h] = rows
        qt[h] = turned(rows)
        rows = stack_head(da_ref, h)
        rows_d[h] = rows
        flipped = rows.astype(F32).T
        dt[h] = flipped.astype(BF)
        delta[h] = jnp.sum(flipped * ot_ref[h], axis=0, keepdims=True)
    acc[...] = jnp.zeros_like(acc)

    def put(slab, f, m, value):
        blocks = value.astype(BF).reshape(4, 2, 48, HALF)
        if slab == 1:
            g1[f, :, m] = blocks
        else:
            (g0 if slab == 0 else g2)[f, m] = blocks

    def right(ref, second, start):
        cols = pl.ds(pl.multiple_of(start + core * HALF, HALF), HALF)
        return jnp.concatenate([ref[:, cols], second[:, cols]], axis=0)

    def left(ref, second, start):
        return jnp.concatenate([ref[:, start : start + HALF], second[:, start : start + HALF]], axis=0)

    outer = right(df, df_o, 0)
    attn = right(dz, dz_o, 0)
    for f in range(2):
        for m in range(4):
            put(*((1, f, m) if m < 3 else (0, f, 0)), tn(left(g, g_o, f * 1536 + m * HALF), outer))
        rows = left(yb, yb_o, f * HALF)
        for m in range(4):
            put(*((2, f, m) if m < 3 else (0, f, 1)), tn(rows, right(du, du_o, m * D)))
        put(0, f, 2, tn(left(a, a_o, f * HALF), attn))
    pl.semaphore_wait(barrier, 37 + 16 * lax.rem(xl + core, 2))

    def first(part):
        m, n = part
        late = 0 if part is EARLY else 4

        def one(k, carry):
            e = wrap(x_at + k, 4)
            send(
                g1.at[:, wrap(y + k, 4), pl.ds(m, n)], r1.at[k - 1, :, pl.ds(m, n)],
                a_out.at[late + 1, k], a_in.at[late + 1, k], at_yz(k * 4),
            )
            send(
                g2.at[:, pl.ds(m, n), wrap(z + k, 4)], r2.at[k - 1, :, pl.ds(m, n)],
                a_out.at[late + 2, k], a_in.at[late + 2, k], at_yz(k),
            )
            send(
                g0.at[lax.div(e, 2), pl.ds(m, n), :, lax.rem(e, 2)], r0.at[k - 1, pl.ds(m, n)],
                a_out.at[late, k], a_in.at[late, k], along_x(k),
            )
            return carry

        lax.fori_loop(1, 4, one, 0)

    first(EARLY)

    def work(k):
        i, j = turn.ahead(k, 16)
        kv = load_chunk(kv_ref, (i, j))
        keys, values = [], []
        for h in range(3):
            key = kv[:, h * HD : (h + 1) * HD]
            value = kv[:, GROUP + h * HD : GROUP + (h + 1) * HD]
            probs = jnp.exp(nn(key, qt[h]) - lse_ref[h])
            slopes = (probs * (nn(value, dt[h]) - delta[h])).astype(BF)
            keys.append(nn(slopes, rows_q[h]).astype(BF))
            values.append(nn(probs.astype(BF), rows_d[h]).astype(BF))
            acc[h] += tn(key, slopes)
        dkv[i, j] = jnp.concatenate(keys + values, axis=1).reshape(2, ROWS, HALF)
        send(dkv.at[i, j, 1 - core], other.at[i, j], fs.at[k], fr.at[k], sibling)

    def join(k):
        i, j = turn.ahead(k, 16)
        finish(other.at[i, j], other.at[i, j], fs.at[k], fr.at[k], sibling)
        other[i, j] = (dkv[i, j, core].astype(F32) + other[i, j].astype(F32)).astype(BF)

    def relay(k):
        join(k)
        turn.push(k, 16, other.at[turn.ahead(k, 16)], home.at[y, z], ks, kr)

    work(0)
    work(1)
    join(0)
    turn.first(16, other.at[y, z], home.at[y, z], ks, kr)

    def step(k, carry):
        work(k)
        relay(k - 1)
        return carry

    lax.fori_loop(2, 16, step, 0)
    relay(15)
    heads = [(acc[h] * 0.125).T.astype(BF) for h in range(3)]
    heads.append(jnp.zeros((512, 64), BF))
    turned_back = jnp.concatenate(heads, axis=1)
    for i in range(4):
        dq[i] = turned_back[i * ROWS : (i + 1) * ROWS]
    turn.mates(dq, dqo, qs, qr)

    here = device(y, z, xl, core, half)

    def second(part):
        m, n = part
        late = 0 if part is EARLY else 4

        def add(slab, own, got, to, count, where):
            for k in range(1, 4):
                piece = got.at[k - 1, pl.ds(m, n)] if slab == 0 else got.at[k - 1, :, pl.ds(m, n)]
                finish(piece, piece, a_out.at[late + slab, k], a_in.at[late + slab, k], here)

            def one(i, carry):
                p = where(i)
                total = own(p).astype(F32)
                for k in range(3):
                    total = total + got[(k,) + p].astype(F32)
                to[p] = total.astype(BF)
                return carry

            lax.fori_loop(0, count, one, 0)

        def push(slab, src, got, k, where):
            @pl.when(k > 0)
            def _():
                send(src, got.at[k], b_out.at[slab, k], b_in.at[slab, k], where)

        def spot(i):
            return lax.div(i, 2 * n), m + lax.rem(lax.div(i, 2), n), lax.rem(i, 2)

        add(1, lambda p: g1[p[0], y, p[1], p[2]], r1, s1, 4 * n, spot)

        def push1(i, carry):
            e, to = wrap(x_at + lax.div(i, n), 4), m + lax.rem(i, n)
            k = lax.div(i, n) * 4 + wrap(to - z, 4)
            push(1, s1.at[lax.div(e, 2), to, lax.rem(e, 2)], t1, k, at(e, y, to))
            return carry

        lax.fori_loop(0, 4 * n, push1, 0)
        add(2, lambda p: g2[p[0], p[1], z, p[2]], r2, s2, 4 * n, spot)

        def push2(i, carry):
            e, to = wrap(x_at + lax.div(i, n), 4), m + lax.rem(i, n)
            k = lax.div(i, n) * 4 + wrap(to - y, 4)
            push(2, s2.at[lax.div(e, 2), to, lax.rem(e, 2)], t2, k, at(e, to, z))
            return carry

        lax.fori_loop(0, 4 * n, push2, 0)
        add(
            0, lambda p: g0[half, p[0], p[1], xl], r0, s0, 4 * n,
            lambda i: (m + lax.div(i, 4), lax.rem(i, 4)),
        )

        def push0(i, carry):
            e, to = wrap(z + lax.div(i, n), 4), m + lax.rem(i, n)
            k = wrap(to - y, 4) * 4 + lax.div(i, n)
            push(0, s0.at[to, e], t0, k, at(x_at, to, e))
            return carry

        lax.fori_loop(0, 4 * n, push0, 0)

    turn.mates_end(dqo, qs, qr)
    turn.end_first(16, home.at[y, z], ks, kr)

    def done(k, carry):
        turn.end(k, 16, home.at[turn.behind(k, 16)], ks, kr)
        return carry

    lax.fori_loop(1, 16, done, 0)
    low[0] = jnp.concatenate([dqo[i][:, :GROUP] for i in range(4)], axis=1)
    sums = []
    for i in range(4):
        total = home[0, i].astype(F32)
        for k in range(1, 4):
            total = total + home[k, i].astype(F32)
        sums.append(total.astype(BF))
    low[1] = jnp.concatenate([v[:, :GROUP] for v in sums], axis=1)
    low[2] = jnp.concatenate([v[:, GROUP:] for v in sums], axis=1)
    send(low, low_o, ls, lr, sibling)
    second(EARLY)
    finish(low, low_o, ls, lr, sibling)
    cols = pl.ds(pl.multiple_of(core * HALF, HALF), HALF)
    both_low = [jnp.concatenate([low[i, :, cols], low_o[i, :, cols]], axis=0) for i in range(3)]
    for f in range(2):
        rows = left(x, x_o, f * HALF)
        for i, slab in enumerate((2, 1, 0)):
            put(slab, f, 3, tn(rows, both_low[i]))
    first(LATE)
    grad = dh1_ref[...]
    for i in range(3):
        grad = grad + nt(low[i], w_ref[i])
    grad_ref[...] = grad
    vg[...] = vg_in[...]
    for row, i in ((0, 0), (1, 2)):
        value = column(low[i].astype(F32))
        for f in range(2):
            vg[f, row : row + 1, :] = value[:, f * HALF : (f + 1) * HALF]

    def first3(k, carry):
        src = vg.at[lax.div(wrap(x_at + k, 4), 2)]
        send(src, rv.at[k - 1], a_out.at[3, k], a_in.at[3, k], along_x(k))
        return carry

    lax.fori_loop(1, 4, first3, 0)

    def third(part):
        early = part is EARLY

        def whole(own, got, slab):
            def wait(k, carry):
                arrived(got.at[k], b_in.at[slab, k], here)
                return carry

            lax.fori_loop(1, 16, wait, 0)

            def one(k, total):
                return total + got[k].astype(F32)

            out[core, slab, y, z, xl] = lax.fori_loop(1, 16, one, own.astype(F32)).astype(BF)

        def spread(slab, count, where):
            mine = out.at[core, slab, y, z, xl]

            def one(k, carry):
                send(mine, mine, c_out.at[slab, k], c_in.at[slab, k], where(k))
                return carry

            lax.fori_loop(1, count, one, 0)

        @pl.when(z < 3 if early else z == 3)
        def _():
            whole(s1[half, z, xl], t1, 1)
            spread(1, 8, lambda k: device(y, wrap(z + lax.div(k, 2), 4), wrap(xl + lax.rem(k, 2), 2), core, half))

        @pl.when(y < 3 if early else y == 3)
        def _():
            whole(s2[half, y, xl], t2, 2)
            spread(2, 8, lambda k: device(wrap(y + lax.div(k, 2), 4), z, wrap(xl + lax.rem(k, 2), 2), core, half))
            whole(s0[y, z], t0, 0)
            spread(0, 16, at_yz)

    def fourth(part):
        m, n = part
        late = 0 if part is EARLY else 3

        def wait(slab, piece, k):
            @pl.when(k > 0)
            def _():
                arrived(piece, c_in.at[slab, k], here)

        def got1(i, carry):
            zz, xx = m + lax.div(i, 2), lax.rem(i, 2)
            wait(1, out.at[core, 1, y, zz, xx], wrap(z - zz, 4) * 2 + wrap(xl - xx, 2))
            return carry

        lax.fori_loop(0, 2 * n, got1, 0)

        def push1(k, carry):
            mine = out.at[core, 1, y, pl.ds(m, n)]
            send(mine, mine, d_out.at[late + 1, k], d_in.at[late + 1, k], at_yz(k * 4))
            return carry

        lax.fori_loop(1, 4, push1, 0)

        def got2(i, carry):
            yy, xx = m + lax.div(i, 2), lax.rem(i, 2)
            wait(2, out.at[core, 2, yy, z, xx], wrap(y - yy, 4) * 2 + wrap(xl - xx, 2))
            return carry

        lax.fori_loop(0, 2 * n, got2, 0)

        def push2(k, carry):
            mine = out.at[core, 2, pl.ds(m, n), z]
            send(mine, mine, d_out.at[late + 2, k], d_in.at[late + 2, k], at_yz(k))
            return carry

        lax.fori_loop(1, 4, push2, 0)

        def got0(i, carry):
            yy, zz = m + lax.div(i, 4), lax.rem(i, 4)
            wait(0, out.at[core, 0, yy, zz, xl], wrap(y - yy, 4) * 4 + wrap(z - zz, 4))
            return carry

        lax.fori_loop(0, 4 * n, got0, 0)
        mine0 = out.at[core, 0, pl.ds(m, n), :, xl]
        send(mine0, mine0, d_out.at[late, 1], d_in.at[late, 1], device(y, z, 1 - xl, core, half))

    def own_part(slab, who, part):
        m, n = part
        return out.at[who, 1, :, pl.ds(m, n)] if slab == 1 else out.at[who, slab, pl.ds(m, n)]

    def last(part):
        m, n = part
        late = 0 if part is EARLY else 3

        def got1(k, carry):
            piece = out.at[core, 1, wrap(y - k, 4), pl.ds(m, n)]
            finish(piece, piece, d_out.at[late + 1, k], d_in.at[late + 1, k], here)
            return carry

        def got2(k, carry):
            piece = out.at[core, 2, pl.ds(m, n), wrap(z - k, 4)]
            finish(piece, piece, d_out.at[late + 2, k], d_in.at[late + 2, k], here)
            return carry

        def onward(slab):
            piece = own_part(slab, core, part)
            send(piece, piece, e_out.at[late + slab], e_in.at[late + slab], sibling)

        lax.fori_loop(1, 4, got1, 0)
        onward(1)
        lax.fori_loop(1, 4, got2, 0)
        onward(2)
        piece0 = out.at[core, 0, pl.ds(m, n), :, 1 - xl]
        finish(piece0, piece0, d_out.at[late, 1], d_in.at[late, 1], here)
        onward(0)

    third(EARLY)
    for k in range(1, 4):
        finish(rv.at[k - 1], rv.at[k - 1], a_out.at[3, k], a_in.at[3, k], here)
    part_sum = vg[half] + rv[0] + rv[1] + rv[2]
    sv[...] = part_sum.astype(BF)

    def second3(k, carry):
        send(sv, tv.at[k], b_out.at[3, k], b_in.at[3, k], at_yz(k))
        return carry

    lax.fori_loop(1, 16, second3, 0)
    second(LATE)
    fourth(EARLY)
    third(LATE)

    def done3(k, total):
        finish(tv.at[k], tv.at[k], b_out.at[3, k], b_in.at[3, k], here)
        return total + tv[k].astype(F32)

    vo[...] = lax.fori_loop(1, 16, done3, part_sum)
    send(vo, uv, e_out.at[6], e_in.at[6], sibling)
    fourth(LATE)
    last(EARLY)
    last(LATE)
    for late, part in ((0, EARLY), (3, LATE)):
        for slab in range(3):
            piece = own_part(slab, 1 - core, part)
            finish(piece, piece, e_out.at[late + slab], e_in.at[late + slab], here)
    for slab, count, own, got in ((1, 8, s1, t1), (2, 8, s2, t2), (0, 16, s0, t0)):
        mine = out.at[core, slab, y, z, xl]

        def gone2(k, carry):
            left_here(got.at[k], b_out.at[slab, k], here)
            return carry

        def gone3(k, carry):
            left_here(mine, c_out.at[slab, k], here)
            return carry

        lax.fori_loop(1, 16, gone2, 0)
        lax.fori_loop(1, count, gone3, 0)
    finish(uv, uv, e_out.at[6], e_in.at[6], here)
    vo[...] = vo[...] + uv[...]


def back(*arrays):
    blk = (48, HALF)
    scratch = [
        ((3, 512, HD), BF), ((3, HD, 512), BF), ((3, 512, HD), BF), ((3, HD, 512), BF), ((3, 1, 512), F32),
        ((3, HD, 512), F32), ((4, 4, 2, ROWS, HALF), BF), ((4, 4, ROWS, HALF), BF),
        ((4, ROWS, 256), BF), ((4, ROWS, 256), BF), ((4, 4, ROWS, HALF), BF), ((3, ROWS, D), BF), ((3, ROWS, D), BF),
        ((2, 16, HALF), F32),
        ((2, 4, 4, 2, *blk), BF), ((2, 4, 4, 2, *blk), BF), ((2, 4, 4, 2, *blk), BF),
        ((3, 4, 4, *blk), BF), ((3, 2, 4, 2, *blk), BF), ((3, 2, 4, 2, *blk), BF),
        ((4, 4, *blk), BF), ((2, 4, 2, *blk), BF), ((2, 4, 2, *blk), BF),
        ((16, *blk), BF), ((16, *blk), BF), ((16, *blk), BF),
        ((3, 16, HALF), F32), ((16, HALF), BF), ((16, 16, HALF), BF), ((16, HALF), F32),
    ]
    return pl.pallas_call(
        back_kernel,
        name="back",
        cost_estimate=cost(100),
        out_shape=(
            shape(ROWS, D, dtype=F32), shape(2, 3, 4, 4, 2, *blk), shape(16, HALF, dtype=F32),
        ),
        in_specs=[VM] * 22,
        out_specs=(VM,) * 3,
        scratch_shapes=[pltpu.VMEM(*v) for v in scratch] + [
            DMA((16,)), DMA((16,)), DMA((16,)), DMA((16,)), DMA((4,)), DMA((4,)), DMA, DMA,
            DMA((7, 4)), DMA((7, 4)), DMA((4, 16)), DMA((4, 16)), DMA((3, 16)), DMA((3, 16)),
            DMA((6, 4)), DMA((6, 4)), DMA((7,)), DMA((7,)),
        ],
        compiler_params=pltpu.CompilerParams(
            collective_id=3, has_side_effects=True, vmem_limit_bytes=29 << 20
        ),
    )(*map(vm, arrays))


def spell_kernel(full, vo, layer, grad, *refs):
    q_ref, k_ref, v_ref, o_ref, i_ref, u_ref, layer_ref, grad_ref = refs[:8]
    lines, (stage, sems, direct) = refs[8:17], refs[17:]
    straight = [
        pltpu.make_async_copy(layer, layer_ref, direct.at[0]), pltpu.make_async_copy(grad, grad_ref, direct.at[1])
    ]
    for copy in straight:
        copy.start()
    for i in range(8):
        lines[i][...] = vo[i : i + 1, :].reshape(HALF)
    lines[8][...] = jnp.concatenate([vo[8 + i : 9 + i, :] for i in range(4)], axis=1).reshape(1536)

    def copies(n):
        slot = stage.at[n % 2]
        rows = slice(n * 48, (n + 1) * 48)
        made = [
            pltpu.make_async_copy(slot.at[m], ref.at[rows], sems.at[n % 2, m])
            for m, ref in enumerate((q_ref, k_ref, v_ref, o_ref))
        ]
        for m in range(4):
            made.append(pltpu.make_async_copy(
                slot.at[4 + m], i_ref.at[rows, m * D : (m + 1) * D], sems.at[n % 2, 4 + m]
            ))
            made.append(pltpu.make_async_copy(
                slot.at[8 + m], u_ref.at[m * HALF + n * 48 : m * HALF + (n + 1) * 48], sems.at[n % 2, 8 + m]
            ))
        return made

    for n in range(8):
        if n >= 2:
            for copy in copies(n - 2):
                copy.wait()
        i, xl = n // 2, n % 2
        for c in range(2):
            cols = slice(c * HALF, (c + 1) * HALF)
            units = [(2, 3), (1, 3), (0, 3), (0, 2), (2, 0), (2, 1), (2, 2), (0, 1), (1, 0), (1, 1), (1, 2), (0, 0)]
            for m, (slab, unit) in enumerate(units):
                piece = full[c, 1, i, unit, xl] if slab == 1 else full[c, slab, unit, i, xl]
                stage[n % 2, m, :, cols] = piece.astype(F32)
        for copy in copies(n):
            copy.start()
    for n in (6, 7):
        for copy in copies(n):
            copy.wait()
    for copy in straight:
        copy.wait()


def spell(*arrays):
    return pl.pallas_call(
        spell_kernel,
        name="spell",
        out_shape=tuple(
            plain_shape(*dims, dtype=F32)
            for dims in ((HALF, D), (HALF, D), (HALF, D), (HALF, D), (HALF, FF), (1536, D))
        ) + (plain_shape(ROWS, D), plain_shape(ROWS, D, dtype=F32))
        + (plain_shape(HALF, dtype=F32),) * 8 + (plain_shape(1536, dtype=F32),),
        in_specs=[VM] * 4,
        out_specs=(ANY,) * 8 + (VM,) * 9,
        scratch_shapes=[pltpu.VMEM((2, 12, 48, D), F32), DMA((2, 12)), DMA((2,))],
        compiler_params=plain(),
        cost_estimate=cost(6),
    )(*map(vm, arrays))


def local(
    tokens, cotangent, w_query, w_key, w_value, w_output, b_query, b_value, b_output,
    first_gain, first_shift, w_inner, b_inner, w_outer, b_outer, second_gain, second_shift,
):
    x = tokens[0]
    mixed, q_all, kv_all, mixed_t, lse, w_qkv, w_i, w_u, w_o, vec, bi, x_o = front(
        x, w_query, w_key, w_value, b_query, b_value, b_output, first_gain, first_shift, b_outer, second_gain,
        second_shift, b_inner, w_inner, w_outer, w_output,
    )
    layer_out, dh1, da_all, a, yb, g, df, du, dz, vg, a_o, yb_o, g_o, df_o, du_o, dz_o = block(
        x, cotangent[0], mixed, w_i, w_u, w_o, vec, bi
    )
    tokens_grad, summed, vecs = back(
        q_all, kv_all, da_all, mixed_t, lse, x, x_o, yb, yb_o, g, g_o, a, a_o, df, df_o, du, du_o, dz, dz_o,
        dh1, w_qkv, vg,
    )
    gq, gk, gv, go, gi, gu, layer_out, tokens_grad, *vecs = spell(summed, vecs, layer_out, tokens_grad)
    return (
        layer_out[None], tokens_grad[None], gq, gk, gv, go,
        vecs[0], vecs[1], vecs[2], vecs[3], vecs[4], gi, vecs[8], gu, vecs[5], vecs[6], vecs[7],
    )


def solution(mesh):
    rows = P(("seq", "fsdp"), "ctx", None)
    mat = P("fsdp", None)
    vec = P("fsdp")
    return jax.shard_map(
        local,
        mesh=mesh,
        in_specs=(rows, rows, mat, mat, mat, mat, vec, vec, vec, vec, vec, mat, vec, mat, vec, vec, vec),
        out_specs=(rows, rows, mat, mat, mat, mat, vec, vec, vec, vec, vec, mat, vec, mat, vec, vec, vec),
        check_vma=False,
    )
```

```python
import functools

import jax
import jax.numpy as jnp
from jax import lax
from jax.experimental import pallas as pl
from jax.experimental.pallas import tpu as pltpu
from jax.sharding import PartitionSpec as P

AXES = ("ctx", "seq", "fsdp")
MESH = pl.DeviceIdType.MESH
BF = jnp.bfloat16
F32 = jnp.float32
D = 768
FF = 3072
HALF = 384
GROUP = 192
HD = 64
ROWS = 128
EPS = 1e-12
LIMIT = 12 << 20
VM = pl.BlockSpec(memory_space=pltpu.VMEM)
ANY = pl.BlockSpec(memory_space=pltpu.HBM)


def plain_shape(*dims, dtype=BF):
    return jax.ShapeDtypeStruct(dims, dtype)


def shape(*dims, dtype=BF):
    return pltpu.VMEM(dims, dtype)


def hbm(array):
    return pltpu.with_memory_space_constraint(array, pltpu.HBM)


def vm(array):
    return pltpu.with_memory_space_constraint(array, pltpu.VMEM)


def nn(left, right):
    return jnp.dot(left, right, preferred_element_type=F32)


def nt(left, right):
    return lax.dot_general(left, right, (((1,), (1,)), ((), ())), preferred_element_type=F32)


def tn(left, right):
    return lax.dot_general(left, right, (((0,), (0,)), ((), ())), preferred_element_type=F32)


def wrap(value, size):
    return lax.rem(value + size, size)


def place():
    ctx = lax.axis_index("ctx")
    y = lax.div(ctx, 8)
    z = lax.rem(lax.div(ctx, 2), 4)
    return y, z, lax.rem(ctx, 2), lax.axis_index("seq"), lax.axis_index("fsdp")


def device(y, z, xl, core, half):
    return ((y * 4 + z) * 2 + xl, core, half)


def send(src, dst, out_sem, in_sem, where):
    pltpu.make_async_remote_copy(
        src_ref=src, dst_ref=dst, send_sem=out_sem, recv_sem=in_sem,
        device_id=where, device_id_type=MESH,
    ).start()


def finish(src, dst, out_sem, in_sem, where):
    copy = pltpu.make_async_remote_copy(
        src_ref=src, dst_ref=dst, send_sem=out_sem, recv_sem=in_sem,
        device_id=where, device_id_type=MESH,
    )
    copy.wait_send()
    copy.wait_recv()


def arrived(got, in_sem, where):
    pltpu.make_async_remote_copy(
        src_ref=got, dst_ref=got, send_sem=in_sem, recv_sem=in_sem, device_id=where, device_id_type=MESH
    ).wait_recv()


def left_here(src, out_sem, where):
    pltpu.make_async_remote_copy(
        src_ref=src, dst_ref=src, send_sem=out_sem, recv_sem=out_sem, device_id=where, device_id_type=MESH
    ).wait_send()


def greet(barrier, where):
    pl.semaphore_signal(barrier, inc=1, device_id=where, device_id_type=MESH)


def pair(k):
    return lax.div(k, 4), lax.rem(k, 4)


class Turn:
    def __init__(self):
        self.y, self.z, self.xl, self.core, self.half = place()
        self.stays = self.xl == self.core

    def step(self, k, count):
        if count == 4:
            return 0, k
        return lax.rem(k + lax.div(k, 4), 4), lax.rem(k, 4)

    def partner(self, k, count):
        i, j = self.ahead(k, count)
        return device(i, j, self.core, self.xl, self.half)

    def ahead(self, k, count):
        i, j = self.step(k, count)
        return wrap(self.y + i, 4), wrap(self.z + j, 4)

    def behind(self, k, count):
        i, j = self.step(k, count)
        return wrap(self.y - i, 4), wrap(self.z - j, 4)

    def sibling(self):
        return device(self.y, self.z, self.xl, 1 - self.core, self.half)

    def hello(self, count, others=()):
        barrier = pltpu.get_barrier_semaphore()

        def one(k, carry):
            greet(barrier, self.partner(k, count))
            return carry

        lax.fori_loop(1, count, one, 0)
        for where in others:
            greet(barrier, where)

        @pl.when(jnp.logical_not(self.stays))
        def _():
            greet(barrier, self.partner(0, count))

    def ready(self, count, others=0):
        barrier = pltpu.get_barrier_semaphore()
        pl.semaphore_wait(barrier, count - 1 + others + lax.rem(self.xl + self.core, 2))

    def push(self, k, count, src, dst, outs, ins):
        send(src, dst, outs.at[k], ins.at[k], self.partner(k, count))

    def first(self, count, src, dst, outs, ins):
        @pl.when(self.stays)
        def _():
            pltpu.make_async_copy(src, dst, ins.at[0]).start()

        @pl.when(jnp.logical_not(self.stays))
        def _():
            self.push(0, count, src, dst, outs, ins)

    def start(self, count, src, dst, outs, ins):
        self.first(count, src(0), dst, outs, ins)

        def one(k, carry):
            self.push(k, count, src(k), dst, outs, ins)
            return carry

        lax.fori_loop(1, count, one, 0)

    def end(self, k, count, got, outs, ins):
        finish(got, got, outs.at[k], ins.at[k], self.partner(k, count))

    def end_first(self, count, got, outs, ins):
        @pl.when(self.stays)
        def _():
            pltpu.make_async_copy(got, got, ins.at[0]).wait()

        @pl.when(jnp.logical_not(self.stays))
        def _():
            self.end(0, count, got, outs, ins)

    def mates(self, src, dst, outs, ins, own=None):
        slot = dst.at[self.z] if own is None else dst.at[self.z, own]
        self.start(4, lambda k: src.at[self.ahead(k, 4)[1]], slot, outs, ins)

    def mates_end(self, dst, outs, ins):
        self.end_first(4, dst.at[self.z], outs, ins)

        def one(k, carry):
            self.end(k, 4, dst.at[self.behind(k, 4)[1]], outs, ins)
            return carry

        lax.fori_loop(1, 4, one, 0)


def cost(us):
    return pl.CostEstimate(flops=0, transcendentals=0, bytes_accessed=int(us * 3e6))


def remote(number):
    return pltpu.CompilerParams(collective_id=number, has_side_effects=True, vmem_limit_bytes=LIMIT)


def plain():
    return pltpu.CompilerParams(vmem_limit_bytes=LIMIT)


DMA = pltpu.SemaphoreType.DMA


CHUNK = 256


def load_chunk(ref, at):
    return ref[at].reshape(CHUNK, HALF)


def stack_head(ref, h):
    return jnp.concatenate([ref[i][:, h * HD : (h + 1) * HD] for i in range(4)], axis=0)


def turned(rows):
    return rows.astype(F32).T.astype(BF)


class Fetch:
    def __init__(self, turn, sources, fulls, own, sems):
        self.core, self.half = turn.core, turn.half
        y, z, xl = turn.y, turn.z, turn.xl
        self.odd = (lax.rem(y, 2), lax.rem(z, 2), xl)
        self.across = device(y, z, 1 - xl, turn.core, 1 - turn.half)
        self.beside = (
            device(y + 1 - 2 * self.odd[0], z, xl, turn.core, turn.half),
            device(y, z + 1 - 2 * self.odd[1], xl, turn.core, turn.half),
            device(y, z, 1 - xl, turn.core, turn.half),
        )
        self.sibling = turn.sibling()
        self.sources, self.fulls, self.own = sources, fulls, own
        self.sizes = (HALF, FF // 2, HALF)
        self.xs, self.xr, self.ys, self.yr, self.ds, self.dr, self.es, self.er = sems

    def rows(self, n, c, odd):
        size = self.sizes[n]
        if n == 2:
            return odd * (size // 2), size // 2
        return c * (size // 6) + odd * (size // 12), size // 12

    def piece(self, n, half, c, odd):
        start, size = self.rows(n, c, odd)
        return self.fulls[n].at[pl.ds(pl.multiple_of(half * self.sizes[n] + start, 32), size)]

    def each(self, act, flip=False):
        pl.when(self.core == (1 if flip else 0))(lambda: act(0))
        pl.when(self.core == (0 if flip else 1))(lambda: act(1))

    def keep(self):
        for n in range(3):
            rows = self.fulls[n].at[pl.ds(pl.multiple_of(self.half * self.sizes[n], 32), self.sizes[n])]
            yield pltpu.make_async_copy(self.sources[n], rows, self.own.at[n])

    def give(self, n, c, slot):
        odd = 1 - self.odd[2] if c % 2 else self.odd[1]
        start, size = self.rows(n, c, odd)
        src = self.sources[n].at[pl.ds(pl.multiple_of(start, 32), size)]
        send(src, self.piece(n, self.half, c, odd), self.xs.at[slot], self.xr.at[slot], self.across)

    def own_rows(self):
        for copy in self.keep():
            copy.start()

    def issue(self, c):
        if c == 0:
            pl.when(self.core == 1)(lambda: self.give(2, 1, 6))
        if c < 6:
            self.each(lambda n: self.give(n, c, c))

    def pass_x(self, n, c, slot):
        piece = self.piece(n, 1 - self.half, c, self.odd[1 + c % 2])
        finish(piece, piece, self.xs.at[slot], self.xr.at[slot], self.across)
        send(piece, piece, self.ys.at[slot], self.yr.at[slot], self.beside[1 + c % 2])
        send(piece, piece, self.ds.at[slot], self.dr.at[slot], self.sibling)

    def pass_y(self, n, c, slot):
        piece = self.piece(n, 1 - self.half, c, 1 - self.odd[1 + c % 2])
        finish(piece, piece, self.ys.at[slot], self.yr.at[slot], self.beside[1 + c % 2])
        send(piece, piece, self.es.at[slot], self.er.at[slot], self.sibling)

    def step_x(self, c):
        self.each(lambda n: self.pass_x(n, c, c))
        if c == 0:
            pl.when(self.core == 1)(lambda: self.pass_x(2, 1, 6))

    def step_y(self, c):
        self.each(lambda n: self.pass_y(n, c, c))
        if c == 0:
            pl.when(self.core == 1)(lambda: self.pass_y(2, 1, 6))

    def between(self, n, c, odd, out_sem, in_sem):
        piece = self.piece(n, 1 - self.half, c, odd)
        return pltpu.make_async_remote_copy(
            src_ref=piece, dst_ref=piece, send_sem=out_sem, recv_sem=in_sem,
            device_id=self.sibling, device_id_type=MESH,
        )

    def end(self):
        def sent(n, c, slot):
            odd = self.odd[1 + c % 2]
            self.between(n, c, odd, self.ds.at[slot], self.dr.at[slot]).wait_send()
            self.between(n, c, 1 - odd, self.es.at[slot], self.er.at[slot]).wait_send()

        def came(n, c, slot):
            odd = self.odd[1 + c % 2]
            self.between(n, c, odd, self.ds.at[slot], self.dr.at[slot]).wait_recv()
            self.between(n, c, 1 - odd, self.es.at[slot], self.er.at[slot]).wait_recv()

        def act(n):
            for c in range(6):
                sent(n, c, c)
                came(1 - n, c, c)

        self.each(act)
        pl.when(self.core == 1)(lambda: sent(2, 1, 6))
        pl.when(self.core == 0)(lambda: came(2, 1, 6))
        for copy in self.keep():
            copy.wait()


def front_kernel(
    x_ref, wq, wk, wv, v0, v1, v2, v3, v4, v5, v6, v7, v8, wi, wu, wo,
    a_ref, qo_ref, kvo_ref, ot_ref, lse_ref, w_ref, w_i, w_u, w_o, vec_ref, bi_ref, xo_ref,
    q_ref, kv_ref, small, small_o, o_ref, qt, top, total,
    own_sem, a_out, a_in, b_out, b_in, p_out, p_in, qs, qr, ks, kr, ms, mr, fs, fr, os, om, own, *rest,
):
    sems, lines = rest[:8], rest[8:]
    turn = Turn()
    y, z, xl, core, half = turn.y, turn.z, turn.xl, turn.core, turn.half
    fetch = Fetch(turn, (wi, wu, wo), (w_i, w_u, w_o), own, sems)
    across, sibling = fetch.across, fetch.sibling
    barrier = pltpu.get_barrier_semaphore()
    greet(barrier, across)
    greet(barrier, sibling)
    greet(barrier, fetch.beside[2])

    def mate(dy):
        return device(wrap(y + dy, 4), z, xl, core, half)

    for k in range(1, 4):
        greet(barrier, mate(k))
        greet(barrier, turn.partner(k, 4))

    @pl.when(jnp.logical_not(turn.stays))
    def _():
        greet(barrier, turn.partner(0, 4))
        greet(barrier, fetch.beside[1])

    rows = pl.multiple_of(half * HALF, HALF)
    quarter = GROUP // 2

    def share(i, of, odd, who):
        return w_ref.at[i, pl.ds(pl.multiple_of(of * HALF + odd * GROUP + who * quarter, quarter), quarter)]

    mine = [
        pltpu.make_async_copy(w, w_ref.at[i, pl.ds(rows, HALF)], own_sem.at[i]) for i, w in enumerate((wq, wk, wv))
    ]
    for copy in mine:
        copy.start()
    fetch.own_rows()
    vectors = (v0, v1, v2, v3, v4, v5, v6, v7, v8)
    loads = [pltpu.make_async_copy(v, line, own_sem.at[3 + i]) for i, (v, line) in enumerate(zip(vectors, lines))]
    for copy in loads:
        copy.start()
    for copy in loads:
        copy.wait()
    small[...] = jnp.zeros_like(small)
    for i in range(8):
        small[i : i + 1, :] = lines[i][...].astype(F32).reshape(1, HALF)
    for i in range(4):
        small[8 + i : 9 + i, :] = lines[8][i * HALF : (i + 1) * HALF].astype(F32).reshape(1, HALF)
    pl.semaphore_wait(barrier, 9 + 2 * lax.rem(xl + core, 2))
    send(small, small_o, a_out.at[3], a_in.at[3], across)
    for i in (1, 2, 0):
        odd = 1 - fetch.odd[2] if i == 2 else fetch.odd[i]
        src = (wq, wk, wv)[i].at[pl.ds(pl.multiple_of(odd * GROUP + core * quarter, quarter), quarter)]
        send(src, share(i, half, odd, core), a_out.at[i], a_in.at[i], across)
    finish(small_o, small_o, a_out.at[3], a_in.at[3], across)
    near, far = small[...], small_o[...]
    ahead = jnp.where(half == 0, near, far)
    behind = jnp.where(half == 0, far, near)
    vec_ref[:, :HALF] = ahead[:8]
    vec_ref[:, HALF:] = behind[:8]
    for i in range(4):
        bi_ref[:, i * HALF : (i + 1) * HALF] = ahead[8 + i : 9 + i]
        bi_ref[:, 1536 + i * HALF : 1536 + (i + 1) * HALF] = behind[8 + i : 9 + i]
    send(x_ref, xo_ref, a_out.at[4], a_in.at[4], sibling)
    x = x_ref[...]
    for i in (1, 2, 0):
        piece = share(i, 1 - half, fetch.odd[i], core)
        finish(piece, piece, a_out.at[i], a_in.at[i], across)
        send(piece, piece, p_out.at[i], p_in.at[i], fetch.beside[i])
        send(piece, piece, b_out.at[i], b_in.at[i], sibling)
    fetch.issue(0)
    fetch.issue(1)
    for i in (1, 2, 0):
        piece = share(i, 1 - half, 1 - fetch.odd[i], core)
        finish(piece, piece, p_out.at[i], p_in.at[i], fetch.beside[i])
        send(piece, piece, b_out.at[3 + i], b_in.at[3 + i], sibling)
    done = {}
    for i in (1, 2, 0):
        for n, odd in ((i, fetch.odd[i]), (3 + i, 1 - fetch.odd[i])):
            piece = share(i, 1 - half, odd, 1 - core)
            finish(piece, piece, b_out.at[n], b_in.at[n], sibling)
        mine[i].wait()
        done[i] = nn(x, w_ref[i])
        if i == 2:
            keys = done[1].astype(BF)
            values = (done[2] + vec_ref[1:2, :]).astype(BF)
            for g in range(4):
                cut = slice(g * GROUP, (g + 1) * GROUP)
                kv_ref[g] = jnp.concatenate([keys[:, cut], values[:, cut]], axis=1)
            turn.mates(kv_ref, kvo_ref.at[y], ks, kr, own=xl)
    fetch.issue(2)
    fetch.issue(3)
    pad = jnp.zeros((ROWS, 64), BF)
    query = (done[0] + vec_ref[0:1, :]).astype(BF) * BF(0.125)
    for g in range(4):
        q_ref[g] = jnp.concatenate([query[:, g * GROUP : (g + 1) * GROUP], pad], axis=1)
    turn.mates(q_ref, qo_ref, qs, qr)

    def spot(t):
        g, k = lax.div(t, 4), lax.rem(t, 4)
        dy = g + lax.div(g, 2) * (5 - 2 * g)
        return dy, k, wrap(y - dy, 4), wrap(z - k, 4)

    def onward(t):
        dy, k, i, j = spot(t)
        piece = kvo_ref.at[i, j, core]
        send(piece, piece, fs.at[t], fr.at[t], sibling)

    def hand(piece, dy, n):
        send(piece, piece, ms.at[n], mr.at[n], mate(dy))

    turn.end_first(4, kvo_ref.at[y, z, core], ks, kr)
    hand(kvo_ref.at[y, z, core], 1, 4)
    hand(kvo_ref.at[y, z, core], 3, 12)
    onward(0)
    def work(k):
        _, _, i, j = spot(k)
        piece = kvo_ref.at[i, j, 1 - core]
        finish(piece, piece, fs.at[k], fr.at[k], sibling)
        kv = load_chunk(kvo_ref, (i, j))
        for h in range(3):
            scores = nn(kv[:, h * HD : (h + 1) * HD], qt[h])
            old = top[h]
            new = jnp.maximum(old, jnp.max(scores, axis=0, keepdims=True))
            shrink = jnp.exp(old - new)
            weights = jnp.exp(scores - new)
            total[h] = total[h] * shrink + jnp.sum(weights, axis=0, keepdims=True)
            mixed = tn(kv[:, GROUP + h * HD : GROUP + (h + 1) * HD], weights.astype(BF))
            ot_ref[h] = ot_ref[h] * shrink + mixed
            top[h] = new

    def arrive(k):
        dy, n, i, j = spot(k)
        piece = kvo_ref.at[i, j, core]

        @pl.when(dy == 0)
        def _():
            turn.end(n, 4, piece, ks, kr)
            hand(piece, 1, 4 + n)
            hand(piece, 3, 12 + n)

        @pl.when(dy > 0)
        def _():
            finish(piece, piece, ms.at[dy * 4 + n], mr.at[dy * 4 + n], mate(1))

        pl.when((dy == 1) & (lax.rem(n, 2) == 0))(lambda: hand(piece, 1, 8 + n))
        pl.when((dy == 3) & (lax.rem(n, 2) == 1))(lambda: hand(piece, 3, 8 + n))
        onward(k)

    for k in range(1, 4):
        arrive(k)
    fetch.issue(4)
    fetch.issue(5)
    turn.mates_end(qo_ref, qs, qr)
    for h in range(3):
        qt[h] = turned(stack_head(qo_ref, h))
    top[...] = jnp.full_like(top, -jnp.inf)
    total[...] = jnp.zeros_like(total)
    ot_ref[...] = jnp.zeros_like(ot_ref)

    for k in range(3):
        work(k)

    def relay(k, carry):
        arrive(k)
        work(k - 1)

        for c, when in enumerate((4, 5, 7, 8, 11, 12)):
            pl.when(k == when)(functools.partial(fetch.step_x, c))
        return carry

    lax.fori_loop(4, 16, relay, 0)
    work(15)
    heads = []
    for h in range(3):
        lse_ref[h] = top[h] + jnp.log(total[h])
        normal = ot_ref[h] / total[h]
        ot_ref[h] = normal
        heads.append(normal.T.astype(BF))
    heads.append(jnp.zeros((512, 64), BF))
    out = jnp.concatenate(heads, axis=1)
    for i in range(4):
        o_ref[i] = out[i * ROWS : (i + 1) * ROWS]
    turn.mates(o_ref, a_ref, os, om)
    for c in range(6):
        fetch.step_y(c)
    turn.mates_end(a_ref, os, om)
    finish(xo_ref, xo_ref, a_out.at[4], a_in.at[4], sibling)
    fetch.end()


def front(*arrays):
    return pl.pallas_call(
        front_kernel,
        name="front",
        cost_estimate=cost(70),
        out_shape=(
            shape(4, ROWS, 256), shape(4, ROWS, 256), shape(4, 4, 2, ROWS, HALF),
            shape(3, HD, 512, dtype=F32), shape(3, 1, 512, dtype=F32),
            shape(3, D, D), shape(D, FF), shape(FF, D), shape(D, D), shape(8, D, dtype=F32), shape(1, FF, dtype=F32),
            shape(ROWS, D),
        ),
        in_specs=[VM, ANY, ANY, ANY] + [ANY] * 9 + [ANY] * 3,
        out_specs=(VM,) * 12,
        scratch_shapes=[
            pltpu.VMEM((4, ROWS, 256), BF), pltpu.VMEM((4, ROWS, HALF), BF),
            pltpu.VMEM((16, HALF), F32), pltpu.VMEM((16, HALF), F32),
            pltpu.VMEM((4, ROWS, 256), BF),
            pltpu.VMEM((3, HD, 512), BF), pltpu.VMEM((3, 1, 512), F32), pltpu.VMEM((3, 1, 512), F32),
            DMA((12,)), DMA((5,)), DMA((5,)), DMA((6,)), DMA((6,)), DMA((3,)), DMA((3,)),
            DMA((4,)), DMA((4,)), DMA((4,)), DMA((4,)), DMA((16,)), DMA((16,)), DMA((16,)), DMA((16,)),
            DMA((4,)), DMA((4,)), DMA((3,)),
        ] + [DMA((7,))] * 8 + [pltpu.VMEM((HALF,), BF)] * 8 + [pltpu.VMEM((1536,), BF)],
        compiler_params=remote(1),
    )(arrays[0], *map(hbm, arrays[1:]))


def norm(hidden):
    centred = hidden - jnp.mean(hidden, axis=-1, keepdims=True)
    inverse = lax.rsqrt(jnp.mean(centred * centred, axis=-1, keepdims=True) + EPS)
    return centred * inverse, inverse


def norm_back(scaled, normal, inverse):
    centre = jnp.mean(scaled, axis=-1, keepdims=True)
    along = jnp.mean(scaled * normal, axis=-1, keepdims=True)
    return inverse * (scaled - centre - normal * along)


def column(value):
    return jnp.sum(value, axis=0, keepdims=True)


def block_part(
    turn, ready, x_ref, ct_ref, a_ref, w_i, w_u, w_o, vec_ref, bi_ref,
    out_ref, dh1_ref, da_ref, af_ref, yb_ref, g_ref, df_ref, du_ref, dz_ref, vg_ref,
    af_o, yb_o, g_o, df_o, du_o, dz_o, slope, da_out, outs, ins, p_out, p_in,
):
    passed = ((af_ref, af_o), (yb_ref, yb_o), (g_ref, g_o), (df_ref, df_o), (du_ref, du_o), (dz_ref, dz_o))

    def pass_on(n):
        send(*passed[n], p_out.at[n], p_in.at[n], turn.sibling())

    b_output, first_gain, first_shift = vec_ref[2:3, :], vec_ref[3:4, :], vec_ref[4:5, :]
    b_outer, second_gain, second_shift = vec_ref[5:6, :], vec_ref[6:7, :], vec_ref[7:8, :]
    mixed = jnp.concatenate([a_ref[g][:, :GROUP] for g in range(4)], axis=1)
    af_ref[...] = mixed
    hidden = x_ref[...].astype(F32) + nn(mixed, w_o[...]) + b_output
    normal1, inverse1 = norm(hidden)
    normed = normal1 * first_gain + first_shift
    low = normed.astype(BF)
    yb_ref[...] = low
    ready()
    pass_on(0)
    pass_on(1)
    second_in = normed + b_outer
    for j in range(4):
        cut = slice(j * D, (j + 1) * D)
        inner = nn(low, w_i[:, cut]) + bi_ref[:, cut]
        cdf = 0.5 * (1.0 + lax.erf(inner * (0.5**0.5)))
        active = (inner * cdf).astype(BF)
        slope[:, cut] = cdf + inner * jnp.exp(inner * inner * -0.5) * 0.3989422804014327
        g_ref[:, cut] = active
        second_in = second_in + nn(active, w_u[cut, :])
    pass_on(2)
    normal2, inverse2 = norm(second_in)
    out_ref[...] = (normal2 * second_gain + second_shift).astype(BF)
    upper = ct_ref[...].astype(F32)


    def note(row, value):
        for h in range(2):
            vg_ref[h, row : row + 1, :] = value[:, h * HALF : (h + 1) * HALF]

    vg_ref[...] = jnp.zeros_like(vg_ref)
    note(6, column(upper * normal2))
    note(7, column(upper))
    dh2 = norm_back(upper * second_gain, normal2, inverse2)
    df = dh2.astype(BF)
    df_ref[...] = df
    pass_on(3)
    note(5, column(df.astype(F32)))
    dy1 = dh2
    for j in range(4):
        cut = slice(j * D, (j + 1) * D)
        du = (slope[:, cut] * nt(df, w_u[cut, :])).astype(BF)
        du_ref[:, cut] = du
        sums = column(du.astype(F32))
        for i in range(2):
            n = 2 * j + i
            vg_ref[n // 4, 8 + n % 4 : 9 + n % 4, :] = sums[:, i * HALF : (i + 1) * HALF]
        dy1 = dy1 + nt(du, w_i[:, cut])
    pass_on(4)
    note(3, column(dy1 * normal1))
    note(4, column(dy1))
    dh1 = norm_back(dy1 * first_gain, normal1, inverse1)
    dh1_ref[...] = dh1
    dz = dh1.astype(BF)
    dz_ref[...] = dz
    pass_on(5)
    note(2, column(dz.astype(F32)))
    da = nt(dz, w_o[...]).astype(BF)
    pad = jnp.zeros((ROWS, 64), BF)
    for g in range(4):
        da_out[g] = jnp.concatenate([da[:, g * GROUP : (g + 1) * GROUP], pad], axis=1)
    turn.mates(da_out, da_ref, outs, ins)
    for n, (src, got) in enumerate(passed):
        finish(src, got, p_out.at[n], p_in.at[n], turn.sibling())


EARLY = (0, 3)
LATE = (3, 1)


def back_part(
    turn, da_end, q_ref, kv_ref, da_ref, ot_ref, lse_ref, x, x_o, yb, yb_o, g, g_o, a, a_o, df, df_o, du, du_o, dz, dz_o,
    dh1_ref, w_ref, vg_in,
    grad_ref, out, vo,
    rows_q, qt, rows_d, dt, delta, acc, dkv, other, dq, dqo, home, low, low_o, vg,
    g0, g1, g2, r0, r1, r2, s0, s1, s2, t0, t1, t2, rv, sv, tv, uv,
    fs, fr, ks, kr, qs, qr, ls, lr, a_out, a_in, b_out, b_in, c_out, c_in, d_out, d_in, e_out, e_in,
):
    y, z, xl, core, half = turn.y, turn.z, turn.xl, turn.core, turn.half
    x_at = half * 2 + xl
    sibling = turn.sibling()
    barrier = pltpu.get_barrier_semaphore()

    def at(x_to, y_to, z_to):
        return device(y_to, z_to, lax.rem(x_to, 2), core, lax.div(x_to, 2))

    def along_x(k):
        return at(wrap(x_at + k, 4), y, z)

    def at_yz(k):
        i, j = pair(k)
        return at(x_at, wrap(y + i, 4), wrap(z + j, 4))

    def at_xz(k):
        i, j = pair(k)
        return at(wrap(x_at + i, 4), y, wrap(z + j, 4))

    def at_xy(k):
        i, j = pair(k)
        return at(wrap(x_at + i, 4), wrap(y + j, 4), z)

    def hello_yz(k, carry):
        greet(barrier, at_yz(k))
        return carry

    def hello_x(k, carry):
        i = lax.div(k - 1, 3) + 1
        j = lax.rem(k - 1, 3) + 1
        greet(barrier, at_xz(i * 4 + j))
        greet(barrier, at_xy(i * 4 + j))
        return carry

    def hello_row(k, carry):
        greet(barrier, along_x(k))
        return carry

    def hello_turn(k, carry):
        greet(barrier, turn.partner(k, 16))
        return carry

    def hello_all():
        lax.fori_loop(1, 16, hello_yz, 0)
        lax.fori_loop(1, 10, hello_x, 0)
        lax.fori_loop(1, 4, hello_row, 0)
        greet(barrier, sibling)

        @pl.when(jnp.logical_not(turn.stays))
        def _():
            lax.fori_loop(0, 16, hello_turn, 0)

    def ready():
        pl.semaphore_wait(barrier, 37 + 16 * lax.rem(xl + core, 2))

    def run():
        def put(slab, f, m, value):
            blocks = value.astype(BF).reshape(4, 2, 48, HALF)
            if slab == 1:
                g1[f, :, m] = blocks
            else:
                (g0 if slab == 0 else g2)[f, m] = blocks

        def right(ref, second, start):
            cols = pl.ds(pl.multiple_of(start + core * HALF, HALF), HALF)
            return jnp.concatenate([ref[:, cols], second[:, cols]], axis=0)

        def left(ref, second, start):
            return jnp.concatenate([ref[:, start : start + HALF], second[:, start : start + HALF]], axis=0)

        outer = right(df, df_o, 0)
        attn = right(dz, dz_o, 0)
        for f in range(2):
            for m in range(4):
                put(*((1, f, m) if m < 3 else (0, f, 0)), tn(left(g, g_o, f * 1536 + m * HALF), outer))
            rows = left(yb, yb_o, f * HALF)
            for m in range(4):
                put(*((2, f, m) if m < 3 else (0, f, 1)), tn(rows, right(du, du_o, m * D)))
            put(0, f, 2, tn(left(a, a_o, f * HALF), attn))

        def first(part):
            m, n = part
            late = 0 if part is EARLY else 4

            def one(k, carry):
                e = wrap(x_at + k, 4)
                send(
                    g1.at[:, wrap(y + k, 4), pl.ds(m, n)], r1.at[k - 1, :, pl.ds(m, n)],
                    a_out.at[late + 1, k], a_in.at[late + 1, k], at_yz(k * 4),
                )
                send(
                    g2.at[:, pl.ds(m, n), wrap(z + k, 4)], r2.at[k - 1, :, pl.ds(m, n)],
                    a_out.at[late + 2, k], a_in.at[late + 2, k], at_yz(k),
                )
                send(
                    g0.at[lax.div(e, 2), pl.ds(m, n), :, lax.rem(e, 2)], r0.at[k - 1, pl.ds(m, n)],
                    a_out.at[late, k], a_in.at[late, k], along_x(k),
                )
                return carry

            lax.fori_loop(1, 4, one, 0)

        first(EARLY)

        da_end()
        for h in range(3):
            rows = stack_head(q_ref, h)
            rows_q[h] = rows
            qt[h] = turned(rows)
            rows = stack_head(da_ref, h)
            rows_d[h] = rows
            flipped = rows.astype(F32).T
            dt[h] = flipped.astype(BF)
            delta[h] = jnp.sum(flipped * ot_ref[h], axis=0, keepdims=True)
        acc[...] = jnp.zeros_like(acc)

        def compute(k):
            i, j = turn.ahead(k, 16)
            kv = load_chunk(kv_ref, (i, j))
            keys, values = [], []
            for h in range(3):
                key = kv[:, h * HD : (h + 1) * HD]
                value = kv[:, GROUP + h * HD : GROUP + (h + 1) * HD]
                probs = jnp.exp(nn(key, qt[h]) - lse_ref[h])
                slopes = (probs * (nn(value, dt[h]) - delta[h])).astype(BF)
                keys.append(nn(slopes, rows_q[h]).astype(BF))
                values.append(nn(probs.astype(BF), rows_d[h]).astype(BF))
                acc[h] += tn(key, slopes)
            dkv[lax.rem(k, 4)] = jnp.concatenate(keys + values, axis=1).reshape(2, ROWS, HALF)

        def work(k):
            compute(k)
            pass_half(k)

        def pass_half(k):
            i, j = turn.ahead(k, 16)
            send(dkv.at[lax.rem(k, 4), 1 - core], other.at[i, j], fs.at[k], fr.at[k], sibling)

        def join(k):
            i, j = turn.ahead(k, 16)
            finish(other.at[i, j], other.at[i, j], fs.at[k], fr.at[k], sibling)
            other[i, j] = (dkv[lax.rem(k, 4), core].astype(F32) + other[i, j].astype(F32)).astype(BF)

        def relay(k):
            join(k)
            turn.push(k, 16, other.at[turn.ahead(k, 16)], home.at[y, z], ks, kr)

        for k in range(3):
            work(k)
        join(0)
        turn.first(16, other.at[y, z], home.at[y, z], ks, kr)

        def step(k, carry):
            work(k)
            relay(k - 2)
            return carry

        def finish_up(k, carry):
            relay(k)
            return carry

        lax.fori_loop(3, 16, step, 0)
        lax.fori_loop(14, 16, finish_up, 0)
        heads = [(acc[h] * 0.125).T.astype(BF) for h in range(3)]
        heads.append(jnp.zeros((512, 64), BF))
        turned_back = jnp.concatenate(heads, axis=1)
        for i in range(4):
            dq[i] = turned_back[i * ROWS : (i + 1) * ROWS]
        turn.mates(dq, dqo, qs, qr)

        here = device(y, z, xl, core, half)

        def second(part):
            m, n = part
            late = 0 if part is EARLY else 4

            def add(slab, own, got, to, count, where):
                for k in range(1, 4):
                    piece = got.at[k - 1, pl.ds(m, n)] if slab == 0 else got.at[k - 1, :, pl.ds(m, n)]
                    finish(piece, piece, a_out.at[late + slab, k], a_in.at[late + slab, k], here)

                def one(i, carry):
                    p = where(i)
                    total = own(p).astype(F32)
                    for k in range(3):
                        total = total + got[(k,) + p].astype(F32)
                    to[p] = total.astype(BF)
                    return carry

                lax.fori_loop(0, count, one, 0)

            def push(slab, src, got, k, where):
                @pl.when(k > 0)
                def _():
                    send(src, got.at[k], b_out.at[slab, k], b_in.at[slab, k], where)

            def spot(i):
                return lax.div(i, 2 * n), m + lax.rem(lax.div(i, 2), n), lax.rem(i, 2)

            add(1, lambda p: g1[p[0], y, p[1], p[2]], r1, s1, 4 * n, spot)

            def push1(i, carry):
                e, to = wrap(x_at + lax.div(i, n), 4), m + lax.rem(i, n)
                k = lax.div(i, n) * 4 + wrap(to - z, 4)
                push(1, s1.at[lax.div(e, 2), to, lax.rem(e, 2)], t1, k, at(e, y, to))
                return carry

            lax.fori_loop(0, 4 * n, push1, 0)
            add(2, lambda p: g2[p[0], p[1], z, p[2]], r2, s2, 4 * n, spot)

            def push2(i, carry):
                e, to = wrap(x_at + lax.div(i, n), 4), m + lax.rem(i, n)
                k = lax.div(i, n) * 4 + wrap(to - y, 4)
                push(2, s2.at[lax.div(e, 2), to, lax.rem(e, 2)], t2, k, at(e, to, z))
                return carry

            lax.fori_loop(0, 4 * n, push2, 0)
            add(
                0, lambda p: g0[half, p[0], p[1], xl], r0, s0, 4 * n,
                lambda i: (m + lax.div(i, 4), lax.rem(i, 4)),
            )

            def push0(i, carry):
                e, to = wrap(z + lax.div(i, n), 4), m + lax.rem(i, n)
                k = wrap(to - y, 4) * 4 + lax.div(i, n)
                push(0, s0.at[to, e], t0, k, at(x_at, to, e))
                return carry

            lax.fori_loop(0, 4 * n, push0, 0)

        turn.mates_end(dqo, qs, qr)
        turn.end_first(16, home.at[y, z], ks, kr)

        def done(k, carry):
            turn.end(k, 16, home.at[turn.behind(k, 16)], ks, kr)
            return carry

        lax.fori_loop(1, 16, done, 0)
        low[0] = jnp.concatenate([dqo[i][:, :GROUP] for i in range(4)], axis=1)
        sums = []
        for i in range(4):
            total = home[0, i].astype(F32)
            for k in range(1, 4):
                total = total + home[k, i].astype(F32)
            sums.append(total.astype(BF))
        low[1] = jnp.concatenate([v[:, :GROUP] for v in sums], axis=1)
        low[2] = jnp.concatenate([v[:, GROUP:] for v in sums], axis=1)
        send(low, low_o, ls, lr, sibling)
        second(EARLY)
        finish(low, low_o, ls, lr, sibling)
        cols = pl.ds(pl.multiple_of(core * HALF, HALF), HALF)
        both_low = [jnp.concatenate([low[i, :, cols], low_o[i, :, cols]], axis=0) for i in range(3)]
        for f in range(2):
            rows = left(x, x_o, f * HALF)
            for i, slab in enumerate((2, 1, 0)):
                put(slab, f, 3, tn(rows, both_low[i]))
        first(LATE)
        grad = dh1_ref[...]
        for i in range(3):
            grad = grad + nt(low[i], w_ref[i])
        grad_ref[...] = grad
        vg[...] = vg_in[...]
        for row, i in ((0, 0), (1, 2)):
            value = column(low[i].astype(F32))
            for f in range(2):
                vg[f, row : row + 1, :] = value[:, f * HALF : (f + 1) * HALF]

        def first3(k, carry):
            src = vg.at[lax.div(wrap(x_at + k, 4), 2)]
            send(src, rv.at[k - 1], a_out.at[3, k], a_in.at[3, k], along_x(k))
            return carry

        lax.fori_loop(1, 4, first3, 0)

        def third(part):
            early = part is EARLY

            def whole(own, got, slab):
                def wait(k, carry):
                    arrived(got.at[k], b_in.at[slab, k], here)
                    return carry

                lax.fori_loop(1, 16, wait, 0)

                def one(k, total):
                    return total + got[k].astype(F32)

                out[core, slab, y, z, xl] = lax.fori_loop(1, 16, one, own.astype(F32)).astype(BF)

            def spread(slab, count, where):
                mine = out.at[core, slab, y, z, xl]

                def one(k, carry):
                    send(mine, mine, c_out.at[slab, k], c_in.at[slab, k], where(k))
                    return carry

                lax.fori_loop(1, count, one, 0)

            @pl.when(z < 3 if early else z == 3)
            def _():
                whole(s1[half, z, xl], t1, 1)
                spread(1, 8, lambda k: device(y, wrap(z + lax.div(k, 2), 4), wrap(xl + lax.rem(k, 2), 2), core, half))

            @pl.when(y < 3 if early else y == 3)
            def _():
                whole(s2[half, y, xl], t2, 2)
                spread(2, 8, lambda k: device(wrap(y + lax.div(k, 2), 4), z, wrap(xl + lax.rem(k, 2), 2), core, half))
                whole(s0[y, z], t0, 0)
                spread(0, 16, at_yz)

        def fourth(part):
            m, n = part
            late = 0 if part is EARLY else 3

            def wait(slab, piece, k):
                @pl.when(k > 0)
                def _():
                    arrived(piece, c_in.at[slab, k], here)

            def got1(i, carry):
                zz, xx = m + lax.div(i, 2), lax.rem(i, 2)
                wait(1, out.at[core, 1, y, zz, xx], wrap(z - zz, 4) * 2 + wrap(xl - xx, 2))
                return carry

            lax.fori_loop(0, 2 * n, got1, 0)

            def push1(k, carry):
                mine = out.at[core, 1, y, pl.ds(m, n)]
                send(mine, mine, d_out.at[late + 1, k], d_in.at[late + 1, k], at_yz(k * 4))
                return carry

            lax.fori_loop(1, 4, push1, 0)

            def got2(i, carry):
                yy, xx = m + lax.div(i, 2), lax.rem(i, 2)
                wait(2, out.at[core, 2, yy, z, xx], wrap(y - yy, 4) * 2 + wrap(xl - xx, 2))
                return carry

            lax.fori_loop(0, 2 * n, got2, 0)

            def push2(k, carry):
                mine = out.at[core, 2, pl.ds(m, n), z]
                send(mine, mine, d_out.at[late + 2, k], d_in.at[late + 2, k], at_yz(k))
                return carry

            lax.fori_loop(1, 4, push2, 0)

            def got0(i, carry):
                yy, zz = m + lax.div(i, 4), lax.rem(i, 4)
                wait(0, out.at[core, 0, yy, zz, xl], wrap(y - yy, 4) * 4 + wrap(z - zz, 4))
                return carry

            lax.fori_loop(0, 4 * n, got0, 0)
            mine0 = out.at[core, 0, pl.ds(m, n), :, xl]
            send(mine0, mine0, d_out.at[late, 1], d_in.at[late, 1], device(y, z, 1 - xl, core, half))

        def own_part(slab, who, part):
            m, n = part
            return out.at[who, 1, :, pl.ds(m, n)] if slab == 1 else out.at[who, slab, pl.ds(m, n)]

        def last(part):
            m, n = part
            late = 0 if part is EARLY else 3

            def got1(k, carry):
                piece = out.at[core, 1, wrap(y - k, 4), pl.ds(m, n)]
                finish(piece, piece, d_out.at[late + 1, k], d_in.at[late + 1, k], here)
                return carry

            def got2(k, carry):
                piece = out.at[core, 2, pl.ds(m, n), wrap(z - k, 4)]
                finish(piece, piece, d_out.at[late + 2, k], d_in.at[late + 2, k], here)
                return carry

            def onward(slab):
                piece = own_part(slab, core, part)
                send(piece, piece, e_out.at[late + slab], e_in.at[late + slab], sibling)

            lax.fori_loop(1, 4, got1, 0)
            onward(1)
            lax.fori_loop(1, 4, got2, 0)
            onward(2)
            piece0 = out.at[core, 0, pl.ds(m, n), :, 1 - xl]
            finish(piece0, piece0, d_out.at[late, 1], d_in.at[late, 1], here)
            onward(0)

        third(EARLY)
        for k in range(1, 4):
            finish(rv.at[k - 1], rv.at[k - 1], a_out.at[3, k], a_in.at[3, k], here)
        part_sum = vg[half] + rv[0] + rv[1] + rv[2]
        sv[...] = part_sum.astype(BF)

        def second3(k, carry):
            send(sv, tv.at[k], b_out.at[3, k], b_in.at[3, k], at_yz(k))
            return carry

        lax.fori_loop(1, 16, second3, 0)
        second(LATE)
        fourth(EARLY)
        third(LATE)

        def done3(k, total):
            finish(tv.at[k], tv.at[k], b_out.at[3, k], b_in.at[3, k], here)
            return total + tv[k].astype(F32)

        vo[...] = lax.fori_loop(1, 16, done3, part_sum)
        send(vo, uv, e_out.at[6], e_in.at[6], sibling)
        fourth(LATE)
        last(EARLY)
        last(LATE)
        for late, part in ((0, EARLY), (3, LATE)):
            for slab in range(3):
                piece = own_part(slab, 1 - core, part)
                finish(piece, piece, e_out.at[late + slab], e_in.at[late + slab], here)
        for slab, count, own, got in ((1, 8, s1, t1), (2, 8, s2, t2), (0, 16, s0, t0)):
            mine = out.at[core, slab, y, z, xl]

            def gone2(k, carry):
                left_here(got.at[k], b_out.at[slab, k], here)
                return carry

            def gone3(k, carry):
                left_here(mine, c_out.at[slab, k], here)
                return carry

            lax.fori_loop(1, 16, gone2, 0)
            lax.fori_loop(1, count, gone3, 0)
        finish(uv, uv, e_out.at[6], e_in.at[6], here)
        vo[...] = vo[...] + uv[...]

    return hello_all, ready, run


BLOCK_ACTS = ((ROWS, D), (ROWS, D), (ROWS, FF), (ROWS, D), (ROWS, FF), (ROWS, D))


def rest_kernel(
    x, ct, mixed, w_i, w_u, w_o, vec, bi, q, kv, ot, lse, x_o, w_qkv,
    layer_ref, grad_ref, out, vo,
    dh1, da, vg_in, a, yb, g, df, du, dz, a_o, yb_o, g_o, df_o, du_o, dz_o, slope, da_out, *more,
):
    (outs, ins, p_out, p_in), more = more[:4], more[4:]
    turn = Turn()
    hello_all, ready, run = back_part(
        turn, lambda: turn.mates_end(da, outs, ins), q, kv, da, ot, lse, x, x_o, yb, yb_o, g, g_o, a, a_o, df, df_o,
        du, du_o, dz, dz_o, dh1, w_qkv, vg_in, grad_ref, out, vo, *more,
    )
    hello_all()
    block_part(
        turn, ready, x, ct, mixed, w_i, w_u, w_o, vec, bi, layer_ref, dh1, da, a, yb, g, df, du, dz, vg_in,
        a_o, yb_o, g_o, df_o, du_o, dz_o, slope, da_out, outs, ins, p_out, p_in,
    )
    run()


def rest(*arrays):
    blk = (48, HALF)
    acts = [(v, BF) for v in BLOCK_ACTS]
    first = [((ROWS, D), F32), ((4, ROWS, 256), BF), ((2, 16, HALF), F32)] + acts + acts + [
        ((ROWS, FF), F32), ((4, ROWS, 256), BF),
    ]
    second = [
        ((3, 512, HD), BF), ((3, HD, 512), BF), ((3, 512, HD), BF), ((3, HD, 512), BF), ((3, 1, 512), F32),
        ((3, HD, 512), F32), ((4, 2, ROWS, HALF), BF), ((4, 4, ROWS, HALF), BF),
        ((4, ROWS, 256), BF), ((4, ROWS, 256), BF), ((4, 4, ROWS, HALF), BF), ((3, ROWS, D), BF), ((3, ROWS, D), BF),
        ((2, 16, HALF), F32),
        ((2, 4, 4, 2, *blk), BF), ((2, 4, 4, 2, *blk), BF), ((2, 4, 4, 2, *blk), BF),
        ((3, 4, 4, *blk), BF), ((3, 2, 4, 2, *blk), BF), ((3, 2, 4, 2, *blk), BF),
        ((4, 4, *blk), BF), ((2, 4, 2, *blk), BF), ((2, 4, 2, *blk), BF),
        ((16, *blk), BF), ((16, *blk), BF), ((16, *blk), BF),
        ((3, 16, HALF), F32), ((16, HALF), BF), ((16, 16, HALF), BF), ((16, HALF), F32),
    ]
    return pl.pallas_call(
        rest_kernel,
        name="rest",
        cost_estimate=cost(130),
        out_shape=(
            shape(ROWS, D), shape(ROWS, D, dtype=F32), shape(2, 3, 4, 4, 2, *blk), shape(16, HALF, dtype=F32),
        ),
        in_specs=[VM] * 14,
        out_specs=(VM,) * 4,
        scratch_shapes=[pltpu.VMEM(*v) for v in first] + [DMA((4,)), DMA((4,)), DMA((6,)), DMA((6,))]
        + [pltpu.VMEM(*v) for v in second] + [
            DMA((16,)), DMA((16,)), DMA((16,)), DMA((16,)), DMA((4,)), DMA((4,)), DMA, DMA,
            DMA((7, 4)), DMA((7, 4)), DMA((4, 16)), DMA((4, 16)), DMA((3, 16)), DMA((3, 16)),
            DMA((6, 4)), DMA((6, 4)), DMA((7,)), DMA((7,)),
        ],
        compiler_params=pltpu.CompilerParams(
            collective_id=3, has_side_effects=True, vmem_limit_bytes=34 << 20
        ),
    )(*map(vm, arrays))


def spell_kernel(full, vo, layer, grad, *refs):
    q_ref, k_ref, v_ref, o_ref, i_ref, u_ref, layer_ref, grad_ref = refs[:8]
    lines, (stage, sems, direct) = refs[8:17], refs[17:]
    straight = [
        pltpu.make_async_copy(layer, layer_ref, direct.at[0]), pltpu.make_async_copy(grad, grad_ref, direct.at[1])
    ]
    for copy in straight:
        copy.start()
    for i in range(8):
        lines[i][...] = vo[i : i + 1, :].reshape(HALF)
    lines[8][...] = jnp.concatenate([vo[8 + i : 9 + i, :] for i in range(4)], axis=1).reshape(1536)

    def copies(n):
        slot = stage.at[n % 2]
        rows = slice(n * 48, (n + 1) * 48)
        made = [
            pltpu.make_async_copy(slot.at[m], ref.at[rows], sems.at[n % 2, m])
            for m, ref in enumerate((q_ref, k_ref, v_ref, o_ref))
        ]
        for m in range(4):
            made.append(pltpu.make_async_copy(
                slot.at[4 + m], i_ref.at[rows, m * D : (m + 1) * D], sems.at[n % 2, 4 + m]
            ))
            made.append(pltpu.make_async_copy(
                slot.at[8 + m], u_ref.at[m * HALF + n * 48 : m * HALF + (n + 1) * 48], sems.at[n % 2, 8 + m]
            ))
        return made

    for n in range(8):
        if n >= 2:
            for copy in copies(n - 2):
                copy.wait()
        i, xl = n // 2, n % 2
        for c in range(2):
            cols = slice(c * HALF, (c + 1) * HALF)
            units = [(2, 3), (1, 3), (0, 3), (0, 2), (2, 0), (2, 1), (2, 2), (0, 1), (1, 0), (1, 1), (1, 2), (0, 0)]
            for m, (slab, unit) in enumerate(units):
                piece = full[c, 1, i, unit, xl] if slab == 1 else full[c, slab, unit, i, xl]
                stage[n % 2, m, :, cols] = piece.astype(F32)
        for copy in copies(n):
            copy.start()
    for n in (6, 7):
        for copy in copies(n):
            copy.wait()
    for copy in straight:
        copy.wait()


def spell(*arrays):
    return pl.pallas_call(
        spell_kernel,
        name="spell",
        out_shape=tuple(
            plain_shape(*dims, dtype=F32)
            for dims in ((HALF, D), (HALF, D), (HALF, D), (HALF, D), (HALF, FF), (1536, D))
        ) + (plain_shape(ROWS, D), plain_shape(ROWS, D, dtype=F32))
        + (plain_shape(HALF, dtype=F32),) * 8 + (plain_shape(1536, dtype=F32),),
        in_specs=[VM] * 4,
        out_specs=(ANY,) * 8 + (VM,) * 9,
        scratch_shapes=[pltpu.VMEM((2, 12, 48, D), F32), DMA((2, 12)), DMA((2,))],
        compiler_params=plain(),
        cost_estimate=cost(6),
    )(*map(vm, arrays))


def local(
    tokens, cotangent, w_query, w_key, w_value, w_output, b_query, b_value, b_output,
    first_gain, first_shift, w_inner, b_inner, w_outer, b_outer, second_gain, second_shift,
):
    x = tokens[0]
    mixed, q_all, kv_all, mixed_t, lse, w_qkv, w_i, w_u, w_o, vec, bi, x_o = front(
        x, w_query, w_key, w_value, b_query, b_value, b_output, first_gain, first_shift, b_outer, second_gain,
        second_shift, b_inner, w_inner, w_outer, w_output,
    )
    layer_out, tokens_grad, summed, vecs = rest(
        x, cotangent[0], mixed, w_i, w_u, w_o, vec, bi, q_all, kv_all, mixed_t, lse, x_o, w_qkv
    )
    gq, gk, gv, go, gi, gu, layer_out, tokens_grad, *vecs = spell(summed, vecs, layer_out, tokens_grad)
    return (
        layer_out[None], tokens_grad[None], gq, gk, gv, go,
        vecs[0], vecs[1], vecs[2], vecs[3], vecs[4], gi, vecs[8], gu, vecs[5], vecs[6], vecs[7],
    )


def solution(mesh):
    rows = P(("seq", "fsdp"), "ctx", None)
    mat = P("fsdp", None)
    vec = P("fsdp")
    return jax.shard_map(
        local,
        mesh=mesh,
        in_specs=(rows, rows, mat, mat, mat, mat, vec, vec, vec, vec, vec, mat, vec, mat, vec, vec, vec),
        out_specs=(rows, rows, mat, mat, mat, mat, vec, vec, vec, vec, vec, mat, vec, mat, vec, vec, vec),
        check_vma=False,
    )
```

```python
import functools

import jax
import jax.numpy as jnp
from jax import lax
from jax.experimental import pallas as pl
from jax.experimental.pallas import tpu as pltpu
from jax.sharding import PartitionSpec as P

AXES = ("ctx", "seq", "fsdp")
MESH = pl.DeviceIdType.MESH
BF = jnp.bfloat16
F32 = jnp.float32
D = 768
FF = 3072
HALF = 384
GROUP = 192
HD = 64
ROWS = 128
EPS = 1e-12
LIMIT = 12 << 20
VM = pl.BlockSpec(memory_space=pltpu.VMEM)
ANY = pl.BlockSpec(memory_space=pltpu.HBM)


def plain_shape(*dims, dtype=BF):
    return jax.ShapeDtypeStruct(dims, dtype)


def shape(*dims, dtype=BF):
    return pltpu.VMEM(dims, dtype)


def hbm(array):
    return pltpu.with_memory_space_constraint(array, pltpu.HBM)


def vm(array):
    return pltpu.with_memory_space_constraint(array, pltpu.VMEM)


def nn(left, right):
    return jnp.dot(left, right, preferred_element_type=F32)


def nt(left, right):
    return lax.dot_general(left, right, (((1,), (1,)), ((), ())), preferred_element_type=F32)


def tn(left, right):
    return lax.dot_general(left, right, (((0,), (0,)), ((), ())), preferred_element_type=F32)


def wrap(value, size):
    return lax.rem(value + size, size)


def place():
    ctx = lax.axis_index("ctx")
    y = lax.div(ctx, 8)
    z = lax.rem(lax.div(ctx, 2), 4)
    return y, z, lax.rem(ctx, 2), lax.axis_index("seq"), lax.axis_index("fsdp")


def device(y, z, xl, core, half):
    return ((y * 4 + z) * 2 + xl, core, half)


def send(src, dst, out_sem, in_sem, where):
    pltpu.make_async_remote_copy(
        src_ref=src, dst_ref=dst, send_sem=out_sem, recv_sem=in_sem,
        device_id=where, device_id_type=MESH,
    ).start()


def finish(src, dst, out_sem, in_sem, where):
    copy = pltpu.make_async_remote_copy(
        src_ref=src, dst_ref=dst, send_sem=out_sem, recv_sem=in_sem,
        device_id=where, device_id_type=MESH,
    )
    copy.wait_send()
    copy.wait_recv()


def arrived(got, in_sem, where):
    pltpu.make_async_remote_copy(
        src_ref=got, dst_ref=got, send_sem=in_sem, recv_sem=in_sem, device_id=where, device_id_type=MESH
    ).wait_recv()


def left_here(src, out_sem, where):
    pltpu.make_async_remote_copy(
        src_ref=src, dst_ref=src, send_sem=out_sem, recv_sem=out_sem, device_id=where, device_id_type=MESH
    ).wait_send()


def greet(barrier, where):
    pl.semaphore_signal(barrier, inc=1, device_id=where, device_id_type=MESH)


def pair(k):
    return lax.div(k, 4), lax.rem(k, 4)


class Turn:
    def __init__(self):
        self.y, self.z, self.xl, self.core, self.half = place()
        self.stays = self.xl == self.core

    def step(self, k, count):
        if count == 4:
            return 0, k
        return lax.rem(k + lax.div(k, 4), 4), lax.rem(k, 4)

    def partner(self, k, count):
        i, j = self.ahead(k, count)
        return device(i, j, self.core, self.xl, self.half)

    def ahead(self, k, count):
        i, j = self.step(k, count)
        return wrap(self.y + i, 4), wrap(self.z + j, 4)

    def behind(self, k, count):
        i, j = self.step(k, count)
        return wrap(self.y - i, 4), wrap(self.z - j, 4)

    def sibling(self):
        return device(self.y, self.z, self.xl, 1 - self.core, self.half)

    def hello(self, count, others=()):
        barrier = pltpu.get_barrier_semaphore()

        def one(k, carry):
            greet(barrier, self.partner(k, count))
            return carry

        lax.fori_loop(1, count, one, 0)
        for where in others:
            greet(barrier, where)

        @pl.when(jnp.logical_not(self.stays))
        def _():
            greet(barrier, self.partner(0, count))

    def ready(self, count, others=0):
        barrier = pltpu.get_barrier_semaphore()
        pl.semaphore_wait(barrier, count - 1 + others + lax.rem(self.xl + self.core, 2))

    def push(self, k, count, src, dst, outs, ins):
        send(src, dst, outs.at[k], ins.at[k], self.partner(k, count))

    def first(self, count, src, dst, outs, ins):
        @pl.when(self.stays)
        def _():
            pltpu.make_async_copy(src, dst, ins.at[0]).start()

        @pl.when(jnp.logical_not(self.stays))
        def _():
            self.push(0, count, src, dst, outs, ins)

    def start(self, count, src, dst, outs, ins):
        self.first(count, src(0), dst, outs, ins)

        def one(k, carry):
            self.push(k, count, src(k), dst, outs, ins)
            return carry

        lax.fori_loop(1, count, one, 0)

    def end(self, k, count, got, outs, ins):
        finish(got, got, outs.at[k], ins.at[k], self.partner(k, count))

    def end_first(self, count, got, outs, ins):
        @pl.when(self.stays)
        def _():
            pltpu.make_async_copy(got, got, ins.at[0]).wait()

        @pl.when(jnp.logical_not(self.stays))
        def _():
            self.end(0, count, got, outs, ins)

    def mates(self, src, dst, outs, ins, own=None):
        slot = dst.at[self.z] if own is None else dst.at[self.z, own]
        self.start(4, lambda k: src.at[self.ahead(k, 4)[1]], slot, outs, ins)

    def mates_end(self, dst, outs, ins):
        self.end_first(4, dst.at[self.z], outs, ins)

        def one(k, carry):
            self.end(k, 4, dst.at[self.behind(k, 4)[1]], outs, ins)
            return carry

        lax.fori_loop(1, 4, one, 0)


def cost(us):
    return pl.CostEstimate(flops=0, transcendentals=0, bytes_accessed=int(us * 3e6))


def remote(number):
    return pltpu.CompilerParams(collective_id=number, has_side_effects=True, vmem_limit_bytes=LIMIT)


def plain():
    return pltpu.CompilerParams(vmem_limit_bytes=LIMIT)


DMA = pltpu.SemaphoreType.DMA


CHUNK = 256


def load_chunk(ref, at):
    return ref[at].reshape(CHUNK, HALF)


def packed(heads):
    low = ROWS // 2
    return jnp.concatenate(
        [jnp.concatenate(heads[:2], axis=1), jnp.concatenate([heads[2][:low], heads[2][low:]], axis=1)], axis=0
    )


def packed_columns(value):
    return packed([value[:, h * HD : (h + 1) * HD] for h in range(3)])


def head_of(piece, h):
    if h < 2:
        return piece[:ROWS, h * HD : (h + 1) * HD]
    return jnp.concatenate([piece[ROWS:, :HD], piece[ROWS:, HD:]], axis=0)


def unpacked(piece):
    return jnp.concatenate([piece[:ROWS], head_of(piece, 2)], axis=1)


def stack_head(ref, h):
    return jnp.concatenate([head_of(ref[i], h) for i in range(4)], axis=0)


def turned(rows):
    return rows.astype(F32).T.astype(BF)


class Fetch:
    def __init__(self, turn, sources, fulls, own, sems):
        self.core, self.half = turn.core, turn.half
        y, z, xl = turn.y, turn.z, turn.xl
        self.odd = (lax.rem(y, 2), lax.rem(z, 2), xl)
        self.across = device(y, z, 1 - xl, turn.core, 1 - turn.half)
        self.beside = (
            device(y + 1 - 2 * self.odd[0], z, xl, turn.core, turn.half),
            device(y, z + 1 - 2 * self.odd[1], xl, turn.core, turn.half),
            device(y, z, 1 - xl, turn.core, turn.half),
        )
        self.sibling = turn.sibling()
        self.sources, self.fulls, self.own = sources, fulls, own
        self.sizes = (HALF, FF // 2, HALF)
        self.xs, self.xr, self.ys, self.yr, self.ds, self.dr, self.es, self.er = sems

    def rows(self, n, c, odd):
        size = self.sizes[n]
        if n == 2:
            return odd * (size // 2), size // 2
        return c * (size // 6) + odd * (size // 12), size // 12

    def piece(self, n, half, c, odd):
        start, size = self.rows(n, c, odd)
        return self.fulls[n].at[pl.ds(pl.multiple_of(half * self.sizes[n] + start, 32), size)]

    def each(self, act, flip=False):
        pl.when(self.core == (1 if flip else 0))(lambda: act(0))
        pl.when(self.core == (0 if flip else 1))(lambda: act(1))

    def keep(self):
        for n in range(3):
            rows = self.fulls[n].at[pl.ds(pl.multiple_of(self.half * self.sizes[n], 32), self.sizes[n])]
            yield pltpu.make_async_copy(self.sources[n], rows, self.own.at[n])

    def give(self, n, c, slot):
        odd = 1 - self.odd[2] if c % 2 else self.odd[1]
        start, size = self.rows(n, c, odd)
        src = self.sources[n].at[pl.ds(pl.multiple_of(start, 32), size)]
        send(src, self.piece(n, self.half, c, odd), self.xs.at[slot], self.xr.at[slot], self.across)

    def own_rows(self):
        for copy in self.keep():
            copy.start()

    def issue(self, c):
        if c == 0:
            pl.when(self.core == 1)(lambda: self.give(2, 1, 6))
        if c < 6:
            self.each(lambda n: self.give(n, c, c))

    def pass_x(self, n, c, slot):
        piece = self.piece(n, 1 - self.half, c, self.odd[1 + c % 2])
        finish(piece, piece, self.xs.at[slot], self.xr.at[slot], self.across)
        send(piece, piece, self.ys.at[slot], self.yr.at[slot], self.beside[1 + c % 2])
        send(piece, piece, self.ds.at[slot], self.dr.at[slot], self.sibling)

    def pass_y(self, n, c, slot):
        piece = self.piece(n, 1 - self.half, c, 1 - self.odd[1 + c % 2])
        finish(piece, piece, self.ys.at[slot], self.yr.at[slot], self.beside[1 + c % 2])
        send(piece, piece, self.es.at[slot], self.er.at[slot], self.sibling)

    def step_x(self, c):
        self.each(lambda n: self.pass_x(n, c, c))
        if c == 0:
            pl.when(self.core == 1)(lambda: self.pass_x(2, 1, 6))

    def step_y(self, c):
        self.each(lambda n: self.pass_y(n, c, c))
        if c == 0:
            pl.when(self.core == 1)(lambda: self.pass_y(2, 1, 6))

    def between(self, n, c, odd, out_sem, in_sem):
        piece = self.piece(n, 1 - self.half, c, odd)
        return pltpu.make_async_remote_copy(
            src_ref=piece, dst_ref=piece, send_sem=out_sem, recv_sem=in_sem,
            device_id=self.sibling, device_id_type=MESH,
        )

    def end(self):
        def sent(n, c, slot):
            odd = self.odd[1 + c % 2]
            self.between(n, c, odd, self.ds.at[slot], self.dr.at[slot]).wait_send()
            self.between(n, c, 1 - odd, self.es.at[slot], self.er.at[slot]).wait_send()

        def came(n, c, slot):
            odd = self.odd[1 + c % 2]
            self.between(n, c, odd, self.ds.at[slot], self.dr.at[slot]).wait_recv()
            self.between(n, c, 1 - odd, self.es.at[slot], self.er.at[slot]).wait_recv()

        def act(n):
            for c in range(6):
                sent(n, c, c)
                came(1 - n, c, c)

        self.each(act)
        pl.when(self.core == 1)(lambda: sent(2, 1, 6))
        pl.when(self.core == 0)(lambda: came(2, 1, 6))
        for copy in self.keep():
            copy.wait()


def front_kernel(
    x_hbm, wq, wk, wv, v0, v1, v2, v3, v4, v5, v6, v7, v8, wi, wu, wo,
    a_ref, qo_ref, kvo_ref, ot_ref, lse_ref, w_ref, w_i, w_u, w_o, vec_ref, bi_ref, xo_ref, x_ref,
    q_ref, kv_ref, small, small_o, o_ref, qt, top, total,
    own_sem, a_out, a_in, b_out, b_in, p_out, p_in, qs, qr, ks, kr, ms, mr, fs, fr, os, om, own, *rest,
):
    sems, lines = rest[:8], rest[8:]
    turn = Turn()
    y, z, xl, core, half = turn.y, turn.z, turn.xl, turn.core, turn.half
    fetch = Fetch(turn, (wi, wu, wo), (w_i, w_u, w_o), own, sems)
    across, sibling = fetch.across, fetch.sibling
    barrier = pltpu.get_barrier_semaphore()
    greet(barrier, across)
    greet(barrier, sibling)
    greet(barrier, fetch.beside[2])

    def mate(dy):
        return device(wrap(y + dy, 4), z, xl, core, half)

    for k in range(1, 4):
        greet(barrier, mate(k))
        greet(barrier, turn.partner(k, 4))

    @pl.when(jnp.logical_not(turn.stays))
    def _():
        greet(barrier, turn.partner(0, 4))
        greet(barrier, fetch.beside[1])

    rows = pl.multiple_of(half * HALF, HALF)
    quarter = GROUP // 2

    def share(i, of, odd, who):
        return w_ref.at[i, pl.ds(pl.multiple_of(of * HALF + odd * GROUP + who * quarter, quarter), quarter)]

    mine = [
        pltpu.make_async_copy(w, w_ref.at[i, pl.ds(rows, HALF)], own_sem.at[i]) for i, w in enumerate((wq, wk, wv))
    ]
    x_copy = pltpu.make_async_copy(x_hbm, x_ref, own_sem.at[12])
    x_copy.start()
    for copy in mine:
        copy.start()
    fetch.own_rows()
    vectors = (v0, v1, v2, v3, v4, v5, v6, v7, v8)
    loads = [pltpu.make_async_copy(v, line, own_sem.at[3 + i]) for i, (v, line) in enumerate(zip(vectors, lines))]
    for copy in loads:
        copy.start()
    for copy in loads:
        copy.wait()
    small[...] = jnp.zeros_like(small)
    for i in range(8):
        small[i : i + 1, :] = lines[i][...].astype(F32).reshape(1, HALF)
    for i in range(4):
        small[8 + i : 9 + i, :] = lines[8][i * HALF : (i + 1) * HALF].astype(F32).reshape(1, HALF)
    pl.semaphore_wait(barrier, 9 + 2 * lax.rem(xl + core, 2))
    send(small, small_o, a_out.at[3], a_in.at[3], across)
    for i in (1, 2, 0):
        odd = 1 - fetch.odd[2] if i == 2 else fetch.odd[i]
        src = (wq, wk, wv)[i].at[pl.ds(pl.multiple_of(odd * GROUP + core * quarter, quarter), quarter)]
        send(src, share(i, half, odd, core), a_out.at[i], a_in.at[i], across)
    finish(small_o, small_o, a_out.at[3], a_in.at[3], across)
    near, far = small[...], small_o[...]
    ahead = jnp.where(half == 0, near, far)
    behind = jnp.where(half == 0, far, near)
    vec_ref[:, :HALF] = ahead[:8]
    vec_ref[:, HALF:] = behind[:8]
    for i in range(4):
        bi_ref[:, i * HALF : (i + 1) * HALF] = ahead[8 + i : 9 + i]
        bi_ref[:, 1536 + i * HALF : 1536 + (i + 1) * HALF] = behind[8 + i : 9 + i]
    x_copy.wait()
    send(x_ref, xo_ref, a_out.at[4], a_in.at[4], sibling)
    x = x_ref[...]
    for i in (1, 2, 0):
        piece = share(i, 1 - half, fetch.odd[i], core)
        finish(piece, piece, a_out.at[i], a_in.at[i], across)
        send(piece, piece, p_out.at[i], p_in.at[i], fetch.beside[i])
        send(piece, piece, b_out.at[i], b_in.at[i], sibling)
    fetch.issue(0)
    fetch.issue(1)
    for i in (1, 2, 0):
        piece = share(i, 1 - half, 1 - fetch.odd[i], core)
        finish(piece, piece, p_out.at[i], p_in.at[i], fetch.beside[i])
        send(piece, piece, b_out.at[3 + i], b_in.at[3 + i], sibling)
    done = {}
    for i in (1, 2, 0):
        for n, odd in ((i, fetch.odd[i]), (3 + i, 1 - fetch.odd[i])):
            piece = share(i, 1 - half, odd, 1 - core)
            finish(piece, piece, b_out.at[n], b_in.at[n], sibling)
        mine[i].wait()
        done[i] = nn(x, w_ref[i])
        if i == 2:
            keys = done[1].astype(BF)
            values = (done[2] + vec_ref[1:2, :]).astype(BF)
            for g in range(4):
                cut = slice(g * GROUP, (g + 1) * GROUP)
                kv_ref[g] = jnp.concatenate([keys[:, cut], values[:, cut]], axis=1)
            turn.mates(kv_ref, kvo_ref.at[y], ks, kr, own=xl)
    fetch.issue(2)
    fetch.issue(3)
    query = (done[0] + vec_ref[0:1, :]).astype(BF) * BF(0.125)
    for g in range(4):
        q_ref[g] = packed_columns(query[:, g * GROUP : (g + 1) * GROUP])
    turn.mates(q_ref, qo_ref, qs, qr)

    def spot(t):
        g, k = lax.div(t, 4), lax.rem(t, 4)
        dy = g + lax.div(g, 2) * (5 - 2 * g)
        return dy, k, wrap(y - dy, 4), wrap(z - k, 4)

    def onward(t):
        dy, k, i, j = spot(t)
        piece = kvo_ref.at[i, j, core]
        send(piece, piece, fs.at[t], fr.at[t], sibling)

    def hand(piece, dy, n):
        send(piece, piece, ms.at[n], mr.at[n], mate(dy))

    turn.end_first(4, kvo_ref.at[y, z, core], ks, kr)
    hand(kvo_ref.at[y, z, core], 1, 4)
    hand(kvo_ref.at[y, z, core], 3, 12)
    onward(0)
    def work(k):
        _, _, i, j = spot(k)
        piece = kvo_ref.at[i, j, 1 - core]
        finish(piece, piece, fs.at[k], fr.at[k], sibling)
        kv = load_chunk(kvo_ref, (i, j))
        for h in range(3):
            scores = nn(kv[:, h * HD : (h + 1) * HD], qt[h])
            old = top[h]
            new = jnp.maximum(old, jnp.max(scores, axis=0, keepdims=True))
            shrink = jnp.exp(old - new)
            weights = jnp.exp(scores - new)
            total[h] = total[h] * shrink + jnp.sum(weights, axis=0, keepdims=True)
            mixed = tn(kv[:, GROUP + h * HD : GROUP + (h + 1) * HD], weights.astype(BF))
            ot_ref[h] = ot_ref[h] * shrink + mixed
            top[h] = new

    def arrive(k):
        dy, n, i, j = spot(k)
        piece = kvo_ref.at[i, j, core]

        @pl.when(dy == 0)
        def _():
            turn.end(n, 4, piece, ks, kr)
            hand(piece, 1, 4 + n)
            hand(piece, 3, 12 + n)

        @pl.when(dy > 0)
        def _():
            finish(piece, piece, ms.at[dy * 4 + n], mr.at[dy * 4 + n], mate(1))

        pl.when((dy == 1) & (lax.rem(n, 2) == 0))(lambda: hand(piece, 1, 8 + n))
        pl.when((dy == 3) & (lax.rem(n, 2) == 1))(lambda: hand(piece, 3, 8 + n))
        onward(k)

    for k in range(1, 4):
        arrive(k)
    fetch.issue(4)
    fetch.issue(5)
    turn.mates_end(qo_ref, qs, qr)
    for h in range(3):
        qt[h] = turned(stack_head(qo_ref, h))
    top[...] = jnp.full_like(top, -jnp.inf)
    total[...] = jnp.zeros_like(total)
    ot_ref[...] = jnp.zeros_like(ot_ref)

    for k in range(3):
        work(k)

    def relay(k, carry):
        arrive(k)
        work(k - 1)

        for c, when in enumerate((4, 5, 7, 8, 11, 12)):
            pl.when(k == when)(functools.partial(fetch.step_x, c))
        return carry

    lax.fori_loop(4, 16, relay, 0)
    work(15)
    heads = []
    for h in range(3):
        lse_ref[h] = top[h] + jnp.log(total[h])
        normal = ot_ref[h] / total[h]
        ot_ref[h] = normal
        heads.append(normal.T.astype(BF))
    for i in range(4):
        o_ref[i] = packed([v[i * ROWS : (i + 1) * ROWS] for v in heads])
    turn.mates(o_ref, a_ref, os, om)
    for c in range(6):
        fetch.step_y(c)
    turn.mates_end(a_ref, os, om)
    finish(xo_ref, xo_ref, a_out.at[4], a_in.at[4], sibling)
    fetch.end()


def front(*arrays):
    return pl.pallas_call(
        front_kernel,
        name="front",
        cost_estimate=cost(70),
        out_shape=(
            shape(4, GROUP, ROWS), shape(4, GROUP, ROWS), shape(4, 4, 2, ROWS, HALF),
            shape(3, HD, 512, dtype=F32), shape(3, 1, 512, dtype=F32),
            shape(3, D, D), shape(D, FF), shape(FF, D), shape(D, D), shape(8, D, dtype=F32), shape(1, FF, dtype=F32),
            shape(ROWS, D), shape(ROWS, D),
        ),
        in_specs=[ANY, ANY, ANY, ANY] + [ANY] * 9 + [ANY] * 3,
        out_specs=(VM,) * 13,
        scratch_shapes=[
            pltpu.VMEM((4, GROUP, ROWS), BF), pltpu.VMEM((4, ROWS, HALF), BF),
            pltpu.VMEM((16, HALF), F32), pltpu.VMEM((16, HALF), F32),
            pltpu.VMEM((4, GROUP, ROWS), BF),
            pltpu.VMEM((3, HD, 512), BF), pltpu.VMEM((3, 1, 512), F32), pltpu.VMEM((3, 1, 512), F32),
            DMA((13,)), DMA((5,)), DMA((5,)), DMA((6,)), DMA((6,)), DMA((3,)), DMA((3,)),
            DMA((4,)), DMA((4,)), DMA((4,)), DMA((4,)), DMA((16,)), DMA((16,)), DMA((16,)), DMA((16,)),
            DMA((4,)), DMA((4,)), DMA((3,)),
        ] + [DMA((7,))] * 8 + [pltpu.VMEM((HALF,), BF)] * 8 + [pltpu.VMEM((1536,), BF)],
        compiler_params=remote(1),
    )(*map(hbm, arrays))


def norm(hidden):
    centred = hidden - jnp.mean(hidden, axis=-1, keepdims=True)
    inverse = lax.rsqrt(jnp.mean(centred * centred, axis=-1, keepdims=True) + EPS)
    return centred * inverse, inverse


def norm_back(scaled, normal, inverse):
    centre = jnp.mean(scaled, axis=-1, keepdims=True)
    along = jnp.mean(scaled * normal, axis=-1, keepdims=True)
    return inverse * (scaled - centre - normal * along)


def column(value):
    return jnp.sum(value, axis=0, keepdims=True)


def block_part(
    turn, ready, x_ref, ct_ref, a_ref, w_i, w_u, w_o, vec_ref, bi_ref,
    out_ref, dh1_ref, da_ref, af_ref, yb_ref, g_ref, df_ref, du_ref, dz_ref, vg_ref,
    af_o, yb_o, g_o, df_o, du_o, dz_o, slope, da_out, outs, ins, p_out, p_in,
):
    passed = ((af_ref, af_o), (yb_ref, yb_o), (g_ref, g_o), (df_ref, df_o), (du_ref, du_o), (dz_ref, dz_o))

    def pass_on(n):
        send(*passed[n], p_out.at[n], p_in.at[n], turn.sibling())

    b_output, first_gain, first_shift = vec_ref[2:3, :], vec_ref[3:4, :], vec_ref[4:5, :]
    b_outer, second_gain, second_shift = vec_ref[5:6, :], vec_ref[6:7, :], vec_ref[7:8, :]
    mixed = jnp.concatenate([unpacked(a_ref[g]) for g in range(4)], axis=1)
    af_ref[...] = mixed
    hidden = x_ref[...].astype(F32) + nn(mixed, w_o[...]) + b_output
    normal1, inverse1 = norm(hidden)
    normed = normal1 * first_gain + first_shift
    low = normed.astype(BF)
    yb_ref[...] = low
    ready()
    pass_on(0)
    pass_on(1)
    second_in = normed + b_outer
    for j in range(4):
        cut = slice(j * D, (j + 1) * D)
        inner = nn(low, w_i[:, cut]) + bi_ref[:, cut]
        cdf = 0.5 * (1.0 + lax.erf(inner * (0.5**0.5)))
        active = (inner * cdf).astype(BF)
        slope[:, cut] = cdf + inner * jnp.exp(inner * inner * -0.5) * 0.3989422804014327
        g_ref[:, cut] = active
        second_in = second_in + nn(active, w_u[cut, :])
    pass_on(2)
    normal2, inverse2 = norm(second_in)
    out_ref[...] = (normal2 * second_gain + second_shift).astype(BF)
    upper = ct_ref[...].astype(F32)


    def note(row, value):
        for h in range(2):
            vg_ref[h, row : row + 1, :] = value[:, h * HALF : (h + 1) * HALF]

    vg_ref[...] = jnp.zeros_like(vg_ref)
    note(6, column(upper * normal2))
    note(7, column(upper))
    dh2 = norm_back(upper * second_gain, normal2, inverse2)
    df = dh2.astype(BF)
    df_ref[...] = df
    pass_on(3)
    note(5, column(df.astype(F32)))
    dy1 = dh2
    for j in range(4):
        cut = slice(j * D, (j + 1) * D)
        du = (slope[:, cut] * nt(df, w_u[cut, :])).astype(BF)
        du_ref[:, cut] = du
        sums = column(du.astype(F32))
        for i in range(2):
            n = 2 * j + i
            vg_ref[n // 4, 8 + n % 4 : 9 + n % 4, :] = sums[:, i * HALF : (i + 1) * HALF]
        dy1 = dy1 + nt(du, w_i[:, cut])
    pass_on(4)
    note(3, column(dy1 * normal1))
    note(4, column(dy1))
    dh1 = norm_back(dy1 * first_gain, normal1, inverse1)
    dh1_ref[...] = dh1
    dz = dh1.astype(BF)
    dz_ref[...] = dz
    pass_on(5)
    note(2, column(dz.astype(F32)))
    da = nt(dz, w_o[...]).astype(BF)
    for g in range(4):
        da_out[g] = packed_columns(da[:, g * GROUP : (g + 1) * GROUP])
    turn.mates(da_out, da_ref, outs, ins)
    for n, (src, got) in enumerate(passed):
        finish(src, got, p_out.at[n], p_in.at[n], turn.sibling())


EARLY = (0, 3)
LATE = (3, 1)


def back_part(
    turn, da_end, q_ref, kv_ref, da_ref, ot_ref, lse_ref, x, x_o, yb, yb_o, g, g_o, a, a_o, df, df_o, du, du_o, dz, dz_o,
    dh1_ref, w_ref, vg_in,
    grad_ref, out, vo,
    rows_q, qt, rows_d, dt, delta, acc, dkv, other, dq, dqo, home, low, low_o, vg,
    g0, g1, g2, r0, r1, r2, s0, s1, s2, t0, t1, t2, rv, sv, sw, tv, uv,
    fs, fr, ks, kr, qs, qr, ls, lr, a_out, a_in, b_out, b_in, c_out, c_in, d_out, d_in, e_out, e_in,
):
    y, z, xl, core, half = turn.y, turn.z, turn.xl, turn.core, turn.half
    x_at = half * 2 + xl
    sibling = turn.sibling()
    barrier = pltpu.get_barrier_semaphore()

    def at(x_to, y_to, z_to):
        return device(y_to, z_to, lax.rem(x_to, 2), core, lax.div(x_to, 2))

    def along_x(k):
        return at(wrap(x_at + k, 4), y, z)

    def at_yz(k):
        i, j = pair(k)
        return at(x_at, wrap(y + i, 4), wrap(z + j, 4))

    def at_xz(k):
        i, j = pair(k)
        return at(wrap(x_at + i, 4), y, wrap(z + j, 4))

    def at_xy(k):
        i, j = pair(k)
        return at(wrap(x_at + i, 4), wrap(y + j, 4), z)

    def hello_yz(k, carry):
        greet(barrier, at_yz(k))
        return carry

    def hello_x(k, carry):
        i = lax.div(k - 1, 3) + 1
        j = lax.rem(k - 1, 3) + 1
        greet(barrier, at_xz(i * 4 + j))
        greet(barrier, at_xy(i * 4 + j))
        return carry

    def hello_row(k, carry):
        greet(barrier, along_x(k))
        return carry

    def hello_turn(k, carry):
        greet(barrier, turn.partner(k, 16))
        return carry

    def hello_all():
        lax.fori_loop(1, 16, hello_yz, 0)
        lax.fori_loop(1, 10, hello_x, 0)
        lax.fori_loop(1, 4, hello_row, 0)
        greet(barrier, sibling)

        @pl.when(jnp.logical_not(turn.stays))
        def _():
            lax.fori_loop(0, 16, hello_turn, 0)

    def ready():
        pl.semaphore_wait(barrier, 37 + 16 * lax.rem(xl + core, 2))

    def run():
        def put(slab, f, m, value):
            blocks = value.astype(BF).reshape(4, 2, 48, HALF)
            if slab == 1:
                g1[f, :, m] = blocks
            else:
                (g0 if slab == 0 else g2)[f, m] = blocks

        def right(ref, second, start):
            cols = pl.ds(pl.multiple_of(start + core * HALF, HALF), HALF)
            return jnp.concatenate([ref[:, cols], second[:, cols]], axis=0)

        def left(ref, second, start):
            return jnp.concatenate([ref[:, start : start + HALF], second[:, start : start + HALF]], axis=0)

        outer = right(df, df_o, 0)
        attn = right(dz, dz_o, 0)
        for f in range(2):
            for m in range(4):
                put(*((1, f, m) if m < 3 else (0, f, 0)), tn(left(g, g_o, f * 1536 + m * HALF), outer))
            rows = left(yb, yb_o, f * HALF)
            for m in range(4):
                put(*((2, f, m) if m < 3 else (0, f, 1)), tn(rows, right(du, du_o, m * D)))
            put(0, f, 2, tn(left(a, a_o, f * HALF), attn))

        def first(part):
            m, n = part
            late = 0 if part is EARLY else 4

            def one(k, carry):
                e = wrap(x_at + k, 4)
                send(
                    g1.at[:, wrap(y + k, 4), pl.ds(m, n)], r1.at[k - 1, :, pl.ds(m, n)],
                    a_out.at[late + 1, k], a_in.at[late + 1, k], at_yz(k * 4),
                )
                send(
                    g2.at[:, pl.ds(m, n), wrap(z + k, 4)], r2.at[k - 1, :, pl.ds(m, n)],
                    a_out.at[late + 2, k], a_in.at[late + 2, k], at_yz(k),
                )
                send(
                    g0.at[lax.div(e, 2), pl.ds(m, n), :, lax.rem(e, 2)], r0.at[k - 1, pl.ds(m, n)],
                    a_out.at[late, k], a_in.at[late, k], along_x(k),
                )
                return carry

            lax.fori_loop(1, 4, one, 0)

        first(EARLY)

        da_end()
        for h in range(3):
            rows = stack_head(q_ref, h)
            rows_q[h] = rows
            qt[h] = turned(rows)
            rows = stack_head(da_ref, h)
            rows_d[h] = rows
            flipped = rows.astype(F32).T
            dt[h] = flipped.astype(BF)
            delta[h] = jnp.sum(flipped * ot_ref[h], axis=0, keepdims=True)
        acc[...] = jnp.zeros_like(acc)

        def compute(k):
            i, j = turn.ahead(k, 16)
            kv = load_chunk(kv_ref, (i, j))
            keys, values = [], []
            for h in range(3):
                key = kv[:, h * HD : (h + 1) * HD]
                value = kv[:, GROUP + h * HD : GROUP + (h + 1) * HD]
                probs = jnp.exp(nn(key, qt[h]) - lse_ref[h])
                slopes = (probs * (nn(value, dt[h]) - delta[h])).astype(BF)
                keys.append(nn(slopes, rows_q[h]).astype(BF))
                values.append(nn(probs.astype(BF), rows_d[h]).astype(BF))
                acc[h] += tn(key, slopes)
            dkv[lax.rem(k, 4)] = jnp.concatenate(keys + values, axis=1).reshape(2, ROWS, HALF)

        def work(k):
            compute(k)
            pass_half(k)

        def pass_half(k):
            i, j = turn.ahead(k, 16)
            send(dkv.at[lax.rem(k, 4), 1 - core], other.at[i, j], fs.at[k], fr.at[k], sibling)

        def join(k):
            i, j = turn.ahead(k, 16)
            finish(other.at[i, j], other.at[i, j], fs.at[k], fr.at[k], sibling)
            other[i, j] = (dkv[lax.rem(k, 4), core].astype(F32) + other[i, j].astype(F32)).astype(BF)

        def relay(k):
            join(k)
            turn.push(k, 16, other.at[turn.ahead(k, 16)], home.at[y, z], ks, kr)

        for k in range(3):
            work(k)
        join(0)
        turn.first(16, other.at[y, z], home.at[y, z], ks, kr)

        def step(k, carry):
            work(k)
            relay(k - 2)
            return carry

        def finish_up(k, carry):
            relay(k)
            return carry

        lax.fori_loop(3, 16, step, 0)
        lax.fori_loop(14, 16, finish_up, 0)
        heads = [(acc[h] * 0.125).T.astype(BF) for h in range(3)]
        for i in range(4):
            dq[i] = packed([v[i * ROWS : (i + 1) * ROWS] for v in heads])
        turn.mates(dq, dqo, qs, qr)

        here = device(y, z, xl, core, half)

        def second(part):
            m, n = part
            late = 0 if part is EARLY else 4

            def add(slab, own, got, to, count, where):
                for k in range(1, 4):
                    piece = got.at[k - 1, pl.ds(m, n)] if slab == 0 else got.at[k - 1, :, pl.ds(m, n)]
                    finish(piece, piece, a_out.at[late + slab, k], a_in.at[late + slab, k], here)

                def one(i, carry):
                    p = where(i)
                    total = own(p).astype(F32)
                    for k in range(3):
                        total = total + got[(k,) + p].astype(F32)
                    to[p] = total.astype(BF)
                    return carry

                lax.fori_loop(0, count, one, 0)

            def push(slab, src, got, k, where):
                @pl.when(k > 0)
                def _():
                    send(src, got.at[k], b_out.at[slab, k], b_in.at[slab, k], where)

            def spot(i):
                return lax.div(i, 2 * n), m + lax.rem(lax.div(i, 2), n), lax.rem(i, 2)

            add(1, lambda p: g1[p[0], y, p[1], p[2]], r1, s1, 4 * n, spot)

            def push1(i, carry):
                e, to = wrap(x_at + lax.div(i, n), 4), m + lax.rem(i, n)
                k = lax.div(i, n) * 4 + wrap(to - z, 4)
                push(1, s1.at[lax.div(e, 2), to, lax.rem(e, 2)], t1, k, at(e, y, to))
                return carry

            lax.fori_loop(0, 4 * n, push1, 0)
            add(2, lambda p: g2[p[0], p[1], z, p[2]], r2, s2, 4 * n, spot)

            def push2(i, carry):
                e, to = wrap(x_at + lax.div(i, n), 4), m + lax.rem(i, n)
                k = lax.div(i, n) * 4 + wrap(to - y, 4)
                push(2, s2.at[lax.div(e, 2), to, lax.rem(e, 2)], t2, k, at(e, to, z))
                return carry

            lax.fori_loop(0, 4 * n, push2, 0)
            add(
                0, lambda p: g0[half, p[0], p[1], xl], r0, s0, 4 * n,
                lambda i: (m + lax.div(i, 4), lax.rem(i, 4)),
            )

            def push0(i, carry):
                e, to = wrap(z + lax.div(i, n), 4), m + lax.rem(i, n)
                k = wrap(to - y, 4) * 4 + lax.div(i, n)
                push(0, s0.at[to, e], t0, k, at(x_at, to, e))
                return carry

            lax.fori_loop(0, 4 * n, push0, 0)

        turn.mates_end(dqo, qs, qr)
        turn.end_first(16, home.at[y, z], ks, kr)

        def done(k, carry):
            turn.end(k, 16, home.at[turn.behind(k, 16)], ks, kr)
            return carry

        lax.fori_loop(1, 16, done, 0)
        low[0] = jnp.concatenate([unpacked(dqo[i]) for i in range(4)], axis=1)
        sums = []
        for i in range(4):
            total = home[0, i].astype(F32)
            for k in range(1, 4):
                total = total + home[k, i].astype(F32)
            sums.append(total.astype(BF))
        low[1] = jnp.concatenate([v[:, :GROUP] for v in sums], axis=1)
        low[2] = jnp.concatenate([v[:, GROUP:] for v in sums], axis=1)
        send(low, low_o, ls, lr, sibling)
        second(EARLY)
        finish(low, low_o, ls, lr, sibling)
        cols = pl.ds(pl.multiple_of(core * HALF, HALF), HALF)
        both_low = [jnp.concatenate([low[i, :, cols], low_o[i, :, cols]], axis=0) for i in range(3)]
        for f in range(2):
            rows = left(x, x_o, f * HALF)
            for i, slab in enumerate((2, 1, 0)):
                put(slab, f, 3, tn(rows, both_low[i]))
        first(LATE)
        grad = dh1_ref[...]
        for i in range(3):
            grad = grad + nt(low[i], w_ref[i])
        grad_ref[...] = grad
        vg[...] = vg_in[...]
        for row, i in ((0, 0), (1, 2)):
            value = column(low[i].astype(F32))
            for f in range(2):
                vg[f, row : row + 1, :] = value[:, f * HALF : (f + 1) * HALF]

        def first3(k, carry):
            src = vg.at[lax.div(wrap(x_at + k, 4), 2)]
            send(src, rv.at[k - 1], a_out.at[3, k], a_in.at[3, k], along_x(k))
            return carry

        lax.fori_loop(1, 4, first3, 0)

        def third(part):
            early = part is EARLY

            def whole(own, got, slab):
                def wait(k, carry):
                    arrived(got.at[k], b_in.at[slab, k], here)
                    return carry

                lax.fori_loop(1, 16, wait, 0)

                def one(k, total):
                    return total + got[k].astype(F32)

                out[core, slab, y, z, xl] = lax.fori_loop(1, 16, one, own.astype(F32)).astype(BF)

            def spread(slab, count, where):
                mine = out.at[core, slab, y, z, xl]

                def one(k, carry):
                    send(mine, mine, c_out.at[slab, k], c_in.at[slab, k], where(k))
                    return carry

                lax.fori_loop(1, count, one, 0)

            @pl.when(z < 3 if early else z == 3)
            def _():
                whole(s1[half, z, xl], t1, 1)
                spread(1, 8, lambda k: device(y, wrap(z + lax.div(k, 2), 4), wrap(xl + lax.rem(k, 2), 2), core, half))

            @pl.when(y < 3 if early else y == 3)
            def _():
                whole(s2[half, y, xl], t2, 2)
                spread(2, 8, lambda k: device(wrap(y + lax.div(k, 2), 4), z, wrap(xl + lax.rem(k, 2), 2), core, half))
                whole(s0[y, z], t0, 0)
                spread(0, 16, at_yz)

        def fourth(part):
            m, n = part
            late = 0 if part is EARLY else 3

            def wait(slab, piece, k):
                @pl.when(k > 0)
                def _():
                    arrived(piece, c_in.at[slab, k], here)

            def got1(i, carry):
                zz, xx = m + lax.div(i, 2), lax.rem(i, 2)
                wait(1, out.at[core, 1, y, zz, xx], wrap(z - zz, 4) * 2 + wrap(xl - xx, 2))
                return carry

            lax.fori_loop(0, 2 * n, got1, 0)

            def push1(k, carry):
                mine = out.at[core, 1, y, pl.ds(m, n)]
                send(mine, mine, d_out.at[late + 1, k], d_in.at[late + 1, k], at_yz(k * 4))
                return carry

            for k in (1, 3) if part is EARLY else (1, 2, 3):
                push1(k, 0)

            def got2(i, carry):
                yy, xx = m + lax.div(i, 2), lax.rem(i, 2)
                wait(2, out.at[core, 2, yy, z, xx], wrap(y - yy, 4) * 2 + wrap(xl - xx, 2))
                return carry

            lax.fori_loop(0, 2 * n, got2, 0)

            def push2(k, carry):
                mine = out.at[core, 2, pl.ds(m, n), z]
                send(mine, mine, d_out.at[late + 2, k], d_in.at[late + 2, k], at_yz(k))
                return carry

            for k in (1, 3) if part is EARLY else (1, 2, 3):
                push2(k, 0)

            def got0(i, carry):
                yy, zz = m + lax.div(i, 4), lax.rem(i, 4)
                wait(0, out.at[core, 0, yy, zz, xl], wrap(y - yy, 4) * 4 + wrap(z - zz, 4))
                return carry

            lax.fori_loop(0, 4 * n, got0, 0)
            mine0 = out.at[core, 0, pl.ds(m, n), :, xl]
            send(mine0, mine0, d_out.at[late, 1], d_in.at[late, 1], device(y, z, 1 - xl, core, half))

        def hand_on():
            m, n = EARLY
            for k, side in ((1, 0), (3, 1)):
                y_from, z_from = wrap(y - k, 4), wrap(z - k, 4)
                piece = out.at[core, 1, y_from, pl.ds(m, n)]
                finish(piece, piece, d_out.at[1, k], d_in.at[1, k], here)
                part1 = out.at[core, 1, y_from, pl.ds(m, n), side]
                send(part1, part1, d_out.at[1, 2], d_in.at[1, 2], at_yz(k * 4))
                piece = out.at[core, 2, pl.ds(m, n), z_from]
                finish(piece, piece, d_out.at[2, k], d_in.at[2, k], here)
                part2 = out.at[core, 2, pl.ds(m, n), z_from, side]
                send(part2, part2, d_out.at[2, 2], d_in.at[2, 2], at_yz(k))

        def own_part(slab, who, part):
            m, n = part
            return out.at[who, 1, :, pl.ds(m, n)] if slab == 1 else out.at[who, slab, pl.ds(m, n)]

        def last(part):
            m, n = part
            late = 0 if part is EARLY else 3

            def got1(k, carry):
                piece = out.at[core, 1, wrap(y - k, 4), pl.ds(m, n)]
                finish(piece, piece, d_out.at[late + 1, k], d_in.at[late + 1, k], here)
                return carry

            def got2(k, carry):
                piece = out.at[core, 2, pl.ds(m, n), wrap(z - k, 4)]
                finish(piece, piece, d_out.at[late + 2, k], d_in.at[late + 2, k], here)
                return carry

            def onward(slab):
                piece = own_part(slab, core, part)
                send(piece, piece, e_out.at[late + slab], e_in.at[late + slab], sibling)

            for k in (2,) if part is EARLY else (1, 2, 3):
                got1(k, 0)
            onward(1)
            for k in (2,) if part is EARLY else (1, 2, 3):
                got2(k, 0)
            onward(2)
            piece0 = out.at[core, 0, pl.ds(m, n), :, 1 - xl]
            finish(piece0, piece0, d_out.at[late, 1], d_in.at[late, 1], here)
            onward(0)

        third(EARLY)
        for k in range(1, 4):
            finish(rv.at[k - 1], rv.at[k - 1], a_out.at[3, k], a_in.at[3, k], here)
        part_sum = vg[half] + rv[0] + rv[1] + rv[2]
        sv[...] = part_sum.astype(BF)

        for k in range(1, 4):
            send(sv, tv.at[k], b_out.at[3, k], b_in.at[3, k], at_yz(k * 4))
        second(LATE)
        for k in range(1, 4):
            finish(tv.at[k], tv.at[k], b_out.at[3, k], b_in.at[3, k], here)
            part_sum = part_sum + tv[k].astype(F32)
        sw[...] = part_sum.astype(BF)
        for k in range(1, 4):
            send(sw, tv.at[4 + k], b_out.at[3, 4 + k], b_in.at[3, 4 + k], at_yz(k))
        fourth(EARLY)
        third(LATE)
        hand_on()

        for k in range(5, 8):
            finish(tv.at[k], tv.at[k], b_out.at[3, k], b_in.at[3, k], here)
            part_sum = part_sum + tv[k].astype(F32)
        vo[...] = part_sum
        send(vo, uv, e_out.at[6], e_in.at[6], sibling)
        fourth(LATE)
        last(EARLY)
        for slab, count, own, got in ((1, 8, s1, t1), (2, 8, s2, t2), (0, 16, s0, t0)):
            mine = out.at[core, slab, y, z, xl]

            def gone2(k, carry):
                left_here(got.at[k], b_out.at[slab, k], here)
                return carry

            def gone3(k, carry):
                left_here(mine, c_out.at[slab, k], here)
                return carry

            lax.fori_loop(1, 16, gone2, 0)
            lax.fori_loop(1, count, gone3, 0)
        last(LATE)
        for late, part in ((0, EARLY), (3, LATE)):
            for slab in range(3):
                piece = own_part(slab, 1 - core, part)
                finish(piece, piece, e_out.at[late + slab], e_in.at[late + slab], here)
        finish(uv, uv, e_out.at[6], e_in.at[6], here)
        vo[...] = vo[...] + uv[...]

    return hello_all, ready, run


BLOCK_ACTS = ((ROWS, D), (ROWS, D), (ROWS, FF), (ROWS, D), (ROWS, FF), (ROWS, D))


def rest_kernel(
    x, ct, mixed, w_i, w_u, w_o, vec, bi, q, kv, ot, lse, x_o, w_qkv,
    layer_ref, grad_ref, out, vo,
    dh1, da, vg_in, a, yb, g, df, du, dz, a_o, yb_o, g_o, df_o, du_o, dz_o, slope, da_out, *more,
):
    (outs, ins, p_out, p_in), more = more[:4], more[4:]
    turn = Turn()
    hello_all, ready, run = back_part(
        turn, lambda: turn.mates_end(da, outs, ins), q, kv, da, ot, lse, x, x_o, yb, yb_o, g, g_o, a, a_o, df, df_o,
        du, du_o, dz, dz_o, dh1, w_qkv, vg_in, grad_ref, out, vo, *more,
    )
    hello_all()
    block_part(
        turn, ready, x, ct, mixed, w_i, w_u, w_o, vec, bi, layer_ref, dh1, da, a, yb, g, df, du, dz, vg_in,
        a_o, yb_o, g_o, df_o, du_o, dz_o, slope, da_out, outs, ins, p_out, p_in,
    )
    run()


def rest(*arrays):
    blk = (48, HALF)
    acts = [(v, BF) for v in BLOCK_ACTS]
    first = [((ROWS, D), F32), ((4, GROUP, ROWS), BF), ((2, 16, HALF), F32)] + acts + acts + [
        ((ROWS, FF), F32), ((4, GROUP, ROWS), BF),
    ]
    second = [
        ((3, 512, HD), BF), ((3, HD, 512), BF), ((3, 512, HD), BF), ((3, HD, 512), BF), ((3, 1, 512), F32),
        ((3, HD, 512), F32), ((4, 2, ROWS, HALF), BF), ((4, 4, ROWS, HALF), BF),
        ((4, GROUP, ROWS), BF), ((4, GROUP, ROWS), BF), ((4, 4, ROWS, HALF), BF), ((3, ROWS, D), BF), ((3, ROWS, D), BF),
        ((2, 16, HALF), F32),
        ((2, 4, 4, 2, *blk), BF), ((2, 4, 4, 2, *blk), BF), ((2, 4, 4, 2, *blk), BF),
        ((3, 4, 4, *blk), BF), ((3, 2, 4, 2, *blk), BF), ((3, 2, 4, 2, *blk), BF),
        ((4, 4, *blk), BF), ((2, 4, 2, *blk), BF), ((2, 4, 2, *blk), BF),
        ((16, *blk), BF), ((16, *blk), BF), ((16, *blk), BF),
        ((3, 16, HALF), F32), ((16, HALF), BF), ((16, HALF), BF), ((8, 16, HALF), BF), ((16, HALF), F32),
    ]
    return pl.pallas_call(
        rest_kernel,
        name="rest",
        cost_estimate=cost(130),
        out_shape=(
            shape(ROWS, D), shape(ROWS, D, dtype=F32), shape(2, 3, 4, 4, 2, *blk), shape(16, HALF, dtype=F32),
        ),
        in_specs=[VM] * 14,
        out_specs=(VM,) * 4,
        scratch_shapes=[pltpu.VMEM(*v) for v in first] + [DMA((4,)), DMA((4,)), DMA((6,)), DMA((6,))]
        + [pltpu.VMEM(*v) for v in second] + [
            DMA((16,)), DMA((16,)), DMA((16,)), DMA((16,)), DMA((4,)), DMA((4,)), DMA, DMA,
            DMA((7, 4)), DMA((7, 4)), DMA((4, 16)), DMA((4, 16)), DMA((3, 16)), DMA((3, 16)),
            DMA((6, 4)), DMA((6, 4)), DMA((7,)), DMA((7,)),
        ],
        compiler_params=pltpu.CompilerParams(
            collective_id=3, has_side_effects=True, vmem_limit_bytes=34 << 20
        ),
    )(*map(vm, arrays))


def spell_kernel(full, vo, layer, grad, *refs):
    q_ref, k_ref, v_ref, o_ref, i_ref, u_ref, layer_ref, grad_ref = refs[:8]
    lines, (stage, sems, direct) = refs[8:17], refs[17:]
    straight = [
        pltpu.make_async_copy(layer, layer_ref, direct.at[0]), pltpu.make_async_copy(grad, grad_ref, direct.at[1])
    ]
    for copy in straight:
        copy.start()
    for i in range(8):
        lines[i][...] = vo[i : i + 1, :].reshape(HALF)
    lines[8][...] = jnp.concatenate([vo[8 + i : 9 + i, :] for i in range(4)], axis=1).reshape(1536)

    def copies(n):
        slot = stage.at[n % 3]
        rows = slice(n * 48, (n + 1) * 48)
        made = [
            pltpu.make_async_copy(slot.at[m], ref.at[rows], sems.at[n % 3, m])
            for m, ref in enumerate((q_ref, k_ref, v_ref, o_ref))
        ]
        for m in range(4):
            made.append(pltpu.make_async_copy(
                slot.at[4 + m], i_ref.at[rows, m * D : (m + 1) * D], sems.at[n % 3, 4 + m]
            ))
            made.append(pltpu.make_async_copy(
                slot.at[8 + m], u_ref.at[m * HALF + n * 48 : m * HALF + (n + 1) * 48], sems.at[n % 3, 8 + m]
            ))
        return made

    for n in range(8):
        if n >= 3:
            for copy in copies(n - 3):
                copy.wait()
        i, xl = n // 2, n % 2
        for c in range(2):
            cols = slice(c * HALF, (c + 1) * HALF)
            units = [(2, 3), (1, 3), (0, 3), (0, 2), (2, 0), (2, 1), (2, 2), (0, 1), (1, 0), (1, 1), (1, 2), (0, 0)]
            for m, (slab, unit) in enumerate(units):
                piece = full[c, 1, i, unit, xl] if slab == 1 else full[c, slab, unit, i, xl]
                stage[n % 3, m, :, cols] = piece.astype(F32)
        for copy in copies(n):
            copy.start()
    for n in (5, 6, 7):
        for copy in copies(n):
            copy.wait()
    for copy in straight:
        copy.wait()


def spell(*arrays):
    return pl.pallas_call(
        spell_kernel,
        name="spell",
        out_shape=tuple(
            plain_shape(*dims, dtype=F32)
            for dims in ((HALF, D), (HALF, D), (HALF, D), (HALF, D), (HALF, FF), (1536, D))
        ) + (plain_shape(ROWS, D), plain_shape(ROWS, D, dtype=F32))
        + (plain_shape(HALF, dtype=F32),) * 8 + (plain_shape(1536, dtype=F32),),
        in_specs=[VM] * 4,
        out_specs=(ANY,) * 8 + (VM,) * 9,
        scratch_shapes=[pltpu.VMEM((3, 12, 48, D), F32), DMA((3, 12)), DMA((2,))],
        compiler_params=plain(),
        cost_estimate=cost(6),
    )(*map(vm, arrays))


def local(
    tokens, cotangent, w_query, w_key, w_value, w_output, b_query, b_value, b_output,
    first_gain, first_shift, w_inner, b_inner, w_outer, b_outer, second_gain, second_shift,
):
    x = tokens[0]
    mixed, q_all, kv_all, mixed_t, lse, w_qkv, w_i, w_u, w_o, vec, bi, x_o, x_in = front(
        x, w_query, w_key, w_value, b_query, b_value, b_output, first_gain, first_shift, b_outer, second_gain,
        second_shift, b_inner, w_inner, w_outer, w_output,
    )
    layer_out, tokens_grad, summed, vecs = rest(
        x_in, cotangent[0], mixed, w_i, w_u, w_o, vec, bi, q_all, kv_all, mixed_t, lse, x_o, w_qkv
    )
    gq, gk, gv, go, gi, gu, layer_out, tokens_grad, *vecs = spell(summed, vecs, layer_out, tokens_grad)
    return (
        layer_out[None], tokens_grad[None], gq, gk, gv, go,
        vecs[0], vecs[1], vecs[2], vecs[3], vecs[4], gi, vecs[8], gu, vecs[5], vecs[6], vecs[7],
    )


def solution(mesh):
    rows = P(("seq", "fsdp"), "ctx", None)
    mat = P("fsdp", None)
    vec = P("fsdp")
    return jax.shard_map(
        local,
        mesh=mesh,
        in_specs=(rows, rows, mat, mat, mat, mat, vec, vec, vec, vec, vec, mat, vec, mat, vec, vec, vec),
        out_specs=(rows, rows, mat, mat, mat, mat, vec, vec, vec, vec, vec, mat, vec, mat, vec, vec, vec),
        check_vma=False,
    )
```

```python
import functools

import jax
import jax.numpy as jnp
from jax import lax
from jax.experimental import pallas as pl
from jax.experimental.pallas import tpu as pltpu
from jax.sharding import PartitionSpec as P

AXES = ("ctx", "seq", "fsdp")
MESH = pl.DeviceIdType.MESH
BF = jnp.bfloat16
F32 = jnp.float32
D = 768
FF = 3072
HALF = 384
GROUP = 192
HD = 64
ROWS = 128
EPS = 1e-12
LIMIT = 12 << 20
VM = pl.BlockSpec(memory_space=pltpu.VMEM)
ANY = pl.BlockSpec(memory_space=pltpu.HBM)


def plain_shape(*dims, dtype=BF):
    return jax.ShapeDtypeStruct(dims, dtype)


def shape(*dims, dtype=BF):
    return pltpu.VMEM(dims, dtype)


def hbm(array):
    return pltpu.with_memory_space_constraint(array, pltpu.HBM)


def vm(array):
    return pltpu.with_memory_space_constraint(array, pltpu.VMEM)


def nn(left, right):
    return jnp.dot(left, right, preferred_element_type=F32)


def nt(left, right):
    return lax.dot_general(left, right, (((1,), (1,)), ((), ())), preferred_element_type=F32)


def tn(left, right):
    return lax.dot_general(left, right, (((0,), (0,)), ((), ())), preferred_element_type=F32)


def wrap(value, size):
    return lax.rem(value + size, size)


def place():
    ctx = lax.axis_index("ctx")
    y = lax.div(ctx, 8)
    z = lax.rem(lax.div(ctx, 2), 4)
    return y, z, lax.rem(ctx, 2), lax.axis_index("seq"), lax.axis_index("fsdp")


def device(y, z, xl, core, half):
    return ((y * 4 + z) * 2 + xl, core, half)


def send(src, dst, out_sem, in_sem, where):
    pltpu.make_async_remote_copy(
        src_ref=src, dst_ref=dst, send_sem=out_sem, recv_sem=in_sem,
        device_id=where, device_id_type=MESH,
    ).start()


def finish(src, dst, out_sem, in_sem, where):
    copy = pltpu.make_async_remote_copy(
        src_ref=src, dst_ref=dst, send_sem=out_sem, recv_sem=in_sem,
        device_id=where, device_id_type=MESH,
    )
    copy.wait_send()
    copy.wait_recv()


def arrived(got, in_sem, where):
    pltpu.make_async_remote_copy(
        src_ref=got, dst_ref=got, send_sem=in_sem, recv_sem=in_sem, device_id=where, device_id_type=MESH
    ).wait_recv()


def left_here(src, out_sem, where):
    pltpu.make_async_remote_copy(
        src_ref=src, dst_ref=src, send_sem=out_sem, recv_sem=out_sem, device_id=where, device_id_type=MESH
    ).wait_send()


def greet(barrier, where):
    pl.semaphore_signal(barrier, inc=1, device_id=where, device_id_type=MESH)


def pair(k):
    return lax.div(k, 4), lax.rem(k, 4)


class Turn:
    def __init__(self):
        self.y, self.z, self.xl, self.core, self.half = place()
        self.stays = self.xl == self.core

    def step(self, k, count):
        if count == 4:
            return 0, k
        return lax.rem(k + lax.div(k, 4), 4), lax.rem(k, 4)

    def partner(self, k, count):
        i, j = self.ahead(k, count)
        return device(i, j, self.core, self.xl, self.half)

    def ahead(self, k, count):
        i, j = self.step(k, count)
        return wrap(self.y + i, 4), wrap(self.z + j, 4)

    def behind(self, k, count):
        i, j = self.step(k, count)
        return wrap(self.y - i, 4), wrap(self.z - j, 4)

    def sibling(self):
        return device(self.y, self.z, self.xl, 1 - self.core, self.half)

    def hello(self, count, others=()):
        barrier = pltpu.get_barrier_semaphore()

        def one(k, carry):
            greet(barrier, self.partner(k, count))
            return carry

        lax.fori_loop(1, count, one, 0)
        for where in others:
            greet(barrier, where)

        @pl.when(jnp.logical_not(self.stays))
        def _():
            greet(barrier, self.partner(0, count))

    def ready(self, count, others=0):
        barrier = pltpu.get_barrier_semaphore()
        pl.semaphore_wait(barrier, count - 1 + others + lax.rem(self.xl + self.core, 2))

    def push(self, k, count, src, dst, outs, ins):
        send(src, dst, outs.at[k], ins.at[k], self.partner(k, count))

    def first(self, count, src, dst, outs, ins):
        @pl.when(self.stays)
        def _():
            pltpu.make_async_copy(src, dst, ins.at[0]).start()

        @pl.when(jnp.logical_not(self.stays))
        def _():
            self.push(0, count, src, dst, outs, ins)

    def start(self, count, src, dst, outs, ins):
        self.first(count, src(0), dst, outs, ins)

        def one(k, carry):
            self.push(k, count, src(k), dst, outs, ins)
            return carry

        lax.fori_loop(1, count, one, 0)

    def end(self, k, count, got, outs, ins):
        finish(got, got, outs.at[k], ins.at[k], self.partner(k, count))

    def end_first(self, count, got, outs, ins):
        @pl.when(self.stays)
        def _():
            pltpu.make_async_copy(got, got, ins.at[0]).wait()

        @pl.when(jnp.logical_not(self.stays))
        def _():
            self.end(0, count, got, outs, ins)

    def mates(self, src, dst, outs, ins, own=None):
        slot = dst.at[self.z] if own is None else dst.at[self.z, own]
        self.start(4, lambda k: src.at[self.ahead(k, 4)[1]], slot, outs, ins)

    def mates_end(self, dst, outs, ins):
        self.end_first(4, dst.at[self.z], outs, ins)

        def one(k, carry):
            self.end(k, 4, dst.at[self.behind(k, 4)[1]], outs, ins)
            return carry

        lax.fori_loop(1, 4, one, 0)


def cost(us):
    return pl.CostEstimate(flops=0, transcendentals=0, bytes_accessed=int(us * 3e6))


def remote(number):
    return pltpu.CompilerParams(collective_id=number, has_side_effects=True, vmem_limit_bytes=LIMIT)


def plain():
    return pltpu.CompilerParams(vmem_limit_bytes=LIMIT)


DMA = pltpu.SemaphoreType.DMA


CHUNK = 256


def load_chunk(ref, at):
    return ref[at].reshape(CHUNK, HALF)


def packed(heads):
    low = ROWS // 2
    return jnp.concatenate(
        [jnp.concatenate(heads[:2], axis=1), jnp.concatenate([heads[2][:low], heads[2][low:]], axis=1)], axis=0
    )


def packed_columns(value):
    return packed([value[:, h * HD : (h + 1) * HD] for h in range(3)])


def head_of(piece, h):
    if h < 2:
        return piece[:ROWS, h * HD : (h + 1) * HD]
    return jnp.concatenate([piece[ROWS:, :HD], piece[ROWS:, HD:]], axis=0)


def unpacked(piece):
    return jnp.concatenate([piece[:ROWS], head_of(piece, 2)], axis=1)


def stack_head(ref, h):
    return jnp.concatenate([head_of(ref[i], h) for i in range(4)], axis=0)


def turned(rows):
    return rows.astype(F32).T.astype(BF)


class Fetch:
    def __init__(self, turn, sources, fulls, own, sems):
        self.core, self.half = turn.core, turn.half
        y, z, xl = turn.y, turn.z, turn.xl
        self.odd = (lax.rem(y, 2), lax.rem(z, 2), xl)
        self.across = device(y, z, 1 - xl, turn.core, 1 - turn.half)
        self.beside = (
            device(y + 1 - 2 * self.odd[0], z, xl, turn.core, turn.half),
            device(y, z + 1 - 2 * self.odd[1], xl, turn.core, turn.half),
            device(y, z, 1 - xl, turn.core, turn.half),
        )
        self.sibling = turn.sibling()
        self.sources, self.fulls, self.own = sources, fulls, own
        self.sizes = (HALF, FF // 2, HALF)
        self.xs, self.xr, self.ys, self.yr, self.ds, self.dr, self.es, self.er = sems

    def rows(self, n, c, odd):
        size = self.sizes[n]
        if n == 2:
            return odd * (size // 2), size // 2
        return c * (size // 6) + odd * (size // 12), size // 12

    def piece(self, n, half, c, odd):
        start, size = self.rows(n, c, odd)
        return self.fulls[n].at[pl.ds(pl.multiple_of(half * self.sizes[n] + start, 32), size)]

    def each(self, act, flip=False):
        pl.when(self.core == (1 if flip else 0))(lambda: act(0))
        pl.when(self.core == (0 if flip else 1))(lambda: act(1))

    def keep(self):
        for n in range(3):
            rows = self.fulls[n].at[pl.ds(pl.multiple_of(self.half * self.sizes[n], 32), self.sizes[n])]
            yield pltpu.make_async_copy(self.sources[n], rows, self.own.at[n])

    def give(self, n, c, slot):
        odd = 1 - self.odd[2] if c % 2 else self.odd[1]
        start, size = self.rows(n, c, odd)
        src = self.sources[n].at[pl.ds(pl.multiple_of(start, 32), size)]
        send(src, self.piece(n, self.half, c, odd), self.xs.at[slot], self.xr.at[slot], self.across)

    def own_rows(self):
        for copy in self.keep():
            copy.start()

    def issue(self, c):
        if c == 0:
            pl.when(self.core == 1)(lambda: self.give(2, 1, 6))
        if c < 6:
            self.each(lambda n: self.give(n, c, c))

    def pass_x(self, n, c, slot):
        piece = self.piece(n, 1 - self.half, c, self.odd[1 + c % 2])
        finish(piece, piece, self.xs.at[slot], self.xr.at[slot], self.across)
        send(piece, piece, self.ys.at[slot], self.yr.at[slot], self.beside[1 + c % 2])
        send(piece, piece, self.ds.at[slot], self.dr.at[slot], self.sibling)

    def pass_y(self, n, c, slot):
        piece = self.piece(n, 1 - self.half, c, 1 - self.odd[1 + c % 2])
        finish(piece, piece, self.ys.at[slot], self.yr.at[slot], self.beside[1 + c % 2])
        send(piece, piece, self.es.at[slot], self.er.at[slot], self.sibling)

    def step_x(self, c):
        self.each(lambda n: self.pass_x(n, c, c))
        if c == 0:
            pl.when(self.core == 1)(lambda: self.pass_x(2, 1, 6))

    def step_y(self, c):
        self.each(lambda n: self.pass_y(n, c, c))
        if c == 0:
            pl.when(self.core == 1)(lambda: self.pass_y(2, 1, 6))

    def between(self, n, c, odd, out_sem, in_sem):
        piece = self.piece(n, 1 - self.half, c, odd)
        return pltpu.make_async_remote_copy(
            src_ref=piece, dst_ref=piece, send_sem=out_sem, recv_sem=in_sem,
            device_id=self.sibling, device_id_type=MESH,
        )

    def end(self):
        def sent(n, c, slot):
            odd = self.odd[1 + c % 2]
            self.between(n, c, odd, self.ds.at[slot], self.dr.at[slot]).wait_send()
            self.between(n, c, 1 - odd, self.es.at[slot], self.er.at[slot]).wait_send()

        def came(n, c, slot):
            odd = self.odd[1 + c % 2]
            self.between(n, c, odd, self.ds.at[slot], self.dr.at[slot]).wait_recv()
            self.between(n, c, 1 - odd, self.es.at[slot], self.er.at[slot]).wait_recv()

        def act(n):
            for c in range(6):
                sent(n, c, c)
                came(1 - n, c, c)

        self.each(act)
        pl.when(self.core == 1)(lambda: sent(2, 1, 6))
        pl.when(self.core == 0)(lambda: came(2, 1, 6))
        for copy in self.keep():
            copy.wait()


def front_kernel(
    x_hbm, wq, wk, wv, v0, v1, v2, v3, v4, v5, v6, v7, v8, wi, wu, wo,
    a_ref, qo_ref, kvo_ref, ot_ref, lse_ref, w_ref, w_i, w_u, w_o, vec_ref, bi_ref, xo_ref, x_ref,
    q_ref, kv_ref, small, small_o, o_ref, qt, top, total,
    own_sem, a_out, a_in, b_out, b_in, p_out, p_in, qs, qr, ks, kr, ms, mr, fs, fr, os, om, own, *rest,
):
    sems, lines = rest[:8], rest[8:]
    turn = Turn()
    y, z, xl, core, half = turn.y, turn.z, turn.xl, turn.core, turn.half
    fetch = Fetch(turn, (wi, wu, wo), (w_i, w_u, w_o), own, sems)
    across, sibling = fetch.across, fetch.sibling
    barrier = pltpu.get_barrier_semaphore()
    greet(barrier, across)
    greet(barrier, sibling)
    greet(barrier, fetch.beside[2])

    def mate(dy):
        return device(wrap(y + dy, 4), z, xl, core, half)

    for k in range(1, 4):
        greet(barrier, mate(k))
        greet(barrier, turn.partner(k, 4))

    @pl.when(jnp.logical_not(turn.stays))
    def _():
        greet(barrier, turn.partner(0, 4))
        greet(barrier, fetch.beside[1])

    rows = pl.multiple_of(half * HALF, HALF)
    quarter = GROUP // 2

    def share(i, of, odd, who):
        return w_ref.at[i, pl.ds(pl.multiple_of(of * HALF + odd * GROUP + who * quarter, quarter), quarter)]

    mine = [
        pltpu.make_async_copy(w, w_ref.at[i, pl.ds(rows, HALF)], own_sem.at[i]) for i, w in enumerate((wq, wk, wv))
    ]
    x_copy = pltpu.make_async_copy(x_hbm, x_ref, own_sem.at[12])
    x_copy.start()
    for copy in mine:
        copy.start()
    fetch.own_rows()
    vectors = (v0, v1, v2, v3, v4, v5, v6, v7, v8)
    loads = [pltpu.make_async_copy(v, line, own_sem.at[3 + i]) for i, (v, line) in enumerate(zip(vectors, lines))]
    for copy in loads:
        copy.start()
    for copy in loads:
        copy.wait()
    small[...] = jnp.zeros_like(small)
    for i in range(8):
        small[i : i + 1, :] = lines[i][...].astype(F32).reshape(1, HALF)
    for i in range(4):
        small[8 + i : 9 + i, :] = lines[8][i * HALF : (i + 1) * HALF].astype(F32).reshape(1, HALF)
    pl.semaphore_wait(barrier, 9 + 2 * lax.rem(xl + core, 2))
    send(small, small_o, a_out.at[3], a_in.at[3], across)
    for i in (1, 2, 0):
        odd = 1 - fetch.odd[2] if i == 2 else fetch.odd[i]
        src = (wq, wk, wv)[i].at[pl.ds(pl.multiple_of(odd * GROUP + core * quarter, quarter), quarter)]
        send(src, share(i, half, odd, core), a_out.at[i], a_in.at[i], across)
    finish(small_o, small_o, a_out.at[3], a_in.at[3], across)
    near, far = small[...], small_o[...]
    ahead = jnp.where(half == 0, near, far)
    behind = jnp.where(half == 0, far, near)
    vec_ref[:, :HALF] = ahead[:8]
    vec_ref[:, HALF:] = behind[:8]
    for i in range(4):
        bi_ref[:, i * HALF : (i + 1) * HALF] = ahead[8 + i : 9 + i]
        bi_ref[:, 1536 + i * HALF : 1536 + (i + 1) * HALF] = behind[8 + i : 9 + i]
    x_copy.wait()
    send(x_ref, xo_ref, a_out.at[4], a_in.at[4], sibling)
    x = x_ref[...]
    for i in (1, 2, 0):
        piece = share(i, 1 - half, fetch.odd[i], core)
        finish(piece, piece, a_out.at[i], a_in.at[i], across)
        send(piece, piece, p_out.at[i], p_in.at[i], fetch.beside[i])
        send(piece, piece, b_out.at[i], b_in.at[i], sibling)
    fetch.issue(0)
    fetch.issue(1)
    for i in (1, 2, 0):
        piece = share(i, 1 - half, 1 - fetch.odd[i], core)
        finish(piece, piece, p_out.at[i], p_in.at[i], fetch.beside[i])
        send(piece, piece, b_out.at[3 + i], b_in.at[3 + i], sibling)
    done = {}
    for i in (1, 2, 0):
        for n, odd in ((i, fetch.odd[i]), (3 + i, 1 - fetch.odd[i])):
            piece = share(i, 1 - half, odd, 1 - core)
            finish(piece, piece, b_out.at[n], b_in.at[n], sibling)
        mine[i].wait()
        done[i] = nn(x, w_ref[i])
        if i == 2:
            keys = done[1].astype(BF)
            values = (done[2] + vec_ref[1:2, :]).astype(BF)
            for g in range(4):
                cut = slice(g * GROUP, (g + 1) * GROUP)
                kv_ref[g] = jnp.concatenate([keys[:, cut], values[:, cut]], axis=1)
            turn.mates(kv_ref, kvo_ref.at[y], ks, kr, own=xl)
    fetch.issue(2)
    fetch.issue(3)
    query = (done[0] + vec_ref[0:1, :]).astype(BF) * BF(0.125)
    for g in range(4):
        q_ref[g] = packed_columns(query[:, g * GROUP : (g + 1) * GROUP])
    turn.mates(q_ref, qo_ref, qs, qr)

    def spot(t):
        g, k = lax.div(t, 4), lax.rem(t, 4)
        dy = g + lax.div(g, 2) * (5 - 2 * g)
        return dy, k, wrap(y - dy, 4), wrap(z - k, 4)

    def onward(t):
        dy, k, i, j = spot(t)
        piece = kvo_ref.at[i, j, core]
        send(piece, piece, fs.at[t], fr.at[t], sibling)

    def hand(piece, dy, n):
        send(piece, piece, ms.at[n], mr.at[n], mate(dy))

    turn.end_first(4, kvo_ref.at[y, z, core], ks, kr)
    hand(kvo_ref.at[y, z, core], 1, 4)
    hand(kvo_ref.at[y, z, core], 3, 12)
    onward(0)
    def work(k):
        _, _, i, j = spot(k)
        piece = kvo_ref.at[i, j, 1 - core]
        finish(piece, piece, fs.at[k], fr.at[k], sibling)
        kv = load_chunk(kvo_ref, (i, j))
        for h in range(3):
            scores = nn(kv[:, h * HD : (h + 1) * HD], qt[h])
            old = top[h]
            new = jnp.maximum(old, jnp.max(scores, axis=0, keepdims=True))
            shrink = jnp.exp(old - new)
            weights = jnp.exp(scores - new)
            total[h] = total[h] * shrink + jnp.sum(weights, axis=0, keepdims=True)
            mixed = tn(kv[:, GROUP + h * HD : GROUP + (h + 1) * HD], weights.astype(BF))
            ot_ref[h] = ot_ref[h] * shrink + mixed
            top[h] = new

    def arrive(k):
        dy, n, i, j = spot(k)
        piece = kvo_ref.at[i, j, core]

        @pl.when(dy == 0)
        def _():
            turn.end(n, 4, piece, ks, kr)
            hand(piece, 1, 4 + n)
            hand(piece, 3, 12 + n)

        @pl.when(dy > 0)
        def _():
            finish(piece, piece, ms.at[dy * 4 + n], mr.at[dy * 4 + n], mate(1))

        pl.when((dy == 1) & (lax.rem(n, 2) == 0))(lambda: hand(piece, 1, 8 + n))
        pl.when((dy == 3) & (lax.rem(n, 2) == 1))(lambda: hand(piece, 3, 8 + n))
        onward(k)

    for k in range(1, 4):
        arrive(k)
    fetch.issue(4)
    fetch.issue(5)
    turn.mates_end(qo_ref, qs, qr)
    for h in range(3):
        qt[h] = turned(stack_head(qo_ref, h))
    top[...] = jnp.full_like(top, -jnp.inf)
    total[...] = jnp.zeros_like(total)
    ot_ref[...] = jnp.zeros_like(ot_ref)

    for k in range(3):
        work(k)

    def relay(k, carry):
        arrive(k)
        work(k - 1)

        for c, when in enumerate((4, 5, 7, 8, 11, 12)):
            pl.when(k == when)(functools.partial(fetch.step_x, c))
        return carry

    lax.fori_loop(4, 16, relay, 0)
    work(15)
    heads = []
    for h in range(3):
        lse_ref[h] = top[h] + jnp.log(total[h])
        normal = ot_ref[h] / total[h]
        ot_ref[h] = normal
        heads.append(normal.T.astype(BF))
    for i in range(4):
        o_ref[i] = packed([v[i * ROWS : (i + 1) * ROWS] for v in heads])
    turn.mates(o_ref, a_ref, os, om)
    for c in range(6):
        fetch.step_y(c)
    turn.mates_end(a_ref, os, om)
    finish(xo_ref, xo_ref, a_out.at[4], a_in.at[4], sibling)
    fetch.end()


def front(*arrays):
    return pl.pallas_call(
        front_kernel,
        name="front",
        cost_estimate=cost(70),
        out_shape=(
            shape(4, GROUP, ROWS), shape(4, GROUP, ROWS), shape(4, 4, 2, ROWS, HALF),
            shape(3, HD, 512, dtype=F32), shape(3, 1, 512, dtype=F32),
            shape(3, D, D), shape(D, FF), shape(FF, D), shape(D, D), shape(8, D, dtype=F32), shape(1, FF, dtype=F32),
            shape(ROWS, D), shape(ROWS, D),
        ),
        in_specs=[ANY, ANY, ANY, ANY] + [ANY] * 9 + [ANY] * 3,
        out_specs=(VM,) * 13,
        scratch_shapes=[
            pltpu.VMEM((4, GROUP, ROWS), BF), pltpu.VMEM((4, ROWS, HALF), BF),
            pltpu.VMEM((16, HALF), F32), pltpu.VMEM((16, HALF), F32),
            pltpu.VMEM((4, GROUP, ROWS), BF),
            pltpu.VMEM((3, HD, 512), BF), pltpu.VMEM((3, 1, 512), F32), pltpu.VMEM((3, 1, 512), F32),
            DMA((13,)), DMA((5,)), DMA((5,)), DMA((6,)), DMA((6,)), DMA((3,)), DMA((3,)),
            DMA((4,)), DMA((4,)), DMA((4,)), DMA((4,)), DMA((16,)), DMA((16,)), DMA((16,)), DMA((16,)),
            DMA((4,)), DMA((4,)), DMA((3,)),
        ] + [DMA((7,))] * 8 + [pltpu.VMEM((HALF,), BF)] * 8 + [pltpu.VMEM((1536,), BF)],
        compiler_params=remote(1),
    )(*map(hbm, arrays))


def norm(hidden):
    centred = hidden - jnp.mean(hidden, axis=-1, keepdims=True)
    inverse = lax.rsqrt(jnp.mean(centred * centred, axis=-1, keepdims=True) + EPS)
    return centred * inverse, inverse


def norm_back(scaled, normal, inverse):
    centre = jnp.mean(scaled, axis=-1, keepdims=True)
    along = jnp.mean(scaled * normal, axis=-1, keepdims=True)
    return inverse * (scaled - centre - normal * along)


def column(value):
    return jnp.sum(value, axis=0, keepdims=True)


def block_part(
    turn, ready, x_ref, ct_ref, a_ref, w_i, w_u, w_o, vec_ref, bi_ref,
    out_ref, dh1_ref, da_ref, af_ref, yb_ref, g_ref, df_ref, du_ref, dz_ref, vg_ref,
    af_o, yb_o, g_o, df_o, du_o, dz_o, slope, da_out, outs, ins, p_out, p_in,
):
    passed = ((af_ref, af_o), (yb_ref, yb_o), (g_ref, g_o), (df_ref, df_o), (du_ref, du_o), (dz_ref, dz_o))

    def pass_on(n):
        send(*passed[n], p_out.at[n], p_in.at[n], turn.sibling())

    b_output, first_gain, first_shift = vec_ref[2:3, :], vec_ref[3:4, :], vec_ref[4:5, :]
    b_outer, second_gain, second_shift = vec_ref[5:6, :], vec_ref[6:7, :], vec_ref[7:8, :]
    mixed = jnp.concatenate([unpacked(a_ref[g]) for g in range(4)], axis=1)
    af_ref[...] = mixed
    hidden = x_ref[...].astype(F32) + nn(mixed, w_o[...]) + b_output
    normal1, inverse1 = norm(hidden)
    normed = normal1 * first_gain + first_shift
    low = normed.astype(BF)
    yb_ref[...] = low
    ready()
    pass_on(0)
    pass_on(1)
    second_in = normed + b_outer
    for j in range(4):
        cut = slice(j * D, (j + 1) * D)
        inner = nn(low, w_i[:, cut]) + bi_ref[:, cut]
        cdf = 0.5 * (1.0 + lax.erf(inner * (0.5**0.5)))
        active = (inner * cdf).astype(BF)
        slope[:, cut] = cdf + inner * jnp.exp(inner * inner * -0.5) * 0.3989422804014327
        g_ref[:, cut] = active
        second_in = second_in + nn(active, w_u[cut, :])
    pass_on(2)
    normal2, inverse2 = norm(second_in)
    out_ref[...] = (normal2 * second_gain + second_shift).astype(BF)
    upper = ct_ref[...].astype(F32)


    def note(row, value):
        for h in range(2):
            vg_ref[h, row : row + 1, :] = value[:, h * HALF : (h + 1) * HALF]

    vg_ref[...] = jnp.zeros_like(vg_ref)
    note(6, column(upper * normal2))
    note(7, column(upper))
    dh2 = norm_back(upper * second_gain, normal2, inverse2)
    df = dh2.astype(BF)
    df_ref[...] = df
    pass_on(3)
    note(5, column(df.astype(F32)))
    dy1 = dh2
    for j in range(4):
        cut = slice(j * D, (j + 1) * D)
        du = (slope[:, cut] * nt(df, w_u[cut, :])).astype(BF)
        du_ref[:, cut] = du
        sums = column(du.astype(F32))
        for i in range(2):
            n = 2 * j + i
            vg_ref[n // 4, 8 + n % 4 : 9 + n % 4, :] = sums[:, i * HALF : (i + 1) * HALF]
        dy1 = dy1 + nt(du, w_i[:, cut])
    pass_on(4)
    note(3, column(dy1 * normal1))
    note(4, column(dy1))
    dh1 = norm_back(dy1 * first_gain, normal1, inverse1)
    dh1_ref[...] = dh1
    dz = dh1.astype(BF)
    dz_ref[...] = dz
    pass_on(5)
    note(2, column(dz.astype(F32)))
    da = nt(dz, w_o[...]).astype(BF)
    for g in range(4):
        da_out[g] = packed_columns(da[:, g * GROUP : (g + 1) * GROUP])
    turn.mates(da_out, da_ref, outs, ins)
    for n, (src, got) in enumerate(passed):
        finish(src, got, p_out.at[n], p_in.at[n], turn.sibling())


EARLY = (0, 3)
LATE = (3, 1)


def back_part(
    turn, da_end, q_ref, kv_ref, da_ref, ot_ref, lse_ref, x, x_o, yb, yb_o, g, g_o, a, a_o, df, df_o, du, du_o, dz, dz_o,
    dh1_ref, w_ref, vg_in,
    grad_ref, out, vo,
    rows_q, qt, rows_d, dt, delta, acc, dkv, other, dq, dqo, home, low, low_o, vg,
    g0, g1, g2, r0, r1, r2, s0, s1, s2, t0, t1, t2, rv, sv, sw, tv, uv,
    fs, fr, ks, kr, qs, qr, ls, lr, a_out, a_in, b_out, b_in, c_out, c_in, d_out, d_in, e_out, e_in,
):
    y, z, xl, core, half = turn.y, turn.z, turn.xl, turn.core, turn.half
    x_at = half * 2 + xl
    sibling = turn.sibling()
    barrier = pltpu.get_barrier_semaphore()

    def at(x_to, y_to, z_to):
        return device(y_to, z_to, lax.rem(x_to, 2), core, lax.div(x_to, 2))

    def along_x(k):
        return at(wrap(x_at + k, 4), y, z)

    def at_yz(k):
        i, j = pair(k)
        return at(x_at, wrap(y + i, 4), wrap(z + j, 4))

    def at_xz(k):
        i, j = pair(k)
        return at(wrap(x_at + i, 4), y, wrap(z + j, 4))

    def at_xy(k):
        i, j = pair(k)
        return at(wrap(x_at + i, 4), wrap(y + j, 4), z)

    def hello_yz(k, carry):
        greet(barrier, at_yz(k))
        return carry

    def hello_x(k, carry):
        i = lax.div(k - 1, 3) + 1
        j = lax.rem(k - 1, 3) + 1
        greet(barrier, at_xz(i * 4 + j))
        greet(barrier, at_xy(i * 4 + j))
        return carry

    def hello_row(k, carry):
        greet(barrier, along_x(k))
        return carry

    def hello_turn(k, carry):
        greet(barrier, turn.partner(k, 16))
        return carry

    def hello_all():
        lax.fori_loop(1, 16, hello_yz, 0)
        lax.fori_loop(1, 10, hello_x, 0)
        lax.fori_loop(1, 4, hello_row, 0)
        greet(barrier, sibling)

        @pl.when(jnp.logical_not(turn.stays))
        def _():
            lax.fori_loop(0, 16, hello_turn, 0)

    def ready():
        pl.semaphore_wait(barrier, 37 + 16 * lax.rem(xl + core, 2))

    def run():
        def put(slab, f, m, value):
            blocks = value.astype(BF).reshape(4, 2, 48, HALF)
            if slab == 1:
                g1[f, :, m] = blocks
            else:
                (g0 if slab == 0 else g2)[f, m] = blocks

        def right(ref, second, start):
            cols = pl.ds(pl.multiple_of(start + core * HALF, HALF), HALF)
            return jnp.concatenate([ref[:, cols], second[:, cols]], axis=0)

        def left(ref, second, start):
            return jnp.concatenate([ref[:, start : start + HALF], second[:, start : start + HALF]], axis=0)

        outer = right(df, df_o, 0)
        attn = right(dz, dz_o, 0)
        for f in range(2):
            for m in range(4):
                put(*((1, f, m) if m < 3 else (0, f, 0)), tn(left(g, g_o, f * 1536 + m * HALF), outer))
            rows = left(yb, yb_o, f * HALF)
            for m in range(4):
                put(*((2, f, m) if m < 3 else (0, f, 1)), tn(rows, right(du, du_o, m * D)))
            put(0, f, 2, tn(left(a, a_o, f * HALF), attn))

        def first(part):
            m, n = part
            late = 0 if part is EARLY else 4

            def one(k, carry):
                e = wrap(x_at + k, 4)
                send(
                    g1.at[:, wrap(y + k, 4), pl.ds(m, n)], r1.at[k - 1, :, pl.ds(m, n)],
                    a_out.at[late + 1, k], a_in.at[late + 1, k], at_yz(k * 4),
                )
                send(
                    g2.at[:, pl.ds(m, n), wrap(z + k, 4)], r2.at[k - 1, :, pl.ds(m, n)],
                    a_out.at[late + 2, k], a_in.at[late + 2, k], at_yz(k),
                )
                send(
                    g0.at[lax.div(e, 2), pl.ds(m, n), :, lax.rem(e, 2)], r0.at[k - 1, pl.ds(m, n)],
                    a_out.at[late, k], a_in.at[late, k], along_x(k),
                )
                return carry

            lax.fori_loop(1, 4, one, 0)

        first(EARLY)

        da_end()
        for h in range(3):
            rows = stack_head(q_ref, h)
            rows_q[h] = rows
            qt[h] = turned(rows)
            rows = stack_head(da_ref, h)
            rows_d[h] = rows
            flipped = rows.astype(F32).T
            dt[h] = flipped.astype(BF)
            delta[h] = jnp.sum(flipped * ot_ref[h], axis=0, keepdims=True)
        acc[...] = jnp.zeros_like(acc)

        def compute(k):
            i, j = turn.ahead(k, 16)
            kv = load_chunk(kv_ref, (i, j))
            keys, values = [], []
            for h in range(3):
                key = kv[:, h * HD : (h + 1) * HD]
                value = kv[:, GROUP + h * HD : GROUP + (h + 1) * HD]
                probs = jnp.exp(nn(key, qt[h]) - lse_ref[h])
                slopes = (probs * (nn(value, dt[h]) - delta[h])).astype(BF)
                keys.append(nn(slopes, rows_q[h]).astype(BF))
                values.append(nn(probs.astype(BF), rows_d[h]).astype(BF))
                acc[h] += tn(key, slopes)
            dkv[lax.rem(k, 4)] = jnp.concatenate(keys + values, axis=1).reshape(2, ROWS, HALF)

        def work(k):
            compute(k)
            pass_half(k)

        def pass_half(k):
            i, j = turn.ahead(k, 16)
            send(dkv.at[lax.rem(k, 4), 1 - core], other.at[i, j], fs.at[k], fr.at[k], sibling)

        def join(k):
            i, j = turn.ahead(k, 16)
            finish(other.at[i, j], other.at[i, j], fs.at[k], fr.at[k], sibling)
            other[i, j] = (dkv[lax.rem(k, 4), core].astype(F32) + other[i, j].astype(F32)).astype(BF)

        def relay(k):
            join(k)
            turn.push(k, 16, other.at[turn.ahead(k, 16)], home.at[y, z], ks, kr)

        for k in range(3):
            work(k)
        join(0)
        turn.first(16, other.at[y, z], home.at[y, z], ks, kr)

        def step(k, carry):
            work(k)
            relay(k - 2)
            return carry

        def finish_up(k, carry):
            relay(k)
            return carry

        lax.fori_loop(3, 16, step, 0)
        lax.fori_loop(14, 16, finish_up, 0)
        heads = [(acc[h] * 0.125).T.astype(BF) for h in range(3)]
        for i in range(4):
            dq[i] = packed([v[i * ROWS : (i + 1) * ROWS] for v in heads])
        turn.mates(dq, dqo, qs, qr)

        here = device(y, z, xl, core, half)

        def second(part):
            m, n = part
            late = 0 if part is EARLY else 4

            def add(slab, own, got, to, count, where):
                for k in range(1, 4):
                    piece = got.at[k - 1, pl.ds(m, n)] if slab == 0 else got.at[k - 1, :, pl.ds(m, n)]
                    finish(piece, piece, a_out.at[late + slab, k], a_in.at[late + slab, k], here)

                def one(i, carry):
                    p = where(i)
                    total = own(p).astype(F32)
                    for k in range(3):
                        total = total + got[(k,) + p].astype(F32)
                    to[p] = total.astype(BF)
                    return carry

                lax.fori_loop(0, count, one, 0)

            def push(slab, src, got, k, where):
                @pl.when(k > 0)
                def _():
                    send(src, got.at[k], b_out.at[slab, k], b_in.at[slab, k], where)

            def spot(i):
                return lax.div(i, 2 * n), m + lax.rem(lax.div(i, 2), n), lax.rem(i, 2)

            add(1, lambda p: g1[p[0], y, p[1], p[2]], r1, s1, 4 * n, spot)

            def push1(i, carry):
                e, to = wrap(x_at + lax.div(i, n), 4), m + lax.rem(i, n)
                k = lax.div(i, n) * 4 + wrap(to - z, 4)
                push(1, s1.at[lax.div(e, 2), to, lax.rem(e, 2)], t1, k, at(e, y, to))
                return carry

            lax.fori_loop(0, 4 * n, push1, 0)
            add(2, lambda p: g2[p[0], p[1], z, p[2]], r2, s2, 4 * n, spot)

            def push2(i, carry):
                e, to = wrap(x_at + lax.div(i, n), 4), m + lax.rem(i, n)
                k = lax.div(i, n) * 4 + wrap(to - y, 4)
                push(2, s2.at[lax.div(e, 2), to, lax.rem(e, 2)], t2, k, at(e, to, z))
                return carry

            lax.fori_loop(0, 4 * n, push2, 0)
            add(
                0, lambda p: g0[half, p[0], p[1], xl], r0, s0, 4 * n,
                lambda i: (m + lax.div(i, 4), lax.rem(i, 4)),
            )

            def push0(i, carry):
                e, to = wrap(z + lax.div(i, n), 4), m + lax.rem(i, n)
                k = wrap(to - y, 4) * 4 + lax.div(i, n)
                push(0, s0.at[to, e], t0, k, at(x_at, to, e))
                return carry

            lax.fori_loop(0, 4 * n, push0, 0)

        turn.mates_end(dqo, qs, qr)
        turn.end_first(16, home.at[y, z], ks, kr)

        def done(k, carry):
            turn.end(k, 16, home.at[turn.behind(k, 16)], ks, kr)
            return carry

        lax.fori_loop(1, 16, done, 0)
        low[0] = jnp.concatenate([unpacked(dqo[i]) for i in range(4)], axis=1)
        sums = []
        for i in range(4):
            total = home[0, i].astype(F32)
            for k in range(1, 4):
                total = total + home[k, i].astype(F32)
            sums.append(total.astype(BF))
        low[1] = jnp.concatenate([v[:, :GROUP] for v in sums], axis=1)
        low[2] = jnp.concatenate([v[:, GROUP:] for v in sums], axis=1)
        send(low, low_o, ls, lr, sibling)
        second(EARLY)
        finish(low, low_o, ls, lr, sibling)
        cols = pl.ds(pl.multiple_of(core * HALF, HALF), HALF)
        both_low = [jnp.concatenate([low[i, :, cols], low_o[i, :, cols]], axis=0) for i in range(3)]
        for f in range(2):
            rows = left(x, x_o, f * HALF)
            for i, slab in enumerate((2, 1, 0)):
                put(slab, f, 3, tn(rows, both_low[i]))
        first(LATE)
        grad = dh1_ref[...]
        for i in range(3):
            grad = grad + nt(low[i], w_ref[i])
        grad_ref[...] = grad
        vg[...] = vg_in[...]
        for row, i in ((0, 0), (1, 2)):
            value = column(low[i].astype(F32))
            for f in range(2):
                vg[f, row : row + 1, :] = value[:, f * HALF : (f + 1) * HALF]

        def first3(k, carry):
            src = vg.at[lax.div(wrap(x_at + k, 4), 2)]
            send(src, rv.at[k - 1], a_out.at[3, k], a_in.at[3, k], along_x(k))
            return carry

        lax.fori_loop(1, 4, first3, 0)

        def third(part):
            early = part is EARLY

            def whole(own, got, slab):
                def wait(k, carry):
                    arrived(got.at[k], b_in.at[slab, k], here)
                    return carry

                lax.fori_loop(1, 16, wait, 0)

                def one(k, total):
                    return total + got[k].astype(F32)

                out[core, slab, y, z, xl] = lax.fori_loop(1, 16, one, own.astype(F32)).astype(BF)

            def spread(slab, count, where):
                mine = out.at[core, slab, y, z, xl]

                def one(k, carry):
                    send(mine, mine, c_out.at[slab, k], c_in.at[slab, k], where(k))
                    return carry

                lax.fori_loop(1, count, one, 0)

            @pl.when(z < 3 if early else z == 3)
            def _():
                whole(s1[half, z, xl], t1, 1)
                spread(1, 8, lambda k: device(y, wrap(z + lax.div(k, 2), 4), wrap(xl + lax.rem(k, 2), 2), core, half))

            @pl.when(y < 3 if early else y == 3)
            def _():
                whole(s2[half, y, xl], t2, 2)
                spread(2, 8, lambda k: device(wrap(y + lax.div(k, 2), 4), z, wrap(xl + lax.rem(k, 2), 2), core, half))
                whole(s0[y, z], t0, 0)
                spread(0, 16, at_yz)

        def fourth(part):
            m, n = part
            late = 0 if part is EARLY else 3

            def wait(slab, piece, k):
                @pl.when(k > 0)
                def _():
                    arrived(piece, c_in.at[slab, k], here)

            def got1(i, carry):
                zz, xx = m + lax.div(i, 2), lax.rem(i, 2)
                wait(1, out.at[core, 1, y, zz, xx], wrap(z - zz, 4) * 2 + wrap(xl - xx, 2))
                return carry

            lax.fori_loop(0, 2 * n, got1, 0)

            def push1(k, carry):
                mine = out.at[core, 1, y, pl.ds(m, n)]
                send(mine, mine, d_out.at[late + 1, k], d_in.at[late + 1, k], at_yz(k * 4))
                return carry

            for k in (1, 3) if part is EARLY else (1, 2, 3):
                push1(k, 0)

            def got2(i, carry):
                yy, xx = m + lax.div(i, 2), lax.rem(i, 2)
                wait(2, out.at[core, 2, yy, z, xx], wrap(y - yy, 4) * 2 + wrap(xl - xx, 2))
                return carry

            lax.fori_loop(0, 2 * n, got2, 0)

            def push2(k, carry):
                mine = out.at[core, 2, pl.ds(m, n), z]
                send(mine, mine, d_out.at[late + 2, k], d_in.at[late + 2, k], at_yz(k))
                return carry

            for k in (1, 3) if part is EARLY else (1, 2, 3):
                push2(k, 0)

            def got0(i, carry):
                yy, zz = m + lax.div(i, 4), lax.rem(i, 4)
                wait(0, out.at[core, 0, yy, zz, xl], wrap(y - yy, 4) * 4 + wrap(z - zz, 4))
                return carry

            lax.fori_loop(0, 4 * n, got0, 0)
            mine0 = out.at[core, 0, pl.ds(m, n), :, xl]
            send(mine0, mine0, d_out.at[late, 1], d_in.at[late, 1], device(y, z, 1 - xl, core, half))

        def hand_on():
            m, n = EARLY
            for k, side in ((1, 0), (3, 1)):
                y_from, z_from = wrap(y - k, 4), wrap(z - k, 4)
                piece = out.at[core, 1, y_from, pl.ds(m, n)]
                finish(piece, piece, d_out.at[1, k], d_in.at[1, k], here)
                part1 = out.at[core, 1, y_from, pl.ds(m, n), side]
                send(part1, part1, d_out.at[1, 2], d_in.at[1, 2], at_yz(k * 4))
                piece = out.at[core, 2, pl.ds(m, n), z_from]
                finish(piece, piece, d_out.at[2, k], d_in.at[2, k], here)
                part2 = out.at[core, 2, pl.ds(m, n), z_from, side]
                send(part2, part2, d_out.at[2, 2], d_in.at[2, 2], at_yz(k))

        def own_part(slab, who, part):
            m, n = part
            return out.at[who, 1, :, pl.ds(m, n)] if slab == 1 else out.at[who, slab, pl.ds(m, n)]

        def last(part):
            m, n = part
            late = 0 if part is EARLY else 3

            def got1(k, carry):
                piece = out.at[core, 1, wrap(y - k, 4), pl.ds(m, n)]
                finish(piece, piece, d_out.at[late + 1, k], d_in.at[late + 1, k], here)
                return carry

            def got2(k, carry):
                piece = out.at[core, 2, pl.ds(m, n), wrap(z - k, 4)]
                finish(piece, piece, d_out.at[late + 2, k], d_in.at[late + 2, k], here)
                return carry

            def onward(slab):
                piece = own_part(slab, core, part)
                send(piece, piece, e_out.at[late + slab], e_in.at[late + slab], sibling)

            for k in (2,) if part is EARLY else (1, 2, 3):
                got1(k, 0)
            onward(1)
            for k in (2,) if part is EARLY else (1, 2, 3):
                got2(k, 0)
            onward(2)
            piece0 = out.at[core, 0, pl.ds(m, n), :, 1 - xl]
            finish(piece0, piece0, d_out.at[late, 1], d_in.at[late, 1], here)
            onward(0)

        third(EARLY)
        for k in range(1, 4):
            finish(rv.at[k - 1], rv.at[k - 1], a_out.at[3, k], a_in.at[3, k], here)
        part_sum = vg[half] + rv[0] + rv[1] + rv[2]
        sv[...] = part_sum.astype(BF)

        for k in range(1, 4):
            send(sv, tv.at[k], b_out.at[3, k], b_in.at[3, k], at_yz(k * 4))
        fourth(EARLY)
        second(LATE)
        for k in range(1, 4):
            finish(tv.at[k], tv.at[k], b_out.at[3, k], b_in.at[3, k], here)
            part_sum = part_sum + tv[k].astype(F32)
        sw[...] = part_sum.astype(BF)
        for k in range(1, 4):
            send(sw, tv.at[4 + k], b_out.at[3, 4 + k], b_in.at[3, 4 + k], at_yz(k))
        third(LATE)
        hand_on()

        for k in range(5, 8):
            finish(tv.at[k], tv.at[k], b_out.at[3, k], b_in.at[3, k], here)
            part_sum = part_sum + tv[k].astype(F32)
        vo[...] = part_sum
        send(vo, uv, e_out.at[6], e_in.at[6], sibling)
        fourth(LATE)
        last(EARLY)
        for slab, count, own, got in ((1, 8, s1, t1), (2, 8, s2, t2), (0, 16, s0, t0)):
            mine = out.at[core, slab, y, z, xl]

            def gone2(k, carry):
                left_here(got.at[k], b_out.at[slab, k], here)
                return carry

            def gone3(k, carry):
                left_here(mine, c_out.at[slab, k], here)
                return carry

            lax.fori_loop(1, 16, gone2, 0)
            lax.fori_loop(1, count, gone3, 0)
        last(LATE)
        for late, part in ((0, EARLY), (3, LATE)):
            for slab in range(3):
                piece = own_part(slab, 1 - core, part)
                finish(piece, piece, e_out.at[late + slab], e_in.at[late + slab], here)
        finish(uv, uv, e_out.at[6], e_in.at[6], here)
        vo[...] = vo[...] + uv[...]

    return hello_all, ready, run


BLOCK_ACTS = ((ROWS, D), (ROWS, D), (ROWS, FF), (ROWS, D), (ROWS, FF), (ROWS, D))


def rest_kernel(
    x, ct, mixed, w_i, w_u, w_o, vec, bi, q, kv, ot, lse, x_o, w_qkv,
    layer_ref, grad_ref, out, vo,
    dh1, da, vg_in, a, yb, g, df, du, dz, a_o, yb_o, g_o, df_o, du_o, dz_o, slope, da_out, *more,
):
    (outs, ins, p_out, p_in), more = more[:4], more[4:]
    turn = Turn()
    hello_all, ready, run = back_part(
        turn, lambda: turn.mates_end(da, outs, ins), q, kv, da, ot, lse, x, x_o, yb, yb_o, g, g_o, a, a_o, df, df_o,
        du, du_o, dz, dz_o, dh1, w_qkv, vg_in, grad_ref, out, vo, *more,
    )
    hello_all()
    block_part(
        turn, ready, x, ct, mixed, w_i, w_u, w_o, vec, bi, layer_ref, dh1, da, a, yb, g, df, du, dz, vg_in,
        a_o, yb_o, g_o, df_o, du_o, dz_o, slope, da_out, outs, ins, p_out, p_in,
    )
    run()


def rest(*arrays):
    blk = (48, HALF)
    acts = [(v, BF) for v in BLOCK_ACTS]
    first = [((ROWS, D), F32), ((4, GROUP, ROWS), BF), ((2, 16, HALF), F32)] + acts + acts + [
        ((ROWS, FF), F32), ((4, GROUP, ROWS), BF),
    ]
    second = [
        ((3, 512, HD), BF), ((3, HD, 512), BF), ((3, 512, HD), BF), ((3, HD, 512), BF), ((3, 1, 512), F32),
        ((3, HD, 512), F32), ((4, 2, ROWS, HALF), BF), ((4, 4, ROWS, HALF), BF),
        ((4, GROUP, ROWS), BF), ((4, GROUP, ROWS), BF), ((4, 4, ROWS, HALF), BF), ((3, ROWS, D), BF), ((3, ROWS, D), BF),
        ((2, 16, HALF), F32),
        ((2, 4, 4, 2, *blk), BF), ((2, 4, 4, 2, *blk), BF), ((2, 4, 4, 2, *blk), BF),
        ((3, 4, 4, *blk), BF), ((3, 2, 4, 2, *blk), BF), ((3, 2, 4, 2, *blk), BF),
        ((4, 4, *blk), BF), ((2, 4, 2, *blk), BF), ((2, 4, 2, *blk), BF),
        ((16, *blk), BF), ((16, *blk), BF), ((16, *blk), BF),
        ((3, 16, HALF), F32), ((16, HALF), BF), ((16, HALF), BF), ((8, 16, HALF), BF), ((16, HALF), F32),
    ]
    return pl.pallas_call(
        rest_kernel,
        name="rest",
        cost_estimate=cost(130),
        out_shape=(
            shape(ROWS, D), shape(ROWS, D, dtype=F32), shape(2, 3, 4, 4, 2, *blk), shape(16, HALF, dtype=F32),
        ),
        in_specs=[VM] * 14,
        out_specs=(VM,) * 4,
        scratch_shapes=[pltpu.VMEM(*v) for v in first] + [DMA((4,)), DMA((4,)), DMA((6,)), DMA((6,))]
        + [pltpu.VMEM(*v) for v in second] + [
            DMA((16,)), DMA((16,)), DMA((16,)), DMA((16,)), DMA((4,)), DMA((4,)), DMA, DMA,
            DMA((7, 4)), DMA((7, 4)), DMA((4, 16)), DMA((4, 16)), DMA((3, 16)), DMA((3, 16)),
            DMA((6, 4)), DMA((6, 4)), DMA((7,)), DMA((7,)),
        ],
        compiler_params=pltpu.CompilerParams(
            collective_id=3, has_side_effects=True, vmem_limit_bytes=34 << 20
        ),
    )(*map(vm, arrays))


def spell_kernel(full, vo, layer, grad, *refs):
    q_ref, k_ref, v_ref, o_ref, i_ref, u_ref, layer_ref, grad_ref = refs[:8]
    lines, (stage, sems, direct) = refs[8:17], refs[17:]
    straight = [
        pltpu.make_async_copy(layer, layer_ref, direct.at[0]), pltpu.make_async_copy(grad, grad_ref, direct.at[1])
    ]
    for copy in straight:
        copy.start()
    for i in range(8):
        lines[i][...] = vo[i : i + 1, :].reshape(HALF)
    lines[8][...] = jnp.concatenate([vo[8 + i : 9 + i, :] for i in range(4)], axis=1).reshape(1536)

    def copies(n):
        slot = stage.at[n % 3]
        rows = slice(n * 48, (n + 1) * 48)
        made = [
            pltpu.make_async_copy(slot.at[m], ref.at[rows], sems.at[n % 3, m])
            for m, ref in enumerate((q_ref, k_ref, v_ref, o_ref))
        ]
        for m in range(4):
            made.append(pltpu.make_async_copy(
                slot.at[4 + m], i_ref.at[rows, m * D : (m + 1) * D], sems.at[n % 3, 4 + m]
            ))
            made.append(pltpu.make_async_copy(
                slot.at[8 + m], u_ref.at[m * HALF + n * 48 : m * HALF + (n + 1) * 48], sems.at[n % 3, 8 + m]
            ))
        return made

    for n in range(8):
        if n >= 3:
            for copy in copies(n - 3):
                copy.wait()
        i, xl = n // 2, n % 2
        for c in range(2):
            cols = slice(c * HALF, (c + 1) * HALF)
            units = [(2, 3), (1, 3), (0, 3), (0, 2), (2, 0), (2, 1), (2, 2), (0, 1), (1, 0), (1, 1), (1, 2), (0, 0)]
            for m, (slab, unit) in enumerate(units):
                piece = full[c, 1, i, unit, xl] if slab == 1 else full[c, slab, unit, i, xl]
                stage[n % 3, m, :, cols] = piece.astype(F32)
        for copy in copies(n):
            copy.start()
    for n in (5, 6, 7):
        for copy in copies(n):
            copy.wait()
    for copy in straight:
        copy.wait()


def spell(*arrays):
    return pl.pallas_call(
        spell_kernel,
        name="spell",
        out_shape=tuple(
            plain_shape(*dims, dtype=F32)
            for dims in ((HALF, D), (HALF, D), (HALF, D), (HALF, D), (HALF, FF), (1536, D))
        ) + (plain_shape(ROWS, D), plain_shape(ROWS, D, dtype=F32))
        + (plain_shape(HALF, dtype=F32),) * 8 + (plain_shape(1536, dtype=F32),),
        in_specs=[VM] * 4,
        out_specs=(ANY,) * 8 + (VM,) * 9,
        scratch_shapes=[pltpu.VMEM((3, 12, 48, D), F32), DMA((3, 12)), DMA((2,))],
        compiler_params=plain(),
        cost_estimate=cost(6),
    )(*map(vm, arrays))


def local(
    tokens, cotangent, w_query, w_key, w_value, w_output, b_query, b_value, b_output,
    first_gain, first_shift, w_inner, b_inner, w_outer, b_outer, second_gain, second_shift,
):
    x = tokens[0]
    mixed, q_all, kv_all, mixed_t, lse, w_qkv, w_i, w_u, w_o, vec, bi, x_o, x_in = front(
        x, w_query, w_key, w_value, b_query, b_value, b_output, first_gain, first_shift, b_outer, second_gain,
        second_shift, b_inner, w_inner, w_outer, w_output,
    )
    layer_out, tokens_grad, summed, vecs = rest(
        x_in, cotangent[0], mixed, w_i, w_u, w_o, vec, bi, q_all, kv_all, mixed_t, lse, x_o, w_qkv
    )
    gq, gk, gv, go, gi, gu, layer_out, tokens_grad, *vecs = spell(summed, vecs, layer_out, tokens_grad)
    return (
        layer_out[None], tokens_grad[None], gq, gk, gv, go,
        vecs[0], vecs[1], vecs[2], vecs[3], vecs[4], gi, vecs[8], gu, vecs[5], vecs[6], vecs[7],
    )


def solution(mesh):
    rows = P(("seq", "fsdp"), "ctx", None)
    mat = P("fsdp", None)
    vec = P("fsdp")
    return jax.shard_map(
        local,
        mesh=mesh,
        in_specs=(rows, rows, mat, mat, mat, mat, vec, vec, vec, vec, vec, mat, vec, mat, vec, vec, vec),
        out_specs=(rows, rows, mat, mat, mat, mat, vec, vec, vec, vec, vec, mat, vec, mat, vec, vec, vec),
        check_vma=False,
    )
```
